128 devices in a mesh: mesh: 32 (over z_lo, x, y), harm: 4 (over z_hi, core).
Axes of the slice: x: 4, y: 4, z: 4 (z_hi: 2, z_lo: 2; z = z_hi * 2 + z_lo), core: 2. Of those that a mesh axis runs over, the one named last changes fastest.
Arguments:
- field_in: float32 [64, 163840], P('harm', 'mesh'), may hold values from -6 to 6
- faces: int32 [2, 32768], P(None, 'mesh'), may hold values from 0 to 5119, as said below
- connectivity: int32 [6, 131072], P(None, 'mesh'), may hold values from 0 to 7167
- curl_vectors: float32 [3, 6, 131072], P(None, None, 'mesh'), may hold values from -2.4 to 2.4
- operating_point: float32 [64, 3, 32, 4096], P(None, None, None, ('mesh', 'harm')), may hold values from -2.5 to 2.5
- material: int32 [32, 4096], P(None, ('mesh', 'harm')), may hold values from 0 to 3
- bh_knots: int32 [8], replicated, may hold values from 0 to 15
- curve_base: float32 [4], replicated, may hold values from 0.5 to 2
- curve_slopes: float32 [4, 8], replicated, may hold values from 0.02 to 0.2
Outputs:
- product: float32 [64, 163840], P('harm', 'mesh')
The draws below stay inside these ranges and needn't reach their ends.
Inputs may be any that keep to these rules, and one draw needn't show every extreme that they name: `faces`: for each partition the 1024 lower face edges and the 1024 upper face edges are 2048 distinct local edge numbers. `connectivity`: numbers below 5120 are the partition's own edges, the next 1024 the ghost edges after the upper face list of the partition below, the last 1024 those after the lower face list of the partition above.
All inputs are finite; a program needn't handle non-finite values.
Results may differ from the reference program's by a relative error of at most 0.0003.
Values sent between devices are 32-bit elements; how exact they have to be, the bound alone decides.
A program may use at most 128 MiB of HBM per device.

```python
import math
import jax
import jax.numpy as jnp
from jax import lax

SAMPLES = 64
E_PART = 4096
KNOTS = 8
MATERIALS = 4
EDGES_PART = 5120
FACE = 1024
ELEMS = 131072
EDGES = 163840
N_MESH = 32


def draw_faces(key, part):
    keys = jax.random.split(jax.random.fold_in(key, 7), N_MESH)

    def single(sub_key):
        order = jax.random.permutation(sub_key, jnp.arange(EDGES_PART, dtype=jnp.int32))
        return order[:2 * FACE].reshape(2, FACE)
    lists = jax.vmap(single)(keys)
    return jnp.transpose(lists, (1, 0, 2)).reshape(2, N_MESH * FACE).astype(jnp.int32)


def set_ends(values, rng, smallest, largest):
    place = [jax.random.randint(jax.random.fold_in(rng, axis), (), 0, length) for axis, length in enumerate(values.shape)]
    longest = values.shape.index(max(values.shape))
    next_to = place[:longest] + [(place[longest] + 1) % values.shape[longest]] + place[longest + 1:]
    return values.at[tuple(place)].set(smallest).at[tuple(next_to)].set(largest)


def block_levels(rng, extent, cuts, smallest, high):
    def one(axis_at, shards_of):
        heights = jax.random.uniform(jax.random.fold_in(jax.random.fold_in(rng, 6), axis_at), (shards_of,), jnp.float32, smallest / len(cuts), high / len(cuts))
        return jnp.repeat(jnp.exp(heights), extent[axis_at] // shards_of).reshape((-1,) + (1,) * (len(extent) - axis_at - 1))

    factor_of = one(*cuts[0])
    for cut in cuts[1:]:
        factor_of = factor_of * one(*cut)
    return factor_of


def noise(stream_key, dims, scale, most, shards=(), kind=jnp.bfloat16):
    drawn = scale * jax.random.normal(stream_key, dims, jnp.float32)
    if shards:
        drawn = drawn * block_levels(stream_key, dims, shards, -0.22, 0.18)
    return jnp.clip(drawn, -most, most).astype(kind)


def setup_inputs(seed: int = 0) -> dict:
    key_of = jax.random.split(jax.random.key(seed), 10)
    return {
        "field_in": noise(key_of[0], (SAMPLES, EDGES), 1.0, 6.0, ((0, 4), (1, 32)), jnp.float32),
        "faces": draw_faces(jax.random.fold_in(key_of[9], 71), 0),
        "connectivity": set_ends(jax.random.randint(key_of[2], (6, ELEMS), 0, EDGES_PART + 2 * FACE), jax.random.fold_in(key_of[2], 1), 0, (EDGES_PART + 2 * FACE) - 1).astype(jnp.int32),
        "curl_vectors": noise(key_of[3], (3, 6, ELEMS), 0.4, 2.4, ((2, 32),), jnp.float32),
        "operating_point": noise(key_of[4], (SAMPLES, 3, N_MESH, E_PART), 0.7, 2.5, ((3, 128),), jnp.float32),
        "material": set_ends(jax.random.randint(key_of[5], (N_MESH, E_PART), 0, MATERIALS), jax.random.fold_in(key_of[5], 1), 0, MATERIALS - 1).astype(jnp.int32),
        "bh_knots": set_ends(jax.random.randint(key_of[6], (KNOTS,), 0, 16), jax.random.fold_in(key_of[6], 1), 0, 15).astype(jnp.int32),
        "curve_base": jnp.clip(jnp.exp(jax.random.uniform(key_of[7], (MATERIALS,), jnp.float32, math.log(0.5), math.log(2.0))), 0.5, 2.0),
        "curve_slopes": jnp.clip(jnp.exp(jax.random.uniform(key_of[8], (MATERIALS, KNOTS), jnp.float32, math.log(0.02), math.log(0.2))), 0.02, 0.2),
    }


KNOT_STEP = 0.25
KNOT_WIDTH = 0.5


def dft_tables(length):
    sample_idx = jnp.arange(length, dtype=jnp.int32)
    coef_idx = jnp.arange(length, dtype=jnp.int32)
    half_len = length // 2
    harmonic = jnp.where(coef_idx < half_len, coef_idx, coef_idx - half_len + 1)
    harmonic = jnp.where(coef_idx == length - 1, half_len, harmonic)
    is_sine = (coef_idx >= half_len) & (coef_idx < length - 1)
    phase_int = (harmonic[:, None] * sample_idx[None, :]) % length
    angles = phase_int.astype(jnp.float32) * (2.0 * jnp.pi / length)
    basis_rows = jnp.where(is_sine[:, None], jnp.sin(angles), jnp.cos(angles))
    weight = jnp.where((coef_idx == 0) | (coef_idx == length - 1), 1.0 / length, 2.0 / length)
    return basis_rows.T, basis_rows * weight[:, None].astype(jnp.float32)


def apply_tensor(flux_step, point, material, bh_knots, curve_base, curve_slopes):
    kind_ids = jnp.arange(curve_base.shape[0], dtype=jnp.int32).reshape((-1,) + (1,) * material.ndim)
    one_hot = (material[None] == kind_ids).astype(jnp.float32)
    base_elem = jnp.einsum('a,a...->...', curve_base, one_hot, precision=lax.Precision.HIGHEST)
    slope_elem = jnp.einsum('ak,a...->k...', curve_slopes, one_hot, precision=lax.Precision.HIGHEST)
    flux_sq = jnp.sum(point * point, axis=1)
    knot_pos = bh_knots.astype(jnp.float32) * KNOT_STEP
    scaled = (flux_sq[None] - knot_pos.reshape((-1,) + (1,) * flux_sq.ndim)) / KNOT_WIDTH
    reluct = base_elem[None] + jnp.sum(slope_elem[:, None] * jax.nn.softplus(scaled), axis=0)
    slope_sum = jnp.sum(slope_elem[:, None] * jax.nn.sigmoid(scaled), axis=0) / KNOT_WIDTH
    projected = jnp.sum(point * flux_step, axis=1)
    return reluct[:, None] * flux_step + 2.0 * (slope_sum * projected)[:, None] * point


def reference(field_in, faces, connectivity, curl_vectors, operating_point, material, bh_knots, curve_base, curve_slopes):
    owned = field_in.reshape(SAMPLES, N_MESH, EDGES_PART)
    face_ids = faces.reshape(2, N_MESH, FACE)
    lower_face = jnp.take_along_axis(owned, face_ids[0][None], axis=2)
    upper_face = jnp.take_along_axis(owned, face_ids[1][None], axis=2)
    extended = jnp.concatenate([owned, jnp.roll(upper_face, 1, axis=1), jnp.roll(lower_face, -1, axis=1)], axis=2)
    inverse, forward = dft_tables(SAMPLES)

    def partition(inputs):
        ext_part, conn_part, curl_part, point_part, mat_part = inputs
        gathered = ext_part[:, conn_part]
        flux_coef = jnp.einsum('ije,cje->cie', curl_part, gathered, precision=lax.Precision.HIGHEST)
        flux_step = jnp.einsum('tc,cie->tie', inverse, flux_coef, precision=lax.Precision.HIGHEST)
        field_step = apply_tensor(flux_step, point_part, mat_part, bh_knots, curve_base, curve_slopes)
        field_coef = jnp.einsum('ct,tie->cie', forward, field_step, precision=lax.Precision.HIGHEST)
        contrib = jnp.einsum('ije,cie->cje', curl_part, field_coef, precision=lax.Precision.HIGHEST)
        zeros_ext = jnp.zeros((SAMPLES, EDGES_PART + 2 * FACE), jnp.float32)
        return zeros_ext.at[:, conn_part.reshape(-1)].add(contrib.reshape(SAMPLES, -1))

    assembled = lax.map(partition, (
        jnp.moveaxis(extended, 1, 0),
        jnp.moveaxis(connectivity.reshape(6, N_MESH, E_PART), 1, 0),
        jnp.moveaxis(curl_vectors.reshape(3, 6, N_MESH, E_PART), 2, 0),
        jnp.moveaxis(operating_point, 2, 0),
        material))
    own_sums = assembled[:, :, :EDGES_PART]
    from_below = jnp.roll(assembled[:, :, EDGES_PART + FACE:], 1, axis=0)
    from_above = jnp.roll(assembled[:, :, EDGES_PART:EDGES_PART + FACE], -1, axis=0)

    def add_faces(sums, lower_ids, upper_ids, below_part, above_part):
        return sums.at[:, lower_ids].add(below_part).at[:, upper_ids].add(above_part)

    result = jax.vmap(add_faces)(own_sums, face_ids[0], face_ids[1], from_below, from_above)
    return jnp.moveaxis(result, 0, 1).reshape(SAMPLES, N_MESH * EDGES_PART)
```

```python
import functools

import numpy as np
import jax
import jax.numpy as jnp
from jax import lax
from jax.experimental import pallas as pl
from jax.experimental.pallas import tpu as pltpu
from jax.sharding import PartitionSpec as P

MESH = pl.DeviceIdType.MESH
N_MESH = 32
OWN = 5120
FACE = 1024
EXT = OWN + 2 * FACE
ROWS = 512
MSG = 56


def block_diag_tables():
    length = 64
    t = np.arange(length)
    c = np.arange(length)
    freq = np.where(c < 32, c, c - 31)
    freq[-1] = 32
    sine = (c >= 32) & (c < 63)
    angle = 2.0 * np.pi * ((freq[:, None] * t[None, :]) % length) / length
    basis = np.where(sine[:, None], np.sin(angle), np.cos(angle))
    weight = np.where((c == 0) | (c == 63), 1.0 / length, 2.0 / length)
    inverse = np.kron(np.eye(2), basis)
    forward = np.kron(np.eye(2), (basis * weight[:, None]).T)
    return inverse.astype(np.float32), forward.astype(np.float32)


def spread_kernel(field_ref, faces_ref, point_ref, mat_ref, ext_out, op_out,
                  opsend, field_t, face_rows, face_cols,
                  op_ss, op_rs, own_ss, own_rs, gh_ss, gh_rs, fw_ss, fw_rs, lo_s):
    m = lax.axis_index("mesh")
    h = lax.axis_index("harm")
    up, down = lax.rem(m + 1, N_MESH), lax.rem(m + N_MESH - 1, N_MESH)
    side = h + 1 - 2 * lax.rem(h, 2)
    far = lax.rem(h + 2, 4)

    barrier = pltpu.get_barrier_semaphore()

    @pl.loop(1, N_MESH)
    def _(d):
        pl.semaphore_signal(barrier, inc=1, device_id=(lax.rem(m + d, N_MESH), h), device_id_type=MESH)
    for peer in (side, far):
        pl.semaphore_signal(barrier, inc=1, device_id=(m, peer), device_id_type=MESH)

    lane = lax.broadcasted_iota(jnp.int32, (16, 64), 1)
    del lane

    @pl.loop(0, N_MESH)
    def _(p):
        for i in range(3):
            opsend[p, pl.ds(16 * i, 16), pl.ds(0, 64)] = point_ref[i, p, pl.ds(0, 16), :]
            opsend[p, pl.ds(16 * i, 16), pl.ds(64, 64)] = point_ref[i, p, pl.ds(16, 16), :]
        opsend[p, pl.ds(48, 8), :] = jnp.zeros((8, 128), jnp.float32)
        opsend[p, pl.ds(48, 1), pl.ds(0, 32)] = mat_ref[pl.ds(p, 1), :].astype(jnp.float32)

    pl.semaphore_wait(barrier, N_MESH - 1 + 2)

    rows = pl.ds(pl.multiple_of(16 * h, 16), 16)
    own_cols = pl.ds(0, OWN)
    ghost_cols = pl.ds(OWN, 2 * FACE)

    def own_copy(n, peer):
        return pltpu.make_async_remote_copy(
            src_ref=field_ref, dst_ref=ext_out.at[rows, own_cols],
            send_sem=own_ss.at[n], recv_sem=own_rs.at[n],
            device_id=(m, peer), device_id_type=MESH)

    own_far, own_side = own_copy(0, far), own_copy(1, side)
    own_far.start()
    own_side.start()
    local = pltpu.make_async_copy(field_ref, ext_out.at[rows, own_cols], lo_s)
    local.start()

    def op_copy(d):
        p = lax.rem(m + d, N_MESH)
        return pltpu.make_async_remote_copy(
            src_ref=opsend.at[p], dst_ref=op_out.at[m],
            send_sem=op_ss.at[d], recv_sem=op_rs.at[d],
            device_id=(p, h), device_id_type=MESH)

    @pl.loop(1, N_MESH)
    def _(d):
        op_copy(d).start()
    op_local = pltpu.make_async_copy(opsend.at[m], op_out.at[m], op_ss.at[0])
    op_local.start()

    @pl.loop(0, OWN // 128, unroll=4)
    def _(b):
        at = pl.ds(pl.multiple_of(b * 128, 128), 128)
        field_t[at, :] = field_ref[:, at].T

    for f in range(2):
        @pl.loop(0, FACE // 16)
        def _(b):
            for k in range(16):
                n = faces_ref[f, b * 16 + k]
                face_rows[pl.ds(f * FACE + b * 16 + k, 1), :] = field_t[pl.ds(n, 1), :]

    @pl.loop(0, 2 * FACE // 128, unroll=4)
    def _(b):
        at = pl.ds(pl.multiple_of(b * 128, 128), 128)
        face_cols[:, at] = face_rows[at, :].T

    def ghost_copy(f, peer):
        return pltpu.make_async_remote_copy(
            src_ref=face_cols.at[:, pl.ds(f * FACE, FACE)],
            dst_ref=ext_out.at[rows, pl.ds(OWN + (1 - f) * FACE, FACE)],
            send_sem=gh_ss.at[f], recv_sem=gh_rs.at[f],
            device_id=(peer, h), device_id_type=MESH)

    ghosts = [ghost_copy(0, down), ghost_copy(1, up)]
    for c in ghosts:
        c.start()
    for c in ghosts:
        c.wait_recv()

    def gfwd_copy(n, peer):
        return pltpu.make_async_remote_copy(
            src_ref=ext_out.at[rows, ghost_cols], dst_ref=ext_out.at[rows, ghost_cols],
            send_sem=fw_ss.at[n], recv_sem=fw_rs.at[n],
            device_id=(m, peer), device_id_type=MESH)

    gfar, gside = gfwd_copy(0, far), gfwd_copy(1, side)
    gfar.start()
    gside.start()

    far_rows = pl.ds(pl.multiple_of(16 * far, 16), 16)

    def relay(n, cols):
        return pltpu.make_async_remote_copy(
            src_ref=ext_out.at[far_rows, cols], dst_ref=ext_out.at[far_rows, cols],
            send_sem=fw_ss.at[n], recv_sem=fw_rs.at[n],
            device_id=(m, side), device_id_type=MESH)

    own_far.wait_recv()
    relay_own = relay(2, own_cols)
    relay_own.start()
    gfar.wait_recv()
    relay_gh = relay(3, ghost_cols)
    relay_gh.start()

    own_side.wait_recv()
    gside.wait_recv()
    relay_own.wait_recv()
    relay_gh.wait_recv()

    @pl.loop(1, N_MESH)
    def _(d):
        op_copy(d).wait_recv()

    local.wait()
    op_local.wait()
    for c in (own_far, own_side, gfar, gside, relay_own, relay_gh, *ghosts):
        c.wait_send()

    @pl.loop(1, N_MESH)
    def _(d):
        op_copy(d).wait_send()


def spread(field_in, faces, point, material):
    return pl.pallas_call(
        spread_kernel,
        name="spread",
        out_shape=(jax.ShapeDtypeStruct((64, EXT), jnp.float32),
                   jax.ShapeDtypeStruct((N_MESH, MSG, 128), jnp.float32)),
        in_specs=[pl.BlockSpec(memory_space=pltpu.VMEM), pl.BlockSpec(memory_space=pltpu.SMEM),
                  pl.BlockSpec(memory_space=pltpu.VMEM), pl.BlockSpec(memory_space=pltpu.VMEM)],
        out_specs=(pl.BlockSpec(memory_space=pl.ANY), pl.BlockSpec(memory_space=pl.ANY)),
        scratch_shapes=[
            pltpu.VMEM((N_MESH, MSG, 128), jnp.float32),
            pltpu.VMEM((OWN, 16), jnp.float32),
            pltpu.VMEM((2 * FACE, 16), jnp.float32),
            pltpu.VMEM((16, 2 * FACE), jnp.float32),
            pltpu.SemaphoreType.DMA((N_MESH,)), pltpu.SemaphoreType.DMA((N_MESH,)),
            pltpu.SemaphoreType.DMA((2,)), pltpu.SemaphoreType.DMA((2,)),
            pltpu.SemaphoreType.DMA((2,)), pltpu.SemaphoreType.DMA((2,)),
            pltpu.SemaphoreType.DMA((4,)), pltpu.SemaphoreType.DMA((4,)),
            pltpu.SemaphoreType.DMA,
        ],
        compiler_params=pltpu.CompilerParams(collective_id=0, has_side_effects=True,
                                             vmem_limit_bytes=40 << 20),
    )(field_in, faces, point, material)


def element_kernel(conn_ref, knots_ref, base_ref, slopes_ref, ext_ref, op_ref, curl_ref, inv_ref, fwd_ref,
                   out_ref, ext2, curl_t, mat_b, wide, got, flux, acc0, acc1, acc2, acc3):
    h = lax.axis_index("harm")
    low = lax.broadcasted_iota(jnp.int32, (16, 128), 1) < 64
    low1 = lax.broadcasted_iota(jnp.int32, (1, 128), 1) < 64
    accs = (acc0, acc1, acc2, acc3)

    @pl.loop(0, EXT // 128, unroll=2)
    def _(b):
        at = pl.ds(pl.multiple_of(b * 128, 128), 128)
        x = ext_ref[:, at]
        ext2[at, :] = jnp.concatenate([x, x], axis=0).T

    @pl.loop(0, EXT // 64)
    def _(b):
        at = pl.ds(pl.multiple_of(b * 64, 64), 64)
        for a in accs:
            a[at, :] = jnp.zeros((64, 128), jnp.float32)

    @pl.loop(0, N_MESH)
    def _(m):
        at = pl.ds(pl.multiple_of(m * 128, 128), 128)
        pad = jnp.zeros((2, 128), jnp.float32)
        parts = []
        for i in range(3):
            parts += [curl_ref[i, :, at], pad]
        curl_t[at, :] = jnp.concatenate(parts, axis=0).T

    @pl.loop(0, N_MESH)
    def _(m):
        to = pl.ds(pl.multiple_of(m * 16, 16), 16)
        first = m * 128 + h * 32
        c0 = curl_t[pl.ds(pl.multiple_of(first, 16), 16), :]
        c1 = curl_t[pl.ds(pl.multiple_of(first + 16, 16), 16), :]
        for i in range(3):
            for j in range(6):
                col = i * 8 + j
                wide[i * 6 + j, to, :] = jnp.where(low, jnp.broadcast_to(c0[:, col:col + 1], (16, 128)),
                                                   jnp.broadcast_to(c1[:, col:col + 1], (16, 128)))
        mt = jnp.broadcast_to(op_ref[m, pl.ds(48, 1), :], (8, 128)).T
        mat_b[to, :] = jnp.where(low, jnp.broadcast_to(mt[0:16, 0:1], (16, 128)),
                                 jnp.broadcast_to(mt[16:32, 0:1], (16, 128)))

    @pl.loop(0, N_MESH)
    def _(m):
        to = pl.ds(pl.multiple_of(m * 16, 16), 16)
        first = m * 128 + h * 32
        for j in range(6):
            for k in range(16):
                a = ext2[pl.ds(conn_ref[j, first + k], 1), :]
                b = ext2[pl.ds(conn_ref[j, first + 16 + k], 1), :]
                got[pl.ds(j * 16 + k, 1), :] = jnp.where(low1, a, b)
        for i in range(3):
            s = wide[i * 6, to, :] * got[0:16, :]
            for j in range(1, 6):
                s = s + wide[i * 6 + j, to, :] * got[j * 16:(j + 1) * 16, :]
            flux[i, to, :] = s

    growth = [jnp.exp(jnp.float32(-0.5) * knots_ref[k].astype(jnp.float32)) for k in range(8)]

    @pl.loop(0, ROWS // 64)
    def _(r):
        to = pl.ds(pl.multiple_of(r * 64, 64), 64)
        f = [jnp.dot(flux[i, to, :], inv_ref[...], precision=lax.Precision.HIGHEST,
                     preferred_element_type=jnp.float32) for i in range(3)]
        b = [jnp.concatenate([op_ref[r * 4 + s, 16 * i:16 * i + 16, :] for s in range(4)], axis=0)
             for i in range(3)]
        mat = mat_b[to, :]

        def pick(values):
            x = jnp.where(mat == 1.0, values[1], values[0])
            x = jnp.where(mat == 2.0, values[2], x)
            return jnp.where(mat == 3.0, values[3], x)

        q = b[0] * b[0] + b[1] * b[1] + b[2] * b[2]
        u = jnp.exp(2.0 * q)
        nu = pick([base_ref[a] for a in range(4)])
        dnu = jnp.zeros_like(q)
        for k in range(8):
            slope = pick([slopes_ref[a, k] for a in range(4)])
            e = u * growth[k]
            w = 1.0 + e
            nu = nu + slope * jnp.log(w)
            dnu = dnu + slope * (e / w)
        proj = b[0] * f[0] + b[1] * f[1] + b[2] * f[2]
        scale = 4.0 * dnu * proj
        for i in range(3):
            flux[i, to, :] = jnp.dot(nu * f[i] + scale * b[i], fwd_ref[...], precision=lax.Precision.HIGHEST,
                                     preferred_element_type=jnp.float32)

    @pl.loop(0, N_MESH)
    def _(m):
        to = pl.ds(pl.multiple_of(m * 16, 16), 16)
        first = m * 128 + h * 32
        f = [flux[i, to, :] for i in range(3)]
        for j in range(6):
            got[j * 16:(j + 1) * 16, :] = (wide[j, to, :] * f[0] + wide[6 + j, to, :] * f[1]
                                           + wide[12 + j, to, :] * f[2])
        for k in range(16):
            for j in range(0, 6, 2):
                for jj in range(2):
                    row = got[pl.ds((j + jj) * 16 + k, 1), :]
                    n0 = conn_ref[j + jj, first + k]
                    n1 = conn_ref[j + jj, first + 16 + k]
                    accs[jj][pl.ds(n0, 1), :] = accs[jj][pl.ds(n0, 1), :] + row
                    accs[2 + jj][pl.ds(n1, 1), :] = accs[2 + jj][pl.ds(n1, 1), :] + row

    wide_low = lax.broadcasted_iota(jnp.int32, (128, 128), 1) < 64

    @pl.loop(0, EXT // 128)
    def _(b):
        at = pl.ds(pl.multiple_of(b * 128, 128), 128)
        x = jnp.where(wide_low, acc0[at, :] + acc1[at, :], acc2[at, :] + acc3[at, :]).T
        out_ref[:, at] = x[0:64, :] + x[64:128, :]


def elements(conn, knots, base, slopes, ext, op, curl):
    inverse, forward = block_diag_tables()
    smem = pl.BlockSpec(memory_space=pltpu.SMEM)
    vmem = pl.BlockSpec(memory_space=pltpu.VMEM)
    big = pltpu.VMEM((EXT, 128), jnp.float32)
    return pl.pallas_call(
        element_kernel,
        name="elements",
        out_shape=jax.ShapeDtypeStruct((64, EXT), jnp.float32),
        in_specs=[smem, smem, smem, smem, vmem, vmem, vmem, vmem, vmem],
        out_specs=vmem,
        scratch_shapes=[big, pltpu.VMEM((4096, 24), jnp.float32), pltpu.VMEM((ROWS, 128), jnp.float32),
                        pltpu.VMEM((18, ROWS, 128), jnp.float32), pltpu.VMEM((96, 128), jnp.float32),
                        pltpu.VMEM((3, ROWS, 128), jnp.float32), big, big, big, big],
        compiler_params=pltpu.CompilerParams(vmem_limit_bytes=60 << 20),
    )(conn, knots, base, slopes, ext, op, curl, jnp.asarray(inverse), jnp.asarray(forward))


def combine_kernel(acc_ref, own_out, ghost_out, pairs, summed, zin, ghost_sum,
                   p_ss, p_rs, z_ss, z_rs, g_ss, g_rs):
    m = lax.axis_index("mesh")
    h = lax.axis_index("harm")
    up, down = lax.rem(m + 1, N_MESH), lax.rem(m + N_MESH - 1, N_MESH)
    side = h + 1 - 2 * lax.rem(h, 2)
    far = lax.rem(h + 2, 4)
    cross = lax.rem(side + 2, 4)
    barrier = pltpu.get_barrier_semaphore()
    peers = ((m, side), (m, far), (up, h), (down, h))
    for peer in peers:
        pl.semaphore_signal(barrier, inc=1, device_id=peer, device_id_type=MESH)
    pl.semaphore_wait(barrier, 4)

    chunks = (pl.ds(OWN, 2 * FACE), pl.ds(0, OWN))

    def block(who):
        return pl.ds(pl.multiple_of(16 * who, 16), 16)

    def pair_copy(c, n):
        who = (side, cross)[n]
        return pltpu.make_async_remote_copy(
            src_ref=acc_ref.at[block(who), chunks[c]], dst_ref=pairs.at[n, :, chunks[c]],
            send_sem=p_ss.at[c, n], recv_sem=p_rs.at[c, n],
            device_id=(m, side), device_id_type=MESH)

    def z_copy(c):
        return pltpu.make_async_remote_copy(
            src_ref=summed.at[:, chunks[c]], dst_ref=zin.at[:, chunks[c]],
            send_sem=z_ss.at[c], recv_sem=z_rs.at[c],
            device_id=(m, far), device_id_type=MESH)

    def g_copy(f, peer):
        return pltpu.make_async_remote_copy(
            src_ref=ghost_sum.at[:, pl.ds(f * FACE, FACE)],
            dst_ref=ghost_out.at[:, pl.ds((1 - f) * FACE, FACE)],
            send_sem=g_ss.at[f], recv_sem=g_rs.at[f],
            device_id=(peer, h), device_id_type=MESH)

    order = [(0, 1), (1, 1), (0, 0), (1, 0)]
    pair = {cn: pair_copy(*cn) for cn in order}
    for cn in order:
        pair[cn].start()
    zs = [z_copy(0), z_copy(1)]
    for c in range(2):
        pair[c, 1].wait_recv()
        summed[:, chunks[c]] = acc_ref[block(far), chunks[c]] + pairs[1, :, chunks[c]]
        zs[c].start()
    pair[0, 0].wait_recv()
    zs[0].wait_recv()
    ghost_sum[...] = acc_ref[block(h), chunks[0]] + pairs[0, :, chunks[0]] + zin[:, chunks[0]]
    gs = [g_copy(0, down), g_copy(1, up)]
    for g in gs:
        g.start()
    pair[1, 0].wait_recv()
    zs[1].wait_recv()
    own_out[...] = acc_ref[block(h), chunks[1]] + pairs[0, :, chunks[1]] + zin[:, chunks[1]]
    for g in gs:
        g.wait_recv()
    for c in (*pair.values(), *zs, *gs):
        c.wait_send()


def combine(acc):
    vmem = pl.BlockSpec(memory_space=pltpu.VMEM)
    return pl.pallas_call(
        combine_kernel,
        name="combine",
        out_shape=(jax.ShapeDtypeStruct((16, OWN), jnp.float32),
                   jax.ShapeDtypeStruct((16, 2 * FACE), jnp.float32)),
        in_specs=[vmem],
        out_specs=(vmem, pl.BlockSpec(memory_space=pl.ANY)),
        scratch_shapes=[
            pltpu.VMEM((2, 16, EXT), jnp.float32), pltpu.VMEM((16, EXT), jnp.float32),
            pltpu.VMEM((16, EXT), jnp.float32), pltpu.VMEM((16, 2 * FACE), jnp.float32),
            pltpu.SemaphoreType.DMA((2, 2)), pltpu.SemaphoreType.DMA((2, 2)),
            pltpu.SemaphoreType.DMA((2,)), pltpu.SemaphoreType.DMA((2,)),
            pltpu.SemaphoreType.DMA((2,)), pltpu.SemaphoreType.DMA((2,)),
        ],
        compiler_params=pltpu.CompilerParams(collective_id=1, has_side_effects=True,
                                             vmem_limit_bytes=40 << 20),
    )(acc)


def finish_kernel(faces_ref, own_ref, ghost_ref, out_ref, ghost_t, full_t):
    @pl.loop(0, OWN // 128, unroll=4)
    def _(b):
        full_t[pl.ds(pl.multiple_of(b * 128, 128), 128), :] = jnp.zeros((128, 16), jnp.float32)

    @pl.loop(0, 2 * FACE // 128, unroll=4)
    def _(b):
        at = pl.ds(pl.multiple_of(b * 128, 128), 128)
        ghost_t[at, :] = ghost_ref[:, at].T

    for f in range(2):
        @pl.loop(0, FACE // 16)
        def _(b):
            for k in range(16):
                full_t[pl.ds(faces_ref[f, b * 16 + k], 1), :] = ghost_t[pl.ds(f * FACE + b * 16 + k, 1), :]

    @pl.loop(0, OWN // 128, unroll=4)
    def _(b):
        at = pl.ds(pl.multiple_of(b * 128, 128), 128)
        out_ref[:, at] = own_ref[:, at] + full_t[at, :].T


def finish(faces, own, ghost):
    vmem = pl.BlockSpec(memory_space=pltpu.VMEM)
    return pl.pallas_call(
        finish_kernel,
        name="finish",
        out_shape=jax.ShapeDtypeStruct((16, OWN), jnp.float32),
        in_specs=[pl.BlockSpec(memory_space=pltpu.SMEM), vmem, vmem],
        out_specs=vmem,
        scratch_shapes=[pltpu.VMEM((2 * FACE, 16), jnp.float32), pltpu.VMEM((OWN, 16), jnp.float32)],
        compiler_params=pltpu.CompilerParams(vmem_limit_bytes=40 << 20),
    )(faces, own, ghost)


def per_device(field_in, faces, connectivity, curl_vectors, operating_point, material, bh_knots, curve_base,
               curve_slopes):
    point = jnp.transpose(operating_point, (1, 2, 3, 0))
    ext, op = spread(field_in, faces, point, material)
    acc = elements(connectivity, bh_knots, curve_base, curve_slopes, ext, op, curl_vectors)
    own, ghost = combine(acc)
    return finish(faces, own, ghost)


def solution(mesh):
    return jax.shard_map(
        per_device,
        mesh=mesh,
        in_specs=(P("harm", "mesh"), P(None, "mesh"), P(None, "mesh"), P(None, None, "mesh"),
                  P(None, None, None, ("mesh", "harm")), P(None, ("mesh", "harm")), P(), P(), P()),
        out_specs=P("harm", "mesh"),
        check_vma=False,
    )
```

```python
import functools

import numpy as np
import jax
import jax.numpy as jnp
from jax import lax
from jax.experimental import pallas as pl
from jax.experimental.pallas import tpu as pltpu
from jax.sharding import PartitionSpec as P

MESH = pl.DeviceIdType.MESH
N_MESH = 32
OWN = 5120
FACE = 1024
EXT = OWN + 2 * FACE
ROWS = 512
MSG = 56
PARTS = 4
CHUNK = OWN // PARTS


def block_diag_tables():
    length = 64
    t = np.arange(length)
    c = np.arange(length)
    freq = np.where(c < 32, c, c - 31)
    freq[-1] = 32
    sine = (c >= 32) & (c < 63)
    angle = 2.0 * np.pi * ((freq[:, None] * t[None, :]) % length) / length
    basis = np.where(sine[:, None], np.sin(angle), np.cos(angle))
    weight = np.where((c == 0) | (c == 63), 1.0 / length, 2.0 / length)
    inverse = np.kron(np.eye(2), basis)
    forward = np.kron(np.eye(2), (basis * weight[:, None]).T)
    return inverse.astype(np.float32), forward.astype(np.float32)


def forward_kernel(field_ref, point_ref, mat_ref, curl_ref, faces_ref, conn_ref, knots_ref, base_ref, slopes_ref,
                   inv_ref, fwd_ref, out_ref,
                   field, point, curl, opsend, op_in, field_t, face_rows, face_cols, ext, ext2, curl_t, wide, got, flux,
                   in_s, op_ss, op_rs, far_ss, far_rs, side_ss, side_rs, gh_ss, gh_rs, fw_ss, fw_rs, rel_ss, rel_rs):
    m = lax.axis_index("mesh")
    h = lax.axis_index("harm")
    up, down = lax.rem(m + 1, N_MESH), lax.rem(m + N_MESH - 1, N_MESH)
    side = h + 1 - 2 * lax.rem(h, 2)
    far = lax.rem(h + 2, 4)
    half = m // 16

    def block_of(source, target):
        crossing = (source // 16 + target // 16) % 2
        return lax.rem(h + 2 * crossing * lax.rem(source, 2), 4)

    load_field = pltpu.make_async_copy(field_ref, field, in_s.at[0])
    load_point = pltpu.make_async_copy(point_ref, point, in_s.at[1])
    load_curl = pltpu.make_async_copy(curl_ref, curl, in_s.at[2])
    load_field.start()
    load_point.start()
    load_curl.start()

    barrier = pltpu.get_barrier_semaphore()
    for peer in ((m, far), (m, side), (up, h), (down, h)):
        pl.semaphore_signal(barrier, inc=1, device_id=peer, device_id_type=MESH)

    @pl.loop(1, N_MESH)
    def _(d):
        source = lax.rem(m + N_MESH - d, N_MESH)
        pl.semaphore_signal(barrier, inc=1, device_id=(source, block_of(source, m)), device_id_type=MESH)

    load_field.wait()

    @pl.loop(0, OWN // 128, unroll=8)
    def _(b):
        at = pl.ds(pl.multiple_of(b * 128, 128), 128)
        field_t[at, :] = field[:, at].T

    pl.semaphore_wait(barrier, N_MESH - 1 + 4)

    def rows_of(who):
        return pl.ds(pl.multiple_of(16 * who, 16), 16)

    ghost_cols = pl.ds(OWN, 2 * FACE)

    def cols_of(c):
        return pl.ds(c * CHUNK, CHUNK)

    def own_copy(c, peer, ss, rs):
        return pltpu.make_async_remote_copy(
            src_ref=field.at[:, cols_of(c)], dst_ref=ext.at[rows_of(h), cols_of(c)],
            send_sem=ss.at[c], recv_sem=rs.at[c],
            device_id=(m, peer), device_id_type=MESH)

    to_far = [own_copy(c, far, far_ss, far_rs) for c in range(PARTS)]
    to_side = [own_copy(c, side, side_ss, side_rs) for c in range(PARTS)]
    for c in (*to_far, *to_side):
        c.start()
    keep = pltpu.make_async_copy(field, ext.at[rows_of(h), pl.ds(0, OWN)], in_s.at[3])
    keep.start()

    for f in range(2):
        @pl.loop(0, FACE // 16)
        def _(b):
            for k in range(16):
                n = faces_ref[f, b * 16 + k]
                face_rows[pl.ds(f * FACE + b * 16 + k, 1), :] = field_t[pl.ds(n, 1), :]

    @pl.loop(0, 2 * FACE // 128, unroll=8)
    def _(b):
        at = pl.ds(pl.multiple_of(b * 128, 128), 128)
        face_cols[:, at] = face_rows[at, :].T

    def ghost_copy(f, peer):
        return pltpu.make_async_remote_copy(
            src_ref=face_cols.at[:, pl.ds(f * FACE, FACE)],
            dst_ref=ext.at[rows_of(h), pl.ds(OWN + (1 - f) * FACE, FACE)],
            send_sem=gh_ss.at[f], recv_sem=gh_rs.at[f],
            device_id=(peer, h), device_id_type=MESH)

    ghosts = [ghost_copy(0, down), ghost_copy(1, up)]
    for c in ghosts:
        c.start()

    load_point.wait()

    @pl.loop(0, N_MESH)
    def _(p):
        for i in range(3):
            opsend[p, pl.ds(16 * i, 16), pl.ds(0, 64)] = point[i, p, pl.ds(0, 16), :]
            opsend[p, pl.ds(16 * i, 16), pl.ds(64, 64)] = point[i, p, pl.ds(16, 16), :]
        opsend[p, pl.ds(48, 8), :] = jnp.zeros((8, 128), jnp.float32)
        opsend[p, pl.ds(48, 1), pl.ds(0, 32)] = mat_ref[pl.ds(p, 1), :].astype(jnp.float32)

    def op_copy(d):
        p = lax.rem(m + d, N_MESH)
        target = lax.rem(h + 2 * ((half + p // 16) % 2) * lax.rem(m, 2), 4)
        return pltpu.make_async_remote_copy(
            src_ref=opsend.at[p], dst_ref=op_in.at[m],
            send_sem=op_ss.at[d], recv_sem=op_rs.at[d],
            device_id=(p, target), device_id_type=MESH)

    @pl.loop(1, N_MESH)
    def _(d):
        op_copy(d).start()
    op_keep = pltpu.make_async_copy(opsend.at[m], op_in.at[m], in_s.at[4])
    op_keep.start()

    for c in ghosts:
        c.wait_recv()

    def gfwd_copy(n, peer):
        return pltpu.make_async_remote_copy(
            src_ref=ext.at[rows_of(h), ghost_cols], dst_ref=ext.at[rows_of(h), ghost_cols],
            send_sem=fw_ss.at[n], recv_sem=fw_rs.at[n],
            device_id=(m, peer), device_id_type=MESH)

    gfar, gside = gfwd_copy(0, far), gfwd_copy(1, side)
    gfar.start()
    gside.start()

    def relay(c, cols):
        return pltpu.make_async_remote_copy(
            src_ref=ext.at[rows_of(far), cols], dst_ref=ext.at[rows_of(far), cols],
            send_sem=rel_ss.at[c], recv_sem=rel_rs.at[c],
            device_id=(m, side), device_id_type=MESH)

    relays = [relay(c, cols_of(c)) for c in range(PARTS)] + [relay(PARTS, ghost_cols)]

    low = lax.broadcasted_iota(jnp.int32, (16, 128), 1) < 64
    low1 = lax.broadcasted_iota(jnp.int32, (1, 128), 1) < 64

    load_curl.wait()

    @pl.loop(0, N_MESH, unroll=4)
    def _(s):
        at = pl.ds(pl.multiple_of(s * 128, 128), 128)
        pad = jnp.zeros((2, 128), jnp.float32)
        parts = []
        for i in range(3):
            parts += [curl[i, :, at], pad]
        curl_t[at, :] = jnp.concatenate(parts, axis=0).T

    for c in range(PARTS):
        @pl.loop(c * N_MESH // PARTS, (c + 1) * N_MESH // PARTS)
        def _(s):
            to = pl.ds(pl.multiple_of(s * 16, 16), 16)
            first = s * 128 + block_of(s, m) * 32
            c0 = curl_t[pl.ds(pl.multiple_of(first, 16), 16), :]
            c1 = curl_t[pl.ds(pl.multiple_of(first + 16, 16), 16), :]
            for i in range(3):
                for j in range(6):
                    col = i * 8 + j
                    wide[i * 6 + j, to, :] = jnp.where(low, jnp.broadcast_to(c0[:, col:col + 1], (16, 128)),
                                                       jnp.broadcast_to(c1[:, col:col + 1], (16, 128)))
        to_far[c].wait_recv()
        relays[c].start()
    gfar.wait_recv()
    relays[PARTS].start()

    keep.wait()
    for c in range(PARTS + 1):
        if c < PARTS:
            to_side[c].wait_recv()
        else:
            gside.wait_recv()
        relays[c].wait_recv()
        blocks = CHUNK // 128 if c < PARTS else 2 * FACE // 128

        @pl.loop(0, blocks, unroll=2)
        def _(b):
            at = pl.ds(pl.multiple_of(c * CHUNK + b * 128, 128), 128)
            x = ext[:, at]
            ext2[at, :] = jnp.concatenate([x, x], axis=0).T

    @pl.loop(0, N_MESH)
    def _(s):
        to = pl.ds(pl.multiple_of(s * 16, 16), 16)
        first = s * 128 + block_of(s, m) * 32
        for j in range(6):
            for k in range(16):
                a = ext2[pl.ds(conn_ref[j, first + k], 1), :]
                b = ext2[pl.ds(conn_ref[j, first + 16 + k], 1), :]
                got[pl.ds(j * 16 + k, 1), :] = jnp.where(low1, a, b)
        for i in range(3):
            s_i = wide[i * 6, to, :] * got[0:16, :]
            for j in range(1, 6):
                s_i = s_i + wide[i * 6 + j, to, :] * got[j * 16:(j + 1) * 16, :]
            flux[i, to, :] = s_i

    @pl.loop(1, N_MESH)
    def _(d):
        op_copy(d).wait_recv()

    op_keep.wait()
    growth = [jnp.exp(jnp.float32(-0.5) * knots_ref[k].astype(jnp.float32)) for k in range(8)]

    @pl.loop(0, ROWS // 64)
    def _(r):
        to = pl.ds(pl.multiple_of(r * 64, 64), 64)
        f = [jnp.dot(flux[i, to, :], inv_ref[...], precision=lax.Precision.HIGHEST,
                     preferred_element_type=jnp.float32) for i in range(3)]
        b = [jnp.concatenate([op_in[r * 4 + s, 16 * i:16 * i + 16, :] for s in range(4)], axis=0)
             for i in range(3)]
        kinds = []
        for s in range(4):
            mt = jnp.broadcast_to(op_in[r * 4 + s, pl.ds(48, 1), :], (8, 128)).T
            kinds.append(jnp.where(low, jnp.broadcast_to(mt[0:16, 0:1], (16, 128)),
                                   jnp.broadcast_to(mt[16:32, 0:1], (16, 128))))
        mat = jnp.concatenate(kinds, axis=0)

        def pick(values):
            x = jnp.where(mat == 1.0, values[1], values[0])
            x = jnp.where(mat == 2.0, values[2], x)
            return jnp.where(mat == 3.0, values[3], x)

        q = b[0] * b[0] + b[1] * b[1] + b[2] * b[2]
        u = jnp.exp(2.0 * q)
        nu = pick([base_ref[a] for a in range(4)])
        dnu = jnp.zeros_like(q)
        for k in range(8):
            slope = pick([slopes_ref[a, k] for a in range(4)])
            e = u * growth[k]
            w = 1.0 + e
            nu = nu + slope * jnp.log(w)
            dnu = dnu + slope * (e / w)
        proj = b[0] * f[0] + b[1] * f[1] + b[2] * f[2]
        scale = 4.0 * dnu * proj
        f = [jnp.dot(nu * f[i] + scale * b[i], fwd_ref[...], precision=lax.Precision.HIGHEST,
                     preferred_element_type=jnp.float32) for i in range(3)]
        for j in range(6):
            out_ref[pl.ds(pl.multiple_of(j * ROWS + r * 64, 64), 64), :] = (
                wide[j, to, :] * f[0] + wide[6 + j, to, :] * f[1] + wide[12 + j, to, :] * f[2])

    for c in (*to_far, *to_side, *ghosts, gfar, gside, *relays):
        c.wait_send()

    @pl.loop(1, N_MESH)
    def _(d):
        op_copy(d).wait_send()


def forward(field, point, material, curl, faces, conn, knots, base, slopes):
    inverse, forward_table = block_diag_tables()
    smem = pl.BlockSpec(memory_space=pltpu.SMEM)
    vmem = pl.BlockSpec(memory_space=pltpu.VMEM)
    hbm = pl.BlockSpec(memory_space=pl.ANY)
    f32 = jnp.float32
    dma = pltpu.SemaphoreType.DMA
    return pl.pallas_call(
        forward_kernel,
        name="forward",
        out_shape=jax.ShapeDtypeStruct((6 * ROWS, 128), f32),
        in_specs=[hbm, hbm, vmem, hbm, smem, smem, smem, smem, smem, vmem, vmem],
        out_specs=vmem,
        scratch_shapes=[
            pltpu.VMEM((16, OWN), f32), pltpu.VMEM((3, 32, 32, 64), f32), pltpu.VMEM((3, 6, 4096), f32),
            pltpu.VMEM((N_MESH, MSG, 128), f32), pltpu.VMEM((N_MESH, MSG, 128), f32),
            pltpu.VMEM((OWN, 16), f32), pltpu.VMEM((2 * FACE, 16), f32), pltpu.VMEM((16, 2 * FACE), f32),
            pltpu.VMEM((64, EXT), f32), pltpu.VMEM((EXT, 128), f32), pltpu.VMEM((4096, 24), f32),
            pltpu.VMEM((18, ROWS, 128), f32), pltpu.VMEM((96, 128), f32), pltpu.VMEM((3, ROWS, 128), f32),
            dma((5,)), dma((N_MESH,)), dma((N_MESH,)), dma((PARTS,)), dma((PARTS,)), dma((PARTS,)), dma((PARTS,)),
            dma((2,)), dma((2,)), dma((2,)), dma((2,)), dma((PARTS + 1,)), dma((PARTS + 1,)),
        ],
        compiler_params=pltpu.CompilerParams(collective_id=0, has_side_effects=True,
                                             vmem_limit_bytes=60 << 20),
    )(field, point, material, curl, faces, conn, knots, base, slopes, jnp.asarray(inverse), jnp.asarray(forward_table))


def scatter_kernel(conn_ref, con_ref, out_ref, acc0, acc1, acc2, acc3):
    m = lax.axis_index("mesh")
    h = lax.axis_index("harm")
    accs = (acc0, acc1, acc2, acc3)
    low = lax.broadcasted_iota(jnp.int32, (64, 128), 1) < 64

    def block_of(source, target):
        crossing = (source // 16 + target // 16) % 2
        return lax.rem(h + 2 * crossing * lax.rem(source, 2), 4)

    @pl.loop(0, EXT // 64)
    def _(b):
        at = pl.ds(pl.multiple_of(b * 64, 64), 64)
        for a in accs:
            a[at, :] = jnp.zeros((64, 128), jnp.float32)

    @pl.loop(0, N_MESH)
    def _(s):
        first = s * 128 + block_of(s, m) * 32
        for k in range(16):
            for j in range(6):
                row = con_ref[pl.ds(j * ROWS + s * 16 + k, 1), :]
                n0 = conn_ref[j, first + k]
                n1 = conn_ref[j, first + 16 + k]
                a0, a1 = accs[j % 2], accs[2 + j % 2]
                a0[pl.ds(n0, 1), :] = a0[pl.ds(n0, 1), :] + row
                a1[pl.ds(n1, 1), :] = a1[pl.ds(n1, 1), :] + row

    @pl.loop(0, EXT // 64, unroll=2)
    def _(b):
        at = pl.ds(pl.multiple_of(b * 64, 64), 64)
        out_ref[at, :] = jnp.where(low, acc0[at, :] + acc1[at, :], acc2[at, :] + acc3[at, :])


def scatter(conn, con):
    vmem = pl.BlockSpec(memory_space=pltpu.VMEM)
    big = pltpu.VMEM((EXT, 128), jnp.float32)
    return pl.pallas_call(
        scatter_kernel,
        name="scatter",
        out_shape=jax.ShapeDtypeStruct((EXT, 128), jnp.float32),
        in_specs=[pl.BlockSpec(memory_space=pltpu.SMEM), vmem],
        out_specs=vmem,
        scratch_shapes=[big, big, big, big],
        compiler_params=pltpu.CompilerParams(vmem_limit_bytes=32 << 20),
    )(conn, con)


def combine_kernel(rows_ref, own_out, ghost_out, acc, pairs, summed, zin, ghost_sum, ghost_in,
                   p_ss, p_rs, z_ss, z_rs, g_ss, g_rs):
    m = lax.axis_index("mesh")
    h = lax.axis_index("harm")
    up, down = lax.rem(m + 1, N_MESH), lax.rem(m + N_MESH - 1, N_MESH)
    side = h + 1 - 2 * lax.rem(h, 2)
    far = lax.rem(h + 2, 4)
    cross = lax.rem(side + 2, 4)
    barrier = pltpu.get_barrier_semaphore()
    for peer in ((m, side), (m, far), (up, h), (down, h)):
        pl.semaphore_signal(barrier, inc=1, device_id=peer, device_id_type=MESH)

    bounds = [(OWN, 2 * FACE)] + [(c * CHUNK, CHUNK) for c in range(PARTS)]
    chunks = [pl.ds(a, n) for a, n in bounds]

    def block(who):
        return pl.ds(pl.multiple_of(16 * who, 16), 16)

    def turn(c):
        start, n = bounds[c]

        @pl.loop(0, n // 128, unroll=2)
        def _(b):
            at = pl.ds(pl.multiple_of(start + b * 128, 128), 128)
            x = rows_ref[at, :].T
            acc[:, at] = x[0:64, :] + x[64:128, :]

    def pair_copy(c, n):
        return pltpu.make_async_remote_copy(
            src_ref=acc.at[block((side, cross)[n]), chunks[c]], dst_ref=pairs.at[n, :, chunks[c]],
            send_sem=p_ss.at[c, n], recv_sem=p_rs.at[c, n],
            device_id=(m, side), device_id_type=MESH)

    def z_copy(c):
        return pltpu.make_async_remote_copy(
            src_ref=summed.at[:, chunks[c]], dst_ref=zin.at[:, chunks[c]],
            send_sem=z_ss.at[c], recv_sem=z_rs.at[c],
            device_id=(m, far), device_id_type=MESH)

    def g_copy(f, peer):
        return pltpu.make_async_remote_copy(
            src_ref=ghost_sum.at[:, pl.ds(f * FACE, FACE)],
            dst_ref=ghost_in.at[:, pl.ds((1 - f) * FACE, FACE)],
            send_sem=g_ss.at[f], recv_sem=g_rs.at[f],
            device_id=(peer, h), device_id_type=MESH)

    count = PARTS + 1
    far_pairs = [pair_copy(c, 1) for c in range(count)]
    own_pairs = [pair_copy(c, 0) for c in range(count)]
    zs = [z_copy(c) for c in range(count)]
    gs = [g_copy(0, down), g_copy(1, up)]

    turn(0)
    pl.semaphore_wait(barrier, 4)
    far_pairs[0].start()
    own_pairs[0].start()
    for c in range(count):
        if c + 1 < count:
            turn(c + 1)
            far_pairs[c + 1].start()
            own_pairs[c + 1].start()
        far_pairs[c].wait_recv()
        summed[:, chunks[c]] = acc[block(far), chunks[c]] + pairs[1, :, chunks[c]]
        zs[c].start()

    def total(c):
        own_pairs[c].wait_recv()
        zs[c].wait_recv()
        return acc[block(h), chunks[c]] + pairs[0, :, chunks[c]] + zin[:, chunks[c]]

    ghost_sum[...] = total(0)
    for g in gs:
        g.start()
    for c in range(1, count):
        own_out[:, chunks[c]] = total(c)
    for g in gs:
        g.wait_recv()
    ghost_out[...] = ghost_in[...]
    for c in (*far_pairs, *own_pairs, *zs, *gs):
        c.wait_send()


def combine(rows):
    vmem = pl.BlockSpec(memory_space=pltpu.VMEM)
    dma = pltpu.SemaphoreType.DMA
    f32 = jnp.float32
    return pl.pallas_call(
        combine_kernel,
        name="combine",
        out_shape=(jax.ShapeDtypeStruct((16, OWN), f32), jax.ShapeDtypeStruct((16, 2 * FACE), f32)),
        in_specs=[vmem],
        out_specs=(vmem, vmem),
        scratch_shapes=[
            pltpu.VMEM((64, EXT), f32), pltpu.VMEM((2, 16, EXT), f32), pltpu.VMEM((16, EXT), f32),
            pltpu.VMEM((16, EXT), f32), pltpu.VMEM((16, 2 * FACE), f32), pltpu.VMEM((16, 2 * FACE), f32),
            dma((PARTS + 1, 2)), dma((PARTS + 1, 2)), dma((PARTS + 1,)), dma((PARTS + 1,)), dma((2,)), dma((2,)),
        ],
        compiler_params=pltpu.CompilerParams(collective_id=1, has_side_effects=True,
                                             vmem_limit_bytes=32 << 20),
    )(rows)


def finish_kernel(faces_ref, own_ref, ghost_ref, out_ref, ghost_t, full_t):
    @pl.loop(0, OWN // 128, unroll=8)
    def _(b):
        full_t[pl.ds(pl.multiple_of(b * 128, 128), 128), :] = jnp.zeros((128, 16), jnp.float32)

    @pl.loop(0, 2 * FACE // 128, unroll=8)
    def _(b):
        at = pl.ds(pl.multiple_of(b * 128, 128), 128)
        ghost_t[at, :] = ghost_ref[:, at].T

    for f in range(2):
        @pl.loop(0, FACE // 16)
        def _(b):
            for k in range(16):
                full_t[pl.ds(faces_ref[f, b * 16 + k], 1), :] = ghost_t[pl.ds(f * FACE + b * 16 + k, 1), :]

    @pl.loop(0, OWN // 128, unroll=8)
    def _(b):
        at = pl.ds(pl.multiple_of(b * 128, 128), 128)
        out_ref[:, at] = own_ref[:, at] + full_t[at, :].T


def finish(faces, own, ghost):
    vmem = pl.BlockSpec(memory_space=pltpu.VMEM)
    return pl.pallas_call(
        finish_kernel,
        name="finish",
        out_shape=jax.ShapeDtypeStruct((16, OWN), jnp.float32),
        in_specs=[pl.BlockSpec(memory_space=pltpu.SMEM), vmem, vmem],
        out_specs=vmem,
        scratch_shapes=[pltpu.VMEM((2 * FACE, 16), jnp.float32), pltpu.VMEM((OWN, 16), jnp.float32)],
        compiler_params=pltpu.CompilerParams(vmem_limit_bytes=40 << 20),
    )(faces, own, ghost)


def per_device(field_in, faces, connectivity, curl_vectors, operating_point, material, bh_knots, curve_base,
               curve_slopes):
    point = jnp.transpose(operating_point, (1, 2, 3, 0))
    contributions = forward(field_in, point, material, curl_vectors, faces, connectivity, bh_knots, curve_base,
                            curve_slopes)
    own, ghost = combine(scatter(connectivity, contributions))
    return finish(faces, own, ghost)


def solution(mesh):
    return jax.shard_map(
        per_device,
        mesh=mesh,
        in_specs=(P("harm", "mesh"), P(None, "mesh"), P(None, "mesh"), P(None, None, "mesh"),
                  P(None, None, None, ("mesh", "harm")), P(None, ("mesh", "harm")), P(), P(), P()),
        out_specs=P("harm", "mesh"),
        check_vma=False,
    )
```

```python
import functools

import numpy as np
import jax
import jax.numpy as jnp
from jax import lax
from jax.experimental import pallas as pl
from jax.experimental.pallas import tpu as pltpu
from jax.sharding import PartitionSpec as P

MESH = pl.DeviceIdType.MESH
N_MESH = 32
OWN = 5120
FACE = 1024
EXT = OWN + 2 * FACE
ROWS = 512
MSG = 56
PARTS = 4
CHUNK = OWN // PARTS


def block_diag_tables():
    length = 64
    t = np.arange(length)
    c = np.arange(length)
    freq = np.where(c < 32, c, c - 31)
    freq[-1] = 32
    sine = (c >= 32) & (c < 63)
    angle = 2.0 * np.pi * ((freq[:, None] * t[None, :]) % length) / length
    basis = np.where(sine[:, None], np.sin(angle), np.cos(angle))
    weight = np.where((c == 0) | (c == 63), 1.0 / length, 2.0 / length)
    inverse = np.kron(np.eye(2), basis)
    forward = np.kron(np.eye(2), (basis * weight[:, None]).T)
    return inverse.astype(np.float32), forward.astype(np.float32)


def forward_kernel(field_ref, point_ref, mat_ref, curl_ref, faces_hbm, conn_hbm, knots_ref, base_ref, slopes_ref,
                   inv_ref, fwd_ref, out_ref,
                   field, point, curl, opsend, op_in, field_t, face_rows, face_cols, ext, ext2, curl_t, wide, got, flux, faces_ref, conn_ref,
                   in_s, op_ss, op_rs, far_ss, far_rs, side_ss, side_rs, gh_ss, gh_rs, fw_ss, fw_rs, rel_ss, rel_rs, idx_s):
    m = lax.axis_index("mesh")
    h = lax.axis_index("harm")
    up, down = lax.rem(m + 1, N_MESH), lax.rem(m + N_MESH - 1, N_MESH)
    side = h + 1 - 2 * lax.rem(h, 2)
    far = lax.rem(h + 2, 4)
    half = m // 16

    def block_of(source, target):
        crossing = (source // 16 + target // 16) % 2
        return lax.rem(h + 2 * crossing * lax.rem(source, 2), 4)

    load_field = pltpu.make_async_copy(field_ref, field, in_s.at[0])
    load_point = pltpu.make_async_copy(point_ref, point, in_s.at[1])
    load_curl = pltpu.make_async_copy(curl_ref, curl, in_s.at[2])
    load_field.start()
    load_point.start()
    load_curl.start()
    load_faces = [pltpu.make_async_copy(faces_hbm.at[f], faces_ref.at[pl.ds(f * FACE, FACE)], idx_s.at[f])
                  for f in range(2)]
    load_conn = [pltpu.make_async_copy(conn_hbm.at[j], conn_ref.at[pl.ds(j * 4096, 4096)], idx_s.at[2 + j])
                 for j in range(6)]
    for c in (*load_faces, *load_conn):
        c.start()

    barrier = pltpu.get_barrier_semaphore()
    for peer in ((m, far), (m, side), (up, h), (down, h)):
        pl.semaphore_signal(barrier, inc=1, device_id=peer, device_id_type=MESH)

    @pl.loop(1, N_MESH)
    def _(d):
        source = lax.rem(m + N_MESH - d, N_MESH)
        pl.semaphore_signal(barrier, inc=1, device_id=(source, block_of(source, m)), device_id_type=MESH)

    load_field.wait()

    @pl.loop(0, OWN // 128, unroll=8)
    def _(b):
        at = pl.ds(pl.multiple_of(b * 128, 128), 128)
        field_t[at, :] = field[:, at].T

    pl.semaphore_wait(barrier, N_MESH - 1 + 4)

    def rows_of(who):
        return pl.ds(pl.multiple_of(16 * who, 16), 16)

    ghost_cols = pl.ds(OWN, 2 * FACE)

    def cols_of(c):
        return pl.ds(c * CHUNK, CHUNK)

    def own_copy(c, peer, ss, rs):
        return pltpu.make_async_remote_copy(
            src_ref=field.at[:, cols_of(c)], dst_ref=ext.at[rows_of(h), cols_of(c)],
            send_sem=ss.at[c], recv_sem=rs.at[c],
            device_id=(m, peer), device_id_type=MESH)

    to_far = [own_copy(c, far, far_ss, far_rs) for c in range(PARTS)]
    to_side = [own_copy(c, side, side_ss, side_rs) for c in range(PARTS)]
    for c in (*to_far, *to_side):
        c.start()
    keep = pltpu.make_async_copy(field, ext.at[rows_of(h), pl.ds(0, OWN)], in_s.at[3])
    keep.start()

    for c in load_faces:
        c.wait()

    @pl.loop(0, 2 * FACE // 32)
    def _(b):
        near = faces_ref.at[pl.ds(pl.multiple_of(b * 32, 32), 32)]
        to = face_rows.at[pl.ds(pl.multiple_of(b * 32, 32), 32), :]
        for k in range(32):
            to[pl.ds(k, 1), :] = field_t[pl.ds(near[k], 1), :]

    @pl.loop(0, 2 * FACE // 128, unroll=8)
    def _(b):
        at = pl.ds(pl.multiple_of(b * 128, 128), 128)
        face_cols[:, at] = face_rows[at, :].T

    def ghost_copy(f, peer):
        return pltpu.make_async_remote_copy(
            src_ref=face_cols.at[:, pl.ds(f * FACE, FACE)],
            dst_ref=ext.at[rows_of(h), pl.ds(OWN + (1 - f) * FACE, FACE)],
            send_sem=gh_ss.at[f], recv_sem=gh_rs.at[f],
            device_id=(peer, h), device_id_type=MESH)

    ghosts = [ghost_copy(0, down), ghost_copy(1, up)]
    for c in ghosts:
        c.start()

    load_point.wait()

    @pl.loop(0, N_MESH)
    def _(p):
        for i in range(3):
            opsend[p, pl.ds(16 * i, 16), pl.ds(0, 64)] = point[i, p, pl.ds(0, 16), :]
            opsend[p, pl.ds(16 * i, 16), pl.ds(64, 64)] = point[i, p, pl.ds(16, 16), :]
        opsend[p, pl.ds(48, 8), :] = jnp.zeros((8, 128), jnp.float32)
        opsend[p, pl.ds(48, 1), pl.ds(0, 32)] = mat_ref[pl.ds(p, 1), :].astype(jnp.float32)

    def op_copy(d):
        p = lax.rem(m + d, N_MESH)
        target = lax.rem(h + 2 * ((half + p // 16) % 2) * lax.rem(m, 2), 4)
        return pltpu.make_async_remote_copy(
            src_ref=opsend.at[p], dst_ref=op_in.at[m],
            send_sem=op_ss.at[d], recv_sem=op_rs.at[d],
            device_id=(p, target), device_id_type=MESH)

    @pl.loop(1, N_MESH)
    def _(d):
        op_copy(d).start()
    op_keep = pltpu.make_async_copy(opsend.at[m], op_in.at[m], in_s.at[4])
    op_keep.start()

    for c in ghosts:
        c.wait_recv()

    def gfwd_copy(n, peer):
        return pltpu.make_async_remote_copy(
            src_ref=ext.at[rows_of(h), ghost_cols], dst_ref=ext.at[rows_of(h), ghost_cols],
            send_sem=fw_ss.at[n], recv_sem=fw_rs.at[n],
            device_id=(m, peer), device_id_type=MESH)

    gfar, gside = gfwd_copy(0, far), gfwd_copy(1, side)
    gfar.start()
    gside.start()

    def relay(c, cols):
        return pltpu.make_async_remote_copy(
            src_ref=ext.at[rows_of(far), cols], dst_ref=ext.at[rows_of(far), cols],
            send_sem=rel_ss.at[c], recv_sem=rel_rs.at[c],
            device_id=(m, side), device_id_type=MESH)

    relays = [relay(c, cols_of(c)) for c in range(PARTS)] + [relay(PARTS, ghost_cols)]

    low = lax.broadcasted_iota(jnp.int32, (16, 128), 1) < 64
    low1 = lax.broadcasted_iota(jnp.int32, (1, 128), 1) < 64

    load_curl.wait()

    @pl.loop(0, N_MESH, unroll=4)
    def _(s):
        at = pl.ds(pl.multiple_of(s * 128, 128), 128)
        pad = jnp.zeros((2, 128), jnp.float32)
        parts = []
        for i in range(3):
            parts += [curl[i, :, at], pad]
        curl_t[at, :] = jnp.concatenate(parts, axis=0).T

    for c in range(PARTS):
        @pl.loop(c * N_MESH // PARTS, (c + 1) * N_MESH // PARTS)
        def _(s):
            to = pl.ds(pl.multiple_of(s * 16, 16), 16)
            first = s * 128 + block_of(s, m) * 32
            c0 = curl_t[pl.ds(pl.multiple_of(first, 16), 16), :]
            c1 = curl_t[pl.ds(pl.multiple_of(first + 16, 16), 16), :]
            for i in range(3):
                for j in range(6):
                    col = i * 8 + j
                    wide[i * 6 + j, to, :] = jnp.where(low, jnp.broadcast_to(c0[:, col:col + 1], (16, 128)),
                                                       jnp.broadcast_to(c1[:, col:col + 1], (16, 128)))
        to_far[c].wait_recv()
        relays[c].start()
    gfar.wait_recv()
    relays[PARTS].start()

    for c in load_conn:
        c.wait()
    keep.wait()
    for c in range(PARTS + 1):
        if c < PARTS:
            to_side[c].wait_recv()
        else:
            gside.wait_recv()
        relays[c].wait_recv()
        blocks = CHUNK // 128 if c < PARTS else 2 * FACE // 128

        @pl.loop(0, blocks, unroll=2)
        def _(b):
            at = pl.ds(pl.multiple_of(c * CHUNK + b * 128, 128), 128)
            x = ext[:, at]
            ext2[at, :] = jnp.concatenate([x, x], axis=0).T

    @pl.loop(0, N_MESH)
    def _(s):
        to = pl.ds(pl.multiple_of(s * 16, 16), 16)
        first = pl.multiple_of(s * 128 + block_of(s, m) * 32, 32)
        near = conn_ref.at[pl.ds(first, 5 * 4096 + 32)]
        for j in range(6):
            for k in range(16):
                a = ext2[pl.ds(near[j * 4096 + k], 1), :]
                b = ext2[pl.ds(near[j * 4096 + 16 + k], 1), :]
                got[pl.ds(j * 16 + k, 1), :] = jnp.where(low1, a, b)
        for i in range(3):
            s_i = wide[i * 6, to, :] * got[0:16, :]
            for j in range(1, 6):
                s_i = s_i + wide[i * 6 + j, to, :] * got[j * 16:(j + 1) * 16, :]
            flux[i, to, :] = s_i

    @pl.loop(1, N_MESH)
    def _(d):
        op_copy(d).wait_recv()

    op_keep.wait()
    growth = [jnp.exp(jnp.float32(-0.5) * knots_ref[k].astype(jnp.float32)) for k in range(8)]

    @pl.loop(0, ROWS // 64)
    def _(r):
        to = pl.ds(pl.multiple_of(r * 64, 64), 64)
        f = [jnp.dot(flux[i, to, :], inv_ref[...], precision=lax.Precision.HIGHEST,
                     preferred_element_type=jnp.float32) for i in range(3)]
        b = [jnp.concatenate([op_in[r * 4 + s, 16 * i:16 * i + 16, :] for s in range(4)], axis=0)
             for i in range(3)]
        kinds = []
        for s in range(4):
            mt = jnp.broadcast_to(op_in[r * 4 + s, pl.ds(48, 1), :], (8, 128)).T
            kinds.append(jnp.where(low, jnp.broadcast_to(mt[0:16, 0:1], (16, 128)),
                                   jnp.broadcast_to(mt[16:32, 0:1], (16, 128))))
        mat = jnp.concatenate(kinds, axis=0)

        def pick(values):
            x = jnp.where(mat == 1.0, values[1], values[0])
            x = jnp.where(mat == 2.0, values[2], x)
            return jnp.where(mat == 3.0, values[3], x)

        q = b[0] * b[0] + b[1] * b[1] + b[2] * b[2]
        u = jnp.exp(2.0 * q)
        nu = pick([base_ref[a] for a in range(4)])
        dnu = jnp.zeros_like(q)
        for k in range(8):
            slope = pick([slopes_ref[a, k] for a in range(4)])
            e = u * growth[k]
            w = 1.0 + e
            nu = nu + slope * jnp.log(w)
            dnu = dnu + slope * (e / w)
        proj = b[0] * f[0] + b[1] * f[1] + b[2] * f[2]
        scale = 4.0 * dnu * proj
        f = [jnp.dot(nu * f[i] + scale * b[i], fwd_ref[...], precision=lax.Precision.HIGHEST,
                     preferred_element_type=jnp.float32) for i in range(3)]
        for j in range(6):
            out_ref[pl.ds(pl.multiple_of(j * ROWS + r * 64, 64), 64), :] = (
                wide[j, to, :] * f[0] + wide[6 + j, to, :] * f[1] + wide[12 + j, to, :] * f[2])

    for c in (*to_far, *to_side, *ghosts, gfar, gside, *relays):
        c.wait_send()

    @pl.loop(1, N_MESH)
    def _(d):
        op_copy(d).wait_send()


def forward(field, point, material, curl, faces, conn, knots, base, slopes):
    inverse, forward_table = block_diag_tables()
    smem = pl.BlockSpec(memory_space=pltpu.SMEM)
    vmem = pl.BlockSpec(memory_space=pltpu.VMEM)
    hbm = pl.BlockSpec(memory_space=pl.ANY)
    f32 = jnp.float32
    dma = pltpu.SemaphoreType.DMA
    return pl.pallas_call(
        forward_kernel,
        name="forward",
        out_shape=jax.ShapeDtypeStruct((6 * ROWS, 128), f32),
        in_specs=[hbm, hbm, vmem, hbm, hbm, hbm, smem, smem, smem, vmem, vmem],
        out_specs=vmem,
        scratch_shapes=[
            pltpu.VMEM((16, OWN), f32), pltpu.VMEM((3, 32, 32, 64), f32), pltpu.VMEM((3, 6, 4096), f32),
            pltpu.VMEM((N_MESH, MSG, 128), f32), pltpu.VMEM((N_MESH, MSG, 128), f32),
            pltpu.VMEM((OWN, 16), f32), pltpu.VMEM((2 * FACE, 16), f32), pltpu.VMEM((16, 2 * FACE), f32),
            pltpu.VMEM((64, EXT), f32), pltpu.VMEM((EXT, 128), f32), pltpu.VMEM((4096, 24), f32),
            pltpu.VMEM((18, ROWS, 128), f32), pltpu.VMEM((96, 128), f32), pltpu.VMEM((3, ROWS, 128), f32),
            pltpu.SMEM((2 * FACE,), jnp.int32), pltpu.SMEM((6 * 4096,), jnp.int32),
            dma((5,)), dma((N_MESH,)), dma((N_MESH,)), dma((PARTS,)), dma((PARTS,)), dma((PARTS,)), dma((PARTS,)),
            dma((2,)), dma((2,)), dma((2,)), dma((2,)), dma((PARTS + 1,)), dma((PARTS + 1,)), dma((8,)),
        ],
        compiler_params=pltpu.CompilerParams(collective_id=0, has_side_effects=True,
                                             vmem_limit_bytes=60 << 20),
    )(field, point, material, curl, faces, conn, knots, base, slopes, jnp.asarray(inverse), jnp.asarray(forward_table))


def scatter_kernel(conn_hbm, con_ref, out_ref, acc0, acc1, acc2, acc3, acc4, acc5, conn_ref, sem):
    m = lax.axis_index("mesh")
    h = lax.axis_index("harm")
    accs = (acc0, acc1, acc2, acc3, acc4, acc5)
    low = lax.broadcasted_iota(jnp.int32, (64, 128), 1) < 64

    def block_of(source, target):
        crossing = (source // 16 + target // 16) % 2
        return lax.rem(h + 2 * crossing * lax.rem(source, 2), 4)

    loads = [pltpu.make_async_copy(conn_hbm.at[j], conn_ref.at[pl.ds(j * 4096, 4096)], sem.at[j]) for j in range(6)]
    for c in loads:
        c.start()

    @pl.loop(0, EXT // 64)
    def _(b):
        at = pl.ds(pl.multiple_of(b * 64, 64), 64)
        for a in accs:
            a[at, :] = jnp.zeros((64, 128), jnp.float32)

    for c in loads:
        c.wait()

    @pl.loop(0, N_MESH)
    def _(s):
        first = pl.multiple_of(s * 128 + block_of(s, m) * 32, 32)
        near = conn_ref.at[pl.ds(first, 5 * 4096 + 32)]
        for k in range(16):
            for j in range(6):
                row = con_ref[pl.ds(j * ROWS + s * 16 + k, 1), :]
                n0 = near[j * 4096 + k]
                n1 = near[j * 4096 + 16 + k]
                a0, a1 = accs[j % 3], accs[3 + j % 3]
                a0[pl.ds(n0, 1), :] = a0[pl.ds(n0, 1), :] + row
                a1[pl.ds(n1, 1), :] = a1[pl.ds(n1, 1), :] + row

    @pl.loop(0, EXT // 64, unroll=2)
    def _(b):
        at = pl.ds(pl.multiple_of(b * 64, 64), 64)
        out_ref[at, :] = jnp.where(low, acc0[at, :] + acc1[at, :] + acc2[at, :], acc3[at, :] + acc4[at, :] + acc5[at, :])


def scatter(conn, con):
    vmem = pl.BlockSpec(memory_space=pltpu.VMEM)
    big = pltpu.VMEM((EXT, 128), jnp.float32)
    return pl.pallas_call(
        scatter_kernel,
        name="scatter",
        out_shape=jax.ShapeDtypeStruct((EXT, 128), jnp.float32),
        in_specs=[pl.BlockSpec(memory_space=pl.ANY), vmem],
        out_specs=vmem,
        scratch_shapes=[big, big, big, big, big, big, pltpu.SMEM((6 * 4096,), jnp.int32), pltpu.SemaphoreType.DMA((6,))],
        compiler_params=pltpu.CompilerParams(vmem_limit_bytes=32 << 20),
    )(conn, con)


def combine_kernel(rows_ref, own_out, ghost_out, acc, pairs, summed, zin, ghost_sum, ghost_in,
                   p_ss, p_rs, z_ss, z_rs, g_ss, g_rs):
    m = lax.axis_index("mesh")
    h = lax.axis_index("harm")
    up, down = lax.rem(m + 1, N_MESH), lax.rem(m + N_MESH - 1, N_MESH)
    side = h + 1 - 2 * lax.rem(h, 2)
    far = lax.rem(h + 2, 4)
    cross = lax.rem(side + 2, 4)
    barrier = pltpu.get_barrier_semaphore()
    for peer in ((m, side), (m, far), (up, h), (down, h)):
        pl.semaphore_signal(barrier, inc=1, device_id=peer, device_id_type=MESH)

    bounds = [(OWN, 2 * FACE)] + [(c * CHUNK, CHUNK) for c in range(PARTS)]
    chunks = [pl.ds(a, n) for a, n in bounds]

    def block(who):
        return pl.ds(pl.multiple_of(16 * who, 16), 16)

    def turn(c):
        start, n = bounds[c]

        @pl.loop(0, n // 128, unroll=2)
        def _(b):
            at = pl.ds(pl.multiple_of(start + b * 128, 128), 128)
            x = rows_ref[at, :].T
            acc[:, at] = x[0:64, :] + x[64:128, :]

    def pair_copy(c, n):
        return pltpu.make_async_remote_copy(
            src_ref=acc.at[block((side, cross)[n]), chunks[c]], dst_ref=pairs.at[n, :, chunks[c]],
            send_sem=p_ss.at[c, n], recv_sem=p_rs.at[c, n],
            device_id=(m, side), device_id_type=MESH)

    def z_copy(c):
        return pltpu.make_async_remote_copy(
            src_ref=summed.at[:, chunks[c]], dst_ref=zin.at[:, chunks[c]],
            send_sem=z_ss.at[c], recv_sem=z_rs.at[c],
            device_id=(m, far), device_id_type=MESH)

    def g_copy(f, peer):
        return pltpu.make_async_remote_copy(
            src_ref=ghost_sum.at[:, pl.ds(f * FACE, FACE)],
            dst_ref=ghost_in.at[:, pl.ds((1 - f) * FACE, FACE)],
            send_sem=g_ss.at[f], recv_sem=g_rs.at[f],
            device_id=(peer, h), device_id_type=MESH)

    count = PARTS + 1
    far_pairs = [pair_copy(c, 1) for c in range(count)]
    own_pairs = [pair_copy(c, 0) for c in range(count)]
    zs = [z_copy(c) for c in range(count)]
    gs = [g_copy(0, down), g_copy(1, up)]

    turn(0)
    pl.semaphore_wait(barrier, 4)
    far_pairs[0].start()
    own_pairs[0].start()
    for c in range(count):
        if c + 1 < count:
            turn(c + 1)
            far_pairs[c + 1].start()
            own_pairs[c + 1].start()
        far_pairs[c].wait_recv()
        summed[:, chunks[c]] = acc[block(far), chunks[c]] + pairs[1, :, chunks[c]]
        zs[c].start()

    def total(c):
        own_pairs[c].wait_recv()
        zs[c].wait_recv()
        return acc[block(h), chunks[c]] + pairs[0, :, chunks[c]] + zin[:, chunks[c]]

    ghost_sum[...] = total(0)
    for g in gs:
        g.start()
    for c in range(1, count):
        own_out[:, chunks[c]] = total(c)
    for g in gs:
        g.wait_recv()
    ghost_out[...] = ghost_in[...]
    for c in (*far_pairs, *own_pairs, *zs, *gs):
        c.wait_send()


def combine(rows):
    vmem = pl.BlockSpec(memory_space=pltpu.VMEM)
    dma = pltpu.SemaphoreType.DMA
    f32 = jnp.float32
    return pl.pallas_call(
        combine_kernel,
        name="combine",
        out_shape=(jax.ShapeDtypeStruct((16, OWN), f32), jax.ShapeDtypeStruct((16, 2 * FACE), f32)),
        in_specs=[vmem],
        out_specs=(vmem, vmem),
        scratch_shapes=[
            pltpu.VMEM((64, EXT), f32), pltpu.VMEM((2, 16, EXT), f32), pltpu.VMEM((16, EXT), f32),
            pltpu.VMEM((16, EXT), f32), pltpu.VMEM((16, 2 * FACE), f32), pltpu.VMEM((16, 2 * FACE), f32),
            dma((PARTS + 1, 2)), dma((PARTS + 1, 2)), dma((PARTS + 1,)), dma((PARTS + 1,)), dma((2,)), dma((2,)),
        ],
        compiler_params=pltpu.CompilerParams(collective_id=1, has_side_effects=True,
                                             vmem_limit_bytes=32 << 20),
    )(rows)


def finish_kernel(faces_hbm, own_ref, ghost_ref, out_ref, ghost_t, full_t, faces_ref, idx_s):
    loads = [pltpu.make_async_copy(faces_hbm.at[f], faces_ref.at[pl.ds(f * FACE, FACE)], idx_s.at[f])
             for f in range(2)]
    for c in loads:
        c.start()

    @pl.loop(0, OWN // 128, unroll=8)
    def _(b):
        full_t[pl.ds(pl.multiple_of(b * 128, 128), 128), :] = jnp.zeros((128, 16), jnp.float32)

    @pl.loop(0, 2 * FACE // 128, unroll=8)
    def _(b):
        at = pl.ds(pl.multiple_of(b * 128, 128), 128)
        ghost_t[at, :] = ghost_ref[:, at].T

    for c in loads:
        c.wait()

    @pl.loop(0, 2 * FACE // 32)
    def _(b):
        near = faces_ref.at[pl.ds(pl.multiple_of(b * 32, 32), 32)]
        rows = ghost_t.at[pl.ds(pl.multiple_of(b * 32, 32), 32), :]
        for k in range(32):
            full_t[pl.ds(near[k], 1), :] = rows[pl.ds(k, 1), :]

    @pl.loop(0, OWN // 128, unroll=8)
    def _(b):
        at = pl.ds(pl.multiple_of(b * 128, 128), 128)
        out_ref[:, at] = own_ref[:, at] + full_t[at, :].T


def finish(faces, own, ghost):
    vmem = pl.BlockSpec(memory_space=pltpu.VMEM)
    return pl.pallas_call(
        finish_kernel,
        name="finish",
        out_shape=jax.ShapeDtypeStruct((16, OWN), jnp.float32),
        in_specs=[pl.BlockSpec(memory_space=pl.ANY), vmem, vmem],
        out_specs=vmem,
        scratch_shapes=[pltpu.VMEM((2 * FACE, 16), jnp.float32), pltpu.VMEM((OWN, 16), jnp.float32),
                        pltpu.SMEM((2 * FACE,), jnp.int32), pltpu.SemaphoreType.DMA((2,))],
        compiler_params=pltpu.CompilerParams(vmem_limit_bytes=40 << 20),
    )(faces, own, ghost)


def per_device(field_in, faces, connectivity, curl_vectors, operating_point, material, bh_knots, curve_base,
               curve_slopes):
    point = jnp.transpose(operating_point, (1, 2, 3, 0))
    contributions = forward(field_in, point, material, curl_vectors, faces, connectivity, bh_knots, curve_base,
                            curve_slopes)
    own, ghost = combine(scatter(connectivity, contributions))
    return finish(faces, own, ghost)


def solution(mesh):
    return jax.shard_map(
        per_device,
        mesh=mesh,
        in_specs=(P("harm", "mesh"), P(None, "mesh"), P(None, "mesh"), P(None, None, "mesh"),
                  P(None, None, None, ("mesh", "harm")), P(None, ("mesh", "harm")), P(), P(), P()),
        out_specs=P("harm", "mesh"),
        check_vma=False,
    )
```

```python
import functools

import numpy as np
import jax
import jax.numpy as jnp
from jax import lax
from jax.experimental import pallas as pl
from jax.experimental.pallas import tpu as pltpu
from jax.sharding import PartitionSpec as P

MESH = pl.DeviceIdType.MESH
N_MESH = 32
OWN = 5120
FACE = 1024
EXT = OWN + 2 * FACE
ROWS = 512
MSG = 56
PARTS = 4
CHUNK = OWN // PARTS


def block_diag_tables():
    length = 64
    t = np.arange(length)
    c = np.arange(length)
    freq = np.where(c < 32, c, c - 31)
    freq[-1] = 32
    sine = (c >= 32) & (c < 63)
    angle = 2.0 * np.pi * ((freq[:, None] * t[None, :]) % length) / length
    basis = np.where(sine[:, None], np.sin(angle), np.cos(angle))
    weight = np.where((c == 0) | (c == 63), 1.0 / length, 2.0 / length)
    inverse = np.kron(np.eye(2), basis)
    forward = np.kron(np.eye(2), (basis * weight[:, None]).T)
    return split_table(inverse), split_table(forward)


def split_table(table):
    high = table.astype(jnp.bfloat16)
    rest = (table - high.astype(np.float64)).astype(jnp.bfloat16)
    return np.block([[high, rest], [high, np.zeros_like(rest)]])


def transform(parts, table_ref):
    x = jnp.concatenate(parts, axis=0)
    high = x.astype(jnp.bfloat16)
    rest = (x - high.astype(jnp.float32)).astype(jnp.bfloat16)
    y = jnp.dot(jnp.concatenate([high, rest], axis=1), table_ref[...], preferred_element_type=jnp.float32)
    y = y[:, 0:128] + y[:, 128:256]
    n = parts[0].shape[0]
    return [y[i * n:(i + 1) * n, :] for i in range(len(parts))]


def forward_kernel(field_ref, point_ref, mat_ref, curl_ref, faces_hbm, conn_hbm, knots_ref, base_ref, slopes_ref,
                   inv_hbm, fwd_hbm, out_ref,
                   field, point, curl, opsend, op_in, field_t, face_rows, face_cols, ext, ext2, curl_t, wide, got, flux, inv_ref, fwd_ref, faces_ref, conn_ref,
                   in_s, op_ss, op_rs, far_ss, far_rs, side_ss, side_rs, gh_ss, gh_rs, fw_ss, fw_rs, rel_ss, rel_rs, idx_s):
    m = lax.axis_index("mesh")
    h = lax.axis_index("harm")
    up, down = lax.rem(m + 1, N_MESH), lax.rem(m + N_MESH - 1, N_MESH)
    side = h + 1 - 2 * lax.rem(h, 2)
    far = lax.rem(h + 2, 4)
    half = m // 16

    def block_of(source, target):
        crossing = (source // 16 + target // 16) % 2
        return lax.rem(h + 2 * crossing * lax.rem(source, 2), 4)

    load_field = pltpu.make_async_copy(field_ref, field, in_s.at[0])
    load_point = pltpu.make_async_copy(point_ref, point, in_s.at[1])
    load_curl = pltpu.make_async_copy(curl_ref, curl, in_s.at[2])
    load_field.start()
    load_point.start()
    load_curl.start()
    load_faces = [pltpu.make_async_copy(faces_hbm.at[f], faces_ref.at[pl.ds(f * FACE, FACE)], idx_s.at[f])
                  for f in range(2)]
    load_conn = [pltpu.make_async_copy(conn_hbm.at[j], conn_ref.at[pl.ds(j * 4096, 4096)], idx_s.at[2 + j])
                 for j in range(6)]
    load_conn.append(pltpu.make_async_copy(inv_hbm, inv_ref, idx_s.at[8]))
    load_conn.append(pltpu.make_async_copy(fwd_hbm, fwd_ref, idx_s.at[9]))
    for c in (*load_faces, *load_conn):
        c.start()

    barrier = pltpu.get_barrier_semaphore()
    for peer in ((m, far), (m, side), (up, h), (down, h)):
        pl.semaphore_signal(barrier, inc=1, device_id=peer, device_id_type=MESH)

    @pl.loop(1, N_MESH)
    def _(d):
        source = lax.rem(m + N_MESH - d, N_MESH)
        pl.semaphore_signal(barrier, inc=1, device_id=(source, block_of(source, m)), device_id_type=MESH)

    load_field.wait()

    @pl.loop(0, OWN // 128, unroll=8)
    def _(b):
        at = pl.ds(pl.multiple_of(b * 128, 128), 128)
        field_t[at, :] = field[:, at].T

    pl.semaphore_wait(barrier, N_MESH - 1 + 4)

    def rows_of(who):
        return pl.ds(pl.multiple_of(16 * who, 16), 16)

    ghost_cols = pl.ds(OWN, 2 * FACE)

    def cols_of(c):
        return pl.ds(c * CHUNK, CHUNK)

    def own_copy(c, peer, ss, rs):
        return pltpu.make_async_remote_copy(
            src_ref=field.at[:, cols_of(c)], dst_ref=ext.at[rows_of(h), cols_of(c)],
            send_sem=ss.at[c], recv_sem=rs.at[c],
            device_id=(m, peer), device_id_type=MESH)

    to_far = [own_copy(c, far, far_ss, far_rs) for c in range(PARTS)]
    to_side = [own_copy(c, side, side_ss, side_rs) for c in range(PARTS)]
    for c in (*to_far, *to_side):
        c.start()
    keep = pltpu.make_async_copy(field, ext.at[rows_of(h), pl.ds(0, OWN)], in_s.at[3])
    keep.start()

    for c in load_faces:
        c.wait()

    @pl.loop(0, 2 * FACE // 32)
    def _(b):
        near = faces_ref.at[pl.ds(pl.multiple_of(b * 32, 32), 32)]
        to = face_rows.at[pl.ds(pl.multiple_of(b * 32, 32), 32), :]
        for k in range(32):
            to[pl.ds(k, 1), :] = field_t[pl.ds(near[k], 1), :]

    @pl.loop(0, 2 * FACE // 128, unroll=8)
    def _(b):
        at = pl.ds(pl.multiple_of(b * 128, 128), 128)
        face_cols[:, at] = face_rows[at, :].T

    def ghost_copy(f, peer):
        return pltpu.make_async_remote_copy(
            src_ref=face_cols.at[:, pl.ds(f * FACE, FACE)],
            dst_ref=ext.at[rows_of(h), pl.ds(OWN + (1 - f) * FACE, FACE)],
            send_sem=gh_ss.at[f], recv_sem=gh_rs.at[f],
            device_id=(peer, h), device_id_type=MESH)

    ghosts = [ghost_copy(0, down), ghost_copy(1, up)]
    for c in ghosts:
        c.start()

    load_point.wait()

    @pl.loop(0, N_MESH)
    def _(p):
        for i in range(3):
            opsend[p, pl.ds(16 * i, 16), pl.ds(0, 64)] = point[i, p, pl.ds(0, 16), :]
            opsend[p, pl.ds(16 * i, 16), pl.ds(64, 64)] = point[i, p, pl.ds(16, 16), :]
        opsend[p, pl.ds(48, 8), :] = jnp.zeros((8, 128), jnp.float32)
        opsend[p, pl.ds(48, 1), pl.ds(0, 32)] = mat_ref[pl.ds(p, 1), :].astype(jnp.float32)

    within = lax.rem(m, 16)

    def op_copy(slot):
        cross = slot // 16
        p = lax.rem(half + cross, 2) * 16 + lax.rem(within + slot, 16)
        target = lax.rem(h + 2 * cross * lax.rem(m, 2), 4)
        return pltpu.make_async_remote_copy(
            src_ref=opsend.at[p], dst_ref=op_in.at[m],
            send_sem=op_ss.at[slot], recv_sem=op_rs.at[slot],
            device_id=(p, target), device_id_type=MESH)

    @pl.loop(1, 16)
    def _(slot):
        op_copy(slot).start()
    op_keep = pltpu.make_async_copy(opsend.at[m], op_in.at[m], in_s.at[4])
    op_keep.start()

    for c in ghosts:
        c.wait_recv()

    def gfwd_copy(n, peer):
        return pltpu.make_async_remote_copy(
            src_ref=ext.at[rows_of(h), ghost_cols], dst_ref=ext.at[rows_of(h), ghost_cols],
            send_sem=fw_ss.at[n], recv_sem=fw_rs.at[n],
            device_id=(m, peer), device_id_type=MESH)

    gfar, gside = gfwd_copy(0, far), gfwd_copy(1, side)
    gfar.start()
    gside.start()

    def relay(c, cols):
        return pltpu.make_async_remote_copy(
            src_ref=ext.at[rows_of(far), cols], dst_ref=ext.at[rows_of(far), cols],
            send_sem=rel_ss.at[c], recv_sem=rel_rs.at[c],
            device_id=(m, side), device_id_type=MESH)

    relays = [relay(c, cols_of(c)) for c in range(PARTS)] + [relay(PARTS, ghost_cols)]

    low = lax.broadcasted_iota(jnp.int32, (16, 128), 1) < 64
    low1 = lax.broadcasted_iota(jnp.int32, (1, 128), 1) < 64

    load_curl.wait()

    @pl.loop(0, N_MESH, unroll=4)
    def _(s):
        at = pl.ds(pl.multiple_of(s * 128, 128), 128)
        pad = jnp.zeros((2, 128), jnp.float32)
        parts = []
        for i in range(3):
            parts += [curl[i, :, at], pad]
        curl_t[at, :] = jnp.concatenate(parts, axis=0).T

    for c in range(PARTS):
        @pl.loop(c * N_MESH // PARTS, (c + 1) * N_MESH // PARTS)
        def _(s):
            to = pl.ds(pl.multiple_of(s * 16, 16), 16)
            first = s * 128 + block_of(s, m) * 32
            c0 = curl_t[pl.ds(pl.multiple_of(first, 16), 16), :]
            c1 = curl_t[pl.ds(pl.multiple_of(first + 16, 16), 16), :]
            for i in range(3):
                for j in range(6):
                    col = i * 8 + j
                    wide[i * 6 + j, to, :] = jnp.where(low, jnp.broadcast_to(c0[:, col:col + 1], (16, 128)),
                                                       jnp.broadcast_to(c1[:, col:col + 1], (16, 128)))
        to_far[c].wait_recv()
        relays[c].start()
    gfar.wait_recv()
    relays[PARTS].start()

    @pl.loop(16, N_MESH)
    def _(slot):
        op_copy(slot).start()


    for c in load_conn:
        c.wait()
    keep.wait()
    for c in range(PARTS + 1):
        if c < PARTS:
            to_side[c].wait_recv()
        else:
            gside.wait_recv()
        relays[c].wait_recv()
        blocks = CHUNK // 128 if c < PARTS else 2 * FACE // 128

        @pl.loop(0, blocks, unroll=2)
        def _(b):
            at = pl.ds(pl.multiple_of(c * CHUNK + b * 128, 128), 128)
            x = ext[:, at]
            ext2[at, :] = jnp.concatenate([x, x], axis=0).T

    @pl.loop(0, N_MESH // 2)
    def _(pair):
        for u in range(2):
            s = pair * 2 + u
            to = pl.ds(pl.multiple_of(s * 16, 16), 16)
            first = pl.multiple_of(s * 128 + block_of(s, m) * 32, 32)
            near = conn_ref.at[pl.ds(first, 5 * 4096 + 32)]
            for j in range(6):
                for k in range(16):
                    a = ext2[pl.ds(near[j * 4096 + k], 1), :]
                    b = ext2[pl.ds(near[j * 4096 + 16 + k], 1), :]
                    got[u, pl.ds(j * 16 + k, 1), :] = jnp.where(low1, a, b)
            for i in range(3):
                s_i = wide[i * 6, to, :] * got[u, 0:16, :]
                for j in range(1, 6):
                    s_i = s_i + wide[i * 6 + j, to, :] * got[u, j * 16:(j + 1) * 16, :]
                flux[i, to, :] = s_i

    @pl.loop(1, N_MESH)
    def _(slot):
        op_copy(slot).wait_recv()

    op_keep.wait()
    growth = [jnp.exp(jnp.float32(-0.5) * knots_ref[k].astype(jnp.float32)) for k in range(8)]

    @pl.loop(0, ROWS // 64)
    def _(r):
        to = pl.ds(pl.multiple_of(r * 64, 64), 64)
        f = transform([flux[i, to, :] for i in range(3)], inv_ref)
        b = [jnp.concatenate([op_in[r * 4 + s, 16 * i:16 * i + 16, :] for s in range(4)], axis=0)
             for i in range(3)]
        kinds = []
        for s in range(4):
            mt = jnp.broadcast_to(op_in[r * 4 + s, pl.ds(48, 1), :], (8, 128)).T
            kinds.append(jnp.where(low, jnp.broadcast_to(mt[0:16, 0:1], (16, 128)),
                                   jnp.broadcast_to(mt[16:32, 0:1], (16, 128))))
        mat = jnp.concatenate(kinds, axis=0)

        def pick(values):
            x = jnp.where(mat == 1.0, values[1], values[0])
            x = jnp.where(mat == 2.0, values[2], x)
            return jnp.where(mat == 3.0, values[3], x)

        q = b[0] * b[0] + b[1] * b[1] + b[2] * b[2]
        u = jnp.exp(2.0 * q)
        nu = pick([base_ref[a] for a in range(4)])
        dnu = jnp.zeros_like(q)
        for k in range(0, 8, 2):
            s0, s1 = [pick([slopes_ref[a, k + n] for a in range(4)]) for n in range(2)]
            e0, e1 = u * growth[k], u * growth[k + 1]
            w0, w1 = 1.0 + e0, 1.0 + e1
            nu = nu + s0 * jnp.log(w0) + s1 * jnp.log(w1)
            dnu = dnu + (s0 * e0 * w1 + s1 * e1 * w0) / (w0 * w1)
        proj = b[0] * f[0] + b[1] * f[1] + b[2] * f[2]
        scale = 4.0 * dnu * proj
        f = transform([nu * f[i] + scale * b[i] for i in range(3)], fwd_ref)
        for j in range(6):
            out_ref[r, j * 64:(j + 1) * 64, :] = (
                wide[j, to, :] * f[0] + wide[6 + j, to, :] * f[1] + wide[12 + j, to, :] * f[2])

    for c in (*to_far, *to_side, *ghosts, gfar, gside, *relays):
        c.wait_send()

    @pl.loop(1, N_MESH)
    def _(slot):
        op_copy(slot).wait_send()


def forward(field, point, material, curl, faces, conn, knots, base, slopes):
    inverse, forward_table = block_diag_tables()
    smem = pl.BlockSpec(memory_space=pltpu.SMEM)
    vmem = pl.BlockSpec(memory_space=pltpu.VMEM)
    hbm = pl.BlockSpec(memory_space=pltpu.HBM)
    f32 = jnp.float32
    dma = pltpu.SemaphoreType.DMA
    return pl.pallas_call(
        forward_kernel,
        name="forward",
        out_shape=jax.ShapeDtypeStruct((ROWS // 64, 384, 128), f32),
        in_specs=[hbm, hbm, vmem, hbm, hbm, hbm, smem, smem, smem, hbm, hbm],
        out_specs=vmem,
        scratch_shapes=[
            pltpu.VMEM((16, OWN), f32), pltpu.VMEM((3, 32, 32, 64), f32), pltpu.VMEM((3, 6, 4096), f32),
            pltpu.VMEM((N_MESH, MSG, 128), f32), pltpu.VMEM((N_MESH, MSG, 128), f32),
            pltpu.VMEM((OWN, 16), f32), pltpu.VMEM((2 * FACE, 16), f32), pltpu.VMEM((16, 2 * FACE), f32),
            pltpu.VMEM((64, EXT), f32), pltpu.VMEM((EXT, 128), f32), pltpu.VMEM((4096, 24), f32),
            pltpu.VMEM((18, ROWS, 128), f32), pltpu.VMEM((2, 96, 128), f32), pltpu.VMEM((3, ROWS, 128), f32),
            pltpu.VMEM((256, 256), jnp.bfloat16), pltpu.VMEM((256, 256), jnp.bfloat16),
            pltpu.SMEM((2 * FACE,), jnp.int32), pltpu.SMEM((6 * 4096,), jnp.int32),
            dma((5,)), dma((N_MESH,)), dma((N_MESH,)), dma((PARTS,)), dma((PARTS,)), dma((PARTS,)), dma((PARTS,)),
            dma((2,)), dma((2,)), dma((2,)), dma((2,)), dma((PARTS + 1,)), dma((PARTS + 1,)), dma((10,)),
        ],
        compiler_params=pltpu.CompilerParams(collective_id=0, has_side_effects=True,
                                             vmem_limit_bytes=34 << 20),
    )(field, point, material, curl, faces, conn, knots, base, slopes, pltpu.with_memory_space_constraint(jnp.asarray(inverse), pltpu.HBM),
      pltpu.with_memory_space_constraint(jnp.asarray(forward_table), pltpu.HBM))


def scatter_kernel(conn_hbm, con_ref, acc0, acc1, acc2, acc3, acc4, acc5, conn_ref, sem):
    m = lax.axis_index("mesh")
    h = lax.axis_index("harm")
    accs = (acc0, acc1, acc2, acc3, acc4, acc5)

    def block_of(source, target):
        crossing = (source // 16 + target // 16) % 2
        return lax.rem(h + 2 * crossing * lax.rem(source, 2), 4)

    loads = [pltpu.make_async_copy(conn_hbm.at[j], conn_ref.at[pl.ds(j * 4096, 4096)], sem.at[j]) for j in range(6)]
    for c in loads:
        c.start()

    @pl.loop(0, EXT // 64)
    def _(b):
        at = pl.ds(pl.multiple_of(b * 64, 64), 64)
        for a in accs:
            a[at, :] = jnp.zeros((64, 128), jnp.float32)

    for c in loads:
        c.wait()

    @pl.loop(0, N_MESH)
    def _(s):
        first = pl.multiple_of(s * 128 + block_of(s, m) * 32, 32)
        near = conn_ref.at[pl.ds(first, 5 * 4096 + 32)]
        rows = con_ref.at[s // 4, pl.ds(pl.multiple_of(lax.rem(s, 4) * 16, 16), 336), :]
        for k in range(16):
            for j in range(6):
                row = rows[pl.ds(j * 64 + k, 1), :]
                n0 = near[j * 4096 + k]
                n1 = near[j * 4096 + 16 + k]
                a0, a1 = accs[j % 3], accs[3 + j % 3]
                a0[pl.ds(n0, 1), :] = a0[pl.ds(n0, 1), :] + row
                a1[pl.ds(n1, 1), :] = a1[pl.ds(n1, 1), :] + row


def scatter(conn, con):
    vmem = pl.BlockSpec(memory_space=pltpu.VMEM)
    return pl.pallas_call(
        scatter_kernel,
        name="scatter",
        out_shape=(jax.ShapeDtypeStruct((EXT, 128), jnp.float32),) * 6,
        in_specs=[pl.BlockSpec(memory_space=pltpu.HBM), vmem],
        out_specs=(vmem,) * 6,
        scratch_shapes=[pltpu.SMEM((6 * 4096,), jnp.int32), pltpu.SemaphoreType.DMA((6,))],
        compiler_params=pltpu.CompilerParams(vmem_limit_bytes=28 << 20),
    )(conn, con)


def combine_kernel(acc0, acc1, acc2, acc3, acc4, acc5, own_out, ghost_out, acc, pairs, summed, zin, ghost_sum, ghost_in,
                   p_ss, p_rs, z_ss, z_rs, g_ss, g_rs):
    m = lax.axis_index("mesh")
    h = lax.axis_index("harm")
    up, down = lax.rem(m + 1, N_MESH), lax.rem(m + N_MESH - 1, N_MESH)
    side = h + 1 - 2 * lax.rem(h, 2)
    far = lax.rem(h + 2, 4)
    cross = lax.rem(side + 2, 4)
    barrier = pltpu.get_barrier_semaphore()
    for peer in ((m, side), (m, far), (up, h), (down, h)):
        pl.semaphore_signal(barrier, inc=1, device_id=peer, device_id_type=MESH)

    bounds = [(OWN, FACE), (OWN + FACE, FACE)] + [(c * CHUNK, CHUNK) for c in range(PARTS)]
    chunks = [pl.ds(a, n) for a, n in bounds]

    def block(who):
        return pl.ds(pl.multiple_of(16 * who, 16), 16)

    low = lax.broadcasted_iota(jnp.int32, (128, 128), 1) < 64

    def turn(c):
        start, n = bounds[c]

        @pl.loop(0, n // 128, unroll=2)
        def _(b):
            at = pl.ds(pl.multiple_of(start + b * 128, 128), 128)
            x = jnp.where(low, acc0[at, :] + acc1[at, :] + acc2[at, :], acc3[at, :] + acc4[at, :] + acc5[at, :]).T
            acc[:, at] = x[0:64, :] + x[64:128, :]

    def pair_copy(c, n):
        return pltpu.make_async_remote_copy(
            src_ref=acc.at[block((side, cross)[n]), chunks[c]], dst_ref=pairs.at[n, :, chunks[c]],
            send_sem=p_ss.at[c, n], recv_sem=p_rs.at[c, n],
            device_id=(m, side), device_id_type=MESH)

    def z_copy(c):
        return pltpu.make_async_remote_copy(
            src_ref=summed.at[:, chunks[c]], dst_ref=zin.at[:, chunks[c]],
            send_sem=z_ss.at[c], recv_sem=z_rs.at[c],
            device_id=(m, far), device_id_type=MESH)

    def g_copy(f, peer):
        return pltpu.make_async_remote_copy(
            src_ref=ghost_sum.at[:, pl.ds(f * FACE, FACE)],
            dst_ref=ghost_in.at[:, pl.ds((1 - f) * FACE, FACE)],
            send_sem=g_ss.at[f], recv_sem=g_rs.at[f],
            device_id=(peer, h), device_id_type=MESH)

    count = PARTS + 2
    far_pairs = [pair_copy(c, 1) for c in range(count)]
    own_pairs = [pair_copy(c, 0) for c in range(count)]
    zs = [z_copy(c) for c in range(count)]
    gs = [g_copy(0, down), g_copy(1, up)]

    turn(0)
    pl.semaphore_wait(barrier, 4)
    far_pairs[0].start()
    own_pairs[0].start()
    for c in range(count):
        if c + 1 < count:
            turn(c + 1)
            far_pairs[c + 1].start()
            own_pairs[c + 1].start()
        far_pairs[c].wait_recv()
        summed[:, chunks[c]] = acc[block(far), chunks[c]] + pairs[1, :, chunks[c]]
        zs[c].start()

    def total(c):
        own_pairs[c].wait_recv()
        zs[c].wait_recv()
        return acc[block(h), chunks[c]] + pairs[0, :, chunks[c]] + zin[:, chunks[c]]

    for f in range(2):
        ghost_sum[:, pl.ds(f * FACE, FACE)] = total(f)
        gs[f].start()
    for c in range(2, count):
        own_out[:, chunks[c]] = total(c)
    for g in gs:
        g.wait_recv()
    ghost_out[...] = ghost_in[...]
    for c in (*far_pairs, *own_pairs, *zs, *gs):
        c.wait_send()


def combine(accs):
    vmem = pl.BlockSpec(memory_space=pltpu.VMEM)
    dma = pltpu.SemaphoreType.DMA
    f32 = jnp.float32
    return pl.pallas_call(
        combine_kernel,
        name="combine",
        out_shape=(jax.ShapeDtypeStruct((16, OWN), f32), jax.ShapeDtypeStruct((16, 2 * FACE), f32)),
        in_specs=[vmem] * 6,
        out_specs=(vmem, vmem),
        scratch_shapes=[
            pltpu.VMEM((64, EXT), f32), pltpu.VMEM((2, 16, EXT), f32), pltpu.VMEM((16, EXT), f32),
            pltpu.VMEM((16, EXT), f32), pltpu.VMEM((16, 2 * FACE), f32), pltpu.VMEM((16, 2 * FACE), f32),
            dma((PARTS + 2, 2)), dma((PARTS + 2, 2)), dma((PARTS + 2,)), dma((PARTS + 2,)), dma((2,)), dma((2,)),
        ],
        compiler_params=pltpu.CompilerParams(collective_id=1, has_side_effects=True,
                                             vmem_limit_bytes=28 << 20),
    )(*accs)


def finish_kernel(faces_hbm, own_ref, ghost_ref, out_ref, ghost_t, full_t, faces_ref, idx_s):
    loads = [pltpu.make_async_copy(faces_hbm.at[f], faces_ref.at[pl.ds(f * FACE, FACE)], idx_s.at[f])
             for f in range(2)]
    for c in loads:
        c.start()

    @pl.loop(0, OWN // 128, unroll=8)
    def _(b):
        full_t[pl.ds(pl.multiple_of(b * 128, 128), 128), :] = jnp.zeros((128, 16), jnp.float32)

    @pl.loop(0, 2 * FACE // 128, unroll=8)
    def _(b):
        at = pl.ds(pl.multiple_of(b * 128, 128), 128)
        ghost_t[at, :] = ghost_ref[:, at].T

    for c in loads:
        c.wait()

    @pl.loop(0, 2 * FACE // 32)
    def _(b):
        near = faces_ref.at[pl.ds(pl.multiple_of(b * 32, 32), 32)]
        rows = ghost_t.at[pl.ds(pl.multiple_of(b * 32, 32), 32), :]
        for k in range(32):
            full_t[pl.ds(near[k], 1), :] = rows[pl.ds(k, 1), :]

    @pl.loop(0, OWN // 128, unroll=8)
    def _(b):
        at = pl.ds(pl.multiple_of(b * 128, 128), 128)
        out_ref[:, at] = own_ref[:, at] + full_t[at, :].T


def finish(faces, own, ghost):
    vmem = pl.BlockSpec(memory_space=pltpu.VMEM)
    return pl.pallas_call(
        finish_kernel,
        name="finish",
        out_shape=jax.ShapeDtypeStruct((16, OWN), jnp.float32),
        in_specs=[pl.BlockSpec(memory_space=pl.ANY), vmem, vmem],
        out_specs=vmem,
        scratch_shapes=[pltpu.VMEM((2 * FACE, 16), jnp.float32), pltpu.VMEM((OWN, 16), jnp.float32),
                        pltpu.SMEM((2 * FACE,), jnp.int32), pltpu.SemaphoreType.DMA((2,))],
        compiler_params=pltpu.CompilerParams(vmem_limit_bytes=40 << 20),
    )(faces, own, ghost)


def per_device(field_in, faces, connectivity, curl_vectors, operating_point, material, bh_knots, curve_base,
               curve_slopes):
    point = jnp.transpose(operating_point, (1, 2, 3, 0))
    (field_in, point, material, curl_vectors, faces, connectivity, bh_knots, curve_base, curve_slopes) = [
        pltpu.with_memory_space_constraint(x, pltpu.HBM)
        for x in (field_in, point, material, curl_vectors, faces, connectivity, bh_knots, curve_base, curve_slopes)]
    contributions = forward(field_in, point, material, curl_vectors, faces, connectivity, bh_knots, curve_base,
                            curve_slopes)
    own, ghost = combine(scatter(connectivity, contributions))
    return finish(faces, own, ghost)


def solution(mesh):
    return jax.shard_map(
        per_device,
        mesh=mesh,
        in_specs=(P("harm", "mesh"), P(None, "mesh"), P(None, "mesh"), P(None, None, "mesh"),
                  P(None, None, None, ("mesh", "harm")), P(None, ("mesh", "harm")), P(), P(), P()),
        out_specs=P("harm", "mesh"),
        check_vma=False,
    )
```

```python
import functools

import numpy as np
import jax
import jax.numpy as jnp
from jax import lax
from jax.experimental import pallas as pl
from jax.experimental.pallas import tpu as pltpu
from jax.sharding import PartitionSpec as P

MESH = pl.DeviceIdType.MESH
N_MESH = 32
OWN = 5120
FACE = 1024
EXT = OWN + 2 * FACE
ROWS = 512
MSG = 56
PARTS = 4
CHUNK = OWN // PARTS
EDGE_ORDER = [(j + 3 * g, k) for g in range(2) for k in range(16) for j in range(3)]


def block_diag_tables():
    length = 64
    t = np.arange(length)
    c = np.arange(length)
    freq = np.where(c < 32, c, c - 31)
    freq[-1] = 32
    sine = (c >= 32) & (c < 63)
    angle = 2.0 * np.pi * ((freq[:, None] * t[None, :]) % length) / length
    basis = np.where(sine[:, None], np.sin(angle), np.cos(angle))
    weight = np.where((c == 0) | (c == 63), 1.0 / length, 2.0 / length)
    inverse = np.kron(np.eye(2), basis)
    forward = np.kron(np.eye(2), (basis * weight[:, None]).T)
    return split_table(inverse), split_table(forward)


def split_table(table):
    high = table.astype(jnp.bfloat16)
    rest = (table - high.astype(np.float64)).astype(jnp.bfloat16)
    return np.block([[high, rest], [high, np.zeros_like(rest)]])


def transform(parts, table_ref):
    x = jnp.concatenate(parts, axis=0)
    high = x.astype(jnp.bfloat16)
    rest = (x - high.astype(jnp.float32)).astype(jnp.bfloat16)
    y = jnp.dot(jnp.concatenate([high, rest], axis=1), table_ref[...], preferred_element_type=jnp.float32)
    y = y[:, 0:128] + y[:, 128:256]
    n = parts[0].shape[0]
    return [y[i * n:(i + 1) * n, :] for i in range(len(parts))]


def forward_kernel(field_ref, point_ref, mat_ref, curl_ref, faces_hbm, conn_hbm, knots_ref, base_ref, slopes_ref,
                   inv_hbm, fwd_hbm, out_ref,
                   field, point, curl, opsend, op_in, field_t, face_rows, face_cols, ext, ext2, curl_t, wide, got, flux, inv_ref, fwd_ref, faces_ref, conn_ref,
                   in_s, op_ss, op_rs, far_ss, far_rs, side_ss, side_rs, gh_ss, gh_rs, fw_ss, fw_rs, rel_ss, rel_rs, idx_s):
    m = lax.axis_index("mesh")
    h = lax.axis_index("harm")
    up, down = lax.rem(m + 1, N_MESH), lax.rem(m + N_MESH - 1, N_MESH)
    side = h + 1 - 2 * lax.rem(h, 2)
    far = lax.rem(h + 2, 4)
    half = m // 16

    def block_of(source, target):
        crossing = (source // 16 + target // 16) % 2
        return lax.rem(h + 2 * crossing * lax.rem(source, 2), 4)

    within = lax.rem(m, 16)
    barrier = pltpu.get_barrier_semaphore()
    crossing_h = [h, far]
    for peer in ((m, far), (m, side), (up, h), (down, h)):
        pl.semaphore_signal(barrier, inc=1, device_id=peer, device_id_type=MESH)

    @pl.loop(1, 16, unroll=3)
    def _(d):
        other = lax.rem(within + d, 16)
        pl.semaphore_signal(barrier, inc=1, device_id=(half * 16 + other, h), device_id_type=MESH)

    for odd in range(2):
        @pl.loop(0, 8, unroll=2)
        def _(d):
            pl.semaphore_signal(barrier, inc=1, device_id=((1 - half) * 16 + 2 * d + odd, crossing_h[odd]),
                                device_id_type=MESH)

    load_field = pltpu.make_async_copy(field_ref, field, in_s.at[0])
    load_point = pltpu.make_async_copy(point_ref, point, in_s.at[1])
    load_curl = pltpu.make_async_copy(curl_ref, curl, in_s.at[2])
    load_field.start()
    load_point.start()
    load_curl.start()
    load_faces = [pltpu.make_async_copy(faces_hbm.at[f], faces_ref.at[pl.ds(f * FACE, FACE)], idx_s.at[f])
                  for f in range(2)]
    load_conn = [pltpu.make_async_copy(conn_hbm.at[j], conn_ref.at[pl.ds(j * 4096, 4096)], idx_s.at[2 + j])
                 for j in range(6)]
    load_conn.append(pltpu.make_async_copy(inv_hbm, inv_ref, idx_s.at[8]))
    load_conn.append(pltpu.make_async_copy(fwd_hbm, fwd_ref, idx_s.at[9]))
    for c in (*load_faces, *load_conn):
        c.start()

    load_field.wait()

    pl.semaphore_wait(barrier, N_MESH - 1 + 4)

    def rows_of(who):
        return pl.ds(pl.multiple_of(16 * who, 16), 16)

    ghost_cols = pl.ds(OWN, 2 * FACE)

    def cols_of(c):
        return pl.ds(c * CHUNK, CHUNK)

    def own_copy(c, peer, ss, rs):
        return pltpu.make_async_remote_copy(
            src_ref=field.at[:, cols_of(c)], dst_ref=ext.at[rows_of(h), cols_of(c)],
            send_sem=ss.at[c], recv_sem=rs.at[c],
            device_id=(m, peer), device_id_type=MESH)

    to_far = [own_copy(c, far, far_ss, far_rs) for c in range(PARTS)]
    to_side = [own_copy(c, side, side_ss, side_rs) for c in range(PARTS)]
    for c in (*to_far, *to_side):
        c.start()
    keep = pltpu.make_async_copy(field, ext.at[rows_of(h), pl.ds(0, OWN)], in_s.at[3])
    keep.start()

    @pl.loop(0, OWN // 128, unroll=8)
    def _(b):
        at = pl.ds(pl.multiple_of(b * 128, 128), 128)
        field_t[at, :] = field[:, at].T

    for c in load_faces:
        c.wait()

    @pl.loop(0, 2 * FACE // 32)
    def _(b):
        near = faces_ref.at[pl.ds(pl.multiple_of(b * 32, 32), 32)]
        to = face_rows.at[pl.ds(pl.multiple_of(b * 32, 32), 32), :]
        for k in range(32):
            to[pl.ds(k, 1), :] = field_t[pl.ds(near[k], 1), :]

    @pl.loop(0, 2 * FACE // 128, unroll=8)
    def _(b):
        at = pl.ds(pl.multiple_of(b * 128, 128), 128)
        face_cols[:, at] = face_rows[at, :].T

    def ghost_copy(f, peer):
        return pltpu.make_async_remote_copy(
            src_ref=face_cols.at[:, pl.ds(f * FACE, FACE)],
            dst_ref=ext.at[rows_of(h), pl.ds(OWN + (1 - f) * FACE, FACE)],
            send_sem=gh_ss.at[f], recv_sem=gh_rs.at[f],
            device_id=(peer, h), device_id_type=MESH)

    ghosts = [ghost_copy(0, down), ghost_copy(1, up)]
    for c in ghosts:
        c.start()

    load_point.wait()

    @pl.loop(0, N_MESH)
    def _(p):
        for i in range(3):
            opsend[p, pl.ds(16 * i, 16), pl.ds(0, 64)] = point[i, p, pl.ds(0, 16), :]
            opsend[p, pl.ds(16 * i, 16), pl.ds(64, 64)] = point[i, p, pl.ds(16, 16), :]
        opsend[p, pl.ds(48, 8), :] = jnp.zeros((8, 128), jnp.float32)
        opsend[p, pl.ds(48, 1), pl.ds(0, 32)] = mat_ref[pl.ds(p, 1), :].astype(jnp.float32)

    def op_copy(slot):
        cross = slot // 16
        p = lax.rem(half + cross, 2) * 16 + lax.rem(within + slot, 16)
        target = lax.rem(h + 2 * cross * lax.rem(m, 2), 4)
        return pltpu.make_async_remote_copy(
            src_ref=opsend.at[p], dst_ref=op_in.at[m],
            send_sem=op_ss, recv_sem=op_rs,
            device_id=(p, target), device_id_type=MESH)

    @pl.loop(1, 16)
    def _(slot):
        op_copy(slot).start()
    op_keep = pltpu.make_async_copy(opsend.at[m], op_in.at[m], in_s.at[4])
    op_keep.start()

    for c in ghosts:
        c.wait_recv()

    def gfwd_copy(n, peer):
        return pltpu.make_async_remote_copy(
            src_ref=ext.at[rows_of(h), ghost_cols], dst_ref=ext.at[rows_of(h), ghost_cols],
            send_sem=fw_ss.at[n], recv_sem=fw_rs.at[n],
            device_id=(m, peer), device_id_type=MESH)

    gfar, gside = gfwd_copy(0, far), gfwd_copy(1, side)
    gfar.start()
    gside.start()

    def relay(c, cols):
        return pltpu.make_async_remote_copy(
            src_ref=ext.at[rows_of(far), cols], dst_ref=ext.at[rows_of(far), cols],
            send_sem=rel_ss.at[c], recv_sem=rel_rs.at[c],
            device_id=(m, side), device_id_type=MESH)

    relays = [relay(c, cols_of(c)) for c in range(PARTS)] + [relay(PARTS, ghost_cols)]

    low = lax.broadcasted_iota(jnp.int32, (16, 128), 1) < 64
    low1 = lax.broadcasted_iota(jnp.int32, (1, 128), 1) < 64

    load_curl.wait()

    @pl.loop(0, N_MESH, unroll=4)
    def _(s):
        at = pl.ds(pl.multiple_of(s * 128, 128), 128)
        pad = jnp.zeros((2, 128), jnp.float32)
        parts = []
        for i in range(3):
            parts += [curl[i, :, at], pad]
        curl_t[at, :] = jnp.concatenate(parts, axis=0).T

    for c in range(PARTS):
        @pl.loop(c * N_MESH // PARTS, (c + 1) * N_MESH // PARTS)
        def _(s):
            to = pl.ds(pl.multiple_of(s * 16, 16), 16)
            first = s * 128 + block_of(s, m) * 32
            c0 = curl_t[pl.ds(pl.multiple_of(first, 16), 16), :]
            c1 = curl_t[pl.ds(pl.multiple_of(first + 16, 16), 16), :]
            for i in range(3):
                for j in range(6):
                    col = i * 8 + j
                    wide[i * 6 + j, to, :] = jnp.where(low, jnp.broadcast_to(c0[:, col:col + 1], (16, 128)),
                                                       jnp.broadcast_to(c1[:, col:col + 1], (16, 128)))
        to_far[c].wait_recv()
        relays[c].start()
        if c == PARTS - 2:
            @pl.loop(16, N_MESH)
            def _(slot):
                op_copy(slot).start()
    gfar.wait_recv()
    relays[PARTS].start()

    for c in (*to_far, *to_side, *ghosts, gfar, gside):
        c.wait_send()


    for c in load_conn:
        c.wait()
    keep.wait()
    for c in range(PARTS + 1):
        if c < PARTS:
            to_side[c].wait_recv()
        else:
            gside.wait_recv()
        relays[c].wait_recv()
        blocks = CHUNK // 128 if c < PARTS else 2 * FACE // 128

        @pl.loop(0, blocks, unroll=2)
        def _(b):
            at = pl.ds(pl.multiple_of(c * CHUNK + b * 128, 128), 128)
            x = ext[:, at]
            ext2[at, :] = jnp.concatenate([x, x], axis=0).T

    @pl.loop(0, N_MESH // 2)
    def _(pair):
        for u in range(2):
            s = pair * 2 + u
            to = pl.ds(pl.multiple_of(s * 16, 16), 16)
            first = pl.multiple_of(s * 128 + block_of(s, m) * 32, 32)
            near = [conn_ref.at[pl.ds(first + j * 4096, 32)] for j in range(6)]
            for j, k in EDGE_ORDER:
                a = ext2[pl.ds(near[j][k], 1), :]
                b = ext2[pl.ds(near[j][16 + k], 1), :]
                got[u, pl.ds(j * 16 + k, 1), :] = jnp.where(low1, a, b)
            for i in range(3):
                s_i = wide[i * 6, to, :] * got[u, 0:16, :]
                for j in range(1, 6):
                    s_i = s_i + wide[i * 6 + j, to, :] * got[u, j * 16:(j + 1) * 16, :]
                flux[i, to, :] = s_i

    op_all = pltpu.make_async_remote_copy(
        src_ref=opsend.at[pl.ds(0, N_MESH - 1)], dst_ref=op_in.at[pl.ds(0, N_MESH - 1)],
        send_sem=op_ss, recv_sem=op_rs, device_id=(m, far), device_id_type=MESH)
    op_all.wait_recv()

    op_keep.wait()
    growth = [jnp.exp(jnp.float32(-0.5) * knots_ref[k].astype(jnp.float32)) for k in range(8)]

    @pl.loop(0, ROWS // 64)
    def _(r):
        to = pl.ds(pl.multiple_of(r * 64, 64), 64)
        f = transform([flux[i, to, :] for i in range(3)], inv_ref)
        b = [jnp.concatenate([op_in[r * 4 + s, 16 * i:16 * i + 16, :] for s in range(4)], axis=0)
             for i in range(3)]
        kinds = []
        for s in range(4):
            mt = jnp.broadcast_to(op_in[r * 4 + s, pl.ds(48, 1), :], (8, 128)).T
            kinds.append(jnp.where(low, jnp.broadcast_to(mt[0:16, 0:1], (16, 128)),
                                   jnp.broadcast_to(mt[16:32, 0:1], (16, 128))))
        mat = jnp.concatenate(kinds, axis=0)

        def pick(values):
            x = jnp.where(mat == 1.0, values[1], values[0])
            x = jnp.where(mat == 2.0, values[2], x)
            return jnp.where(mat == 3.0, values[3], x)

        q = b[0] * b[0] + b[1] * b[1] + b[2] * b[2]
        u = jnp.exp(2.0 * q)
        nu = pick([base_ref[a] for a in range(4)])
        dnu = jnp.zeros_like(q)
        for k in range(0, 8, 2):
            s0, s1 = [pick([slopes_ref[a, k + n] for a in range(4)]) for n in range(2)]
            e0, e1 = u * growth[k], u * growth[k + 1]
            w0, w1 = 1.0 + e0, 1.0 + e1
            nu = nu + s0 * jnp.log(w0) + s1 * jnp.log(w1)
            dnu = dnu + (s0 * e0 * w1 + s1 * e1 * w0) / (w0 * w1)
        proj = b[0] * f[0] + b[1] * f[1] + b[2] * f[2]
        scale = 4.0 * dnu * proj
        f = transform([nu * f[i] + scale * b[i] for i in range(3)], fwd_ref)
        for j in range(6):
            out_ref[r, j * 64:(j + 1) * 64, :] = (
                wide[j, to, :] * f[0] + wide[6 + j, to, :] * f[1] + wide[12 + j, to, :] * f[2])

    for c in relays:
        c.wait_send()

    op_all.wait_send()


def forward(field, point, material, curl, faces, conn, knots, base, slopes):
    inverse, forward_table = block_diag_tables()
    smem = pl.BlockSpec(memory_space=pltpu.SMEM)
    vmem = pl.BlockSpec(memory_space=pltpu.VMEM)
    hbm = pl.BlockSpec(memory_space=pltpu.HBM)
    f32 = jnp.float32
    dma = pltpu.SemaphoreType.DMA
    return pl.pallas_call(
        forward_kernel,
        name="forward",
        out_shape=jax.ShapeDtypeStruct((ROWS // 64, 384, 128), f32),
        in_specs=[hbm, hbm, vmem, hbm, hbm, hbm, smem, smem, smem, hbm, hbm],
        out_specs=vmem,
        scratch_shapes=[
            pltpu.VMEM((16, OWN), f32), pltpu.VMEM((3, 32, 32, 64), f32), pltpu.VMEM((3, 6, 4096), f32),
            pltpu.VMEM((N_MESH, MSG, 128), f32), pltpu.VMEM((N_MESH, MSG, 128), f32),
            pltpu.VMEM((OWN, 16), f32), pltpu.VMEM((2 * FACE, 16), f32), pltpu.VMEM((16, 2 * FACE), f32),
            pltpu.VMEM((64, EXT), f32), pltpu.VMEM((EXT, 128), f32), pltpu.VMEM((4096, 24), f32),
            pltpu.VMEM((18, ROWS, 128), f32), pltpu.VMEM((2, 96, 128), f32), pltpu.VMEM((3, ROWS, 128), f32),
            pltpu.VMEM((256, 256), jnp.bfloat16), pltpu.VMEM((256, 256), jnp.bfloat16),
            pltpu.SMEM((2 * FACE,), jnp.int32), pltpu.SMEM((6 * 4096,), jnp.int32),
            dma((5,)), dma, dma, dma((PARTS,)), dma((PARTS,)), dma((PARTS,)), dma((PARTS,)),
            dma((2,)), dma((2,)), dma((2,)), dma((2,)), dma((PARTS + 1,)), dma((PARTS + 1,)), dma((10,)),
        ],
        compiler_params=pltpu.CompilerParams(collective_id=0, has_side_effects=True,
                                             vmem_limit_bytes=34 << 20),
    )(field, point, material, curl, faces, conn, knots, base, slopes, pltpu.with_memory_space_constraint(jnp.asarray(inverse), pltpu.HBM),
      pltpu.with_memory_space_constraint(jnp.asarray(forward_table), pltpu.HBM))


def scatter_kernel(conn_hbm, con_ref, acc0, acc1, acc2, acc3, acc4, acc5, conn_ref, sem):
    m = lax.axis_index("mesh")
    h = lax.axis_index("harm")
    accs = (acc0, acc1, acc2, acc3, acc4, acc5)

    def block_of(source, target):
        crossing = (source // 16 + target // 16) % 2
        return lax.rem(h + 2 * crossing * lax.rem(source, 2), 4)

    loads = [pltpu.make_async_copy(conn_hbm.at[j], conn_ref.at[pl.ds(j * 4096, 4096)], sem.at[j]) for j in range(6)]
    for c in loads:
        c.start()

    @pl.loop(0, EXT // 64)
    def _(b):
        at = pl.ds(pl.multiple_of(b * 64, 64), 64)
        for a in accs:
            a[at, :] = jnp.zeros((64, 128), jnp.float32)

    for c in loads:
        c.wait()

    @pl.loop(0, N_MESH)
    def _(s):
        first = pl.multiple_of(s * 128 + block_of(s, m) * 32, 32)
        near = [conn_ref.at[pl.ds(first + j * 4096, 32)] for j in range(6)]
        rows = con_ref.at[s // 4, pl.ds(pl.multiple_of(lax.rem(s, 4) * 16, 16), 336), :]
        for j, k in EDGE_ORDER:
            row = rows[pl.ds(j * 64 + k, 1), :]
            n0 = near[j][k]
            n1 = near[j][16 + k]
            a0, a1 = accs[j % 3], accs[3 + j % 3]
            a0[pl.ds(n0, 1), :] = a0[pl.ds(n0, 1), :] + row
            a1[pl.ds(n1, 1), :] = a1[pl.ds(n1, 1), :] + row


def scatter(conn, con):
    vmem = pl.BlockSpec(memory_space=pltpu.VMEM)
    return pl.pallas_call(
        scatter_kernel,
        name="scatter",
        out_shape=(jax.ShapeDtypeStruct((EXT, 128), jnp.float32),) * 6,
        in_specs=[pl.BlockSpec(memory_space=pltpu.HBM), vmem],
        out_specs=(vmem,) * 6,
        scratch_shapes=[pltpu.SMEM((6 * 4096,), jnp.int32), pltpu.SemaphoreType.DMA((6,))],
        compiler_params=pltpu.CompilerParams(vmem_limit_bytes=28 << 20),
    )(conn, con)


def combine_kernel(acc0, acc1, acc2, acc3, acc4, acc5, own_out, ghost_out, acc, pairs, summed, zin, ghost_sum, ghost_in,
                   p_ss, p_rs, z_ss, z_rs, g_ss, g_rs):
    m = lax.axis_index("mesh")
    h = lax.axis_index("harm")
    up, down = lax.rem(m + 1, N_MESH), lax.rem(m + N_MESH - 1, N_MESH)
    side = h + 1 - 2 * lax.rem(h, 2)
    far = lax.rem(h + 2, 4)
    cross = lax.rem(side + 2, 4)
    barrier = pltpu.get_barrier_semaphore()
    for peer in ((m, side), (m, far), (up, h), (down, h)):
        pl.semaphore_signal(barrier, inc=1, device_id=peer, device_id_type=MESH)

    bounds = [(OWN, FACE), (OWN + FACE, FACE)] + [(c * CHUNK, CHUNK) for c in range(PARTS)]
    chunks = [pl.ds(a, n) for a, n in bounds]

    def block(who):
        return pl.ds(pl.multiple_of(16 * who, 16), 16)

    low = lax.broadcasted_iota(jnp.int32, (128, 128), 1) < 64

    def turn(c):
        start, n = bounds[c]

        @pl.loop(0, n // 128, unroll=2)
        def _(b):
            at = pl.ds(pl.multiple_of(start + b * 128, 128), 128)
            x = jnp.where(low, acc0[at, :] + acc1[at, :] + acc2[at, :], acc3[at, :] + acc4[at, :] + acc5[at, :]).T
            acc[:, at] = x[0:64, :] + x[64:128, :]

    def pair_copy(c, n):
        return pltpu.make_async_remote_copy(
            src_ref=acc.at[block((side, cross)[n]), chunks[c]], dst_ref=pairs.at[n, :, chunks[c]],
            send_sem=p_ss.at[c, n], recv_sem=p_rs.at[c, n],
            device_id=(m, side), device_id_type=MESH)

    def z_copy(c):
        return pltpu.make_async_remote_copy(
            src_ref=summed.at[:, chunks[c]], dst_ref=zin.at[:, chunks[c]],
            send_sem=z_ss.at[c], recv_sem=z_rs.at[c],
            device_id=(m, far), device_id_type=MESH)

    def g_copy(f, peer):
        return pltpu.make_async_remote_copy(
            src_ref=ghost_sum.at[:, pl.ds(f * FACE, FACE)],
            dst_ref=ghost_in.at[:, pl.ds((1 - f) * FACE, FACE)],
            send_sem=g_ss.at[f], recv_sem=g_rs.at[f],
            device_id=(peer, h), device_id_type=MESH)

    count = PARTS + 2
    far_pairs = [pair_copy(c, 1) for c in range(count)]
    own_pairs = [pair_copy(c, 0) for c in range(count)]
    zs = [z_copy(c) for c in range(count)]
    gs = [g_copy(0, down), g_copy(1, up)]

    turn(0)
    pl.semaphore_wait(barrier, 4)
    far_pairs[0].start()
    own_pairs[0].start()
    for c in range(count):
        if c + 1 < count:
            turn(c + 1)
            far_pairs[c + 1].start()
            own_pairs[c + 1].start()
        far_pairs[c].wait_recv()
        summed[:, chunks[c]] = acc[block(far), chunks[c]] + pairs[1, :, chunks[c]]
        zs[c].start()

    def total(c):
        own_pairs[c].wait_recv()
        zs[c].wait_recv()
        return acc[block(h), chunks[c]] + pairs[0, :, chunks[c]] + zin[:, chunks[c]]

    for f in range(2):
        ghost_sum[:, pl.ds(f * FACE, FACE)] = total(f)
        gs[f].start()
    for c in range(2, count):
        own_out[:, chunks[c]] = total(c)
    for g in gs:
        g.wait_recv()
    ghost_out[...] = ghost_in[...]
    for c in (*far_pairs, *own_pairs, *zs, *gs):
        c.wait_send()


def combine(accs):
    vmem = pl.BlockSpec(memory_space=pltpu.VMEM)
    dma = pltpu.SemaphoreType.DMA
    f32 = jnp.float32
    return pl.pallas_call(
        combine_kernel,
        name="combine",
        out_shape=(jax.ShapeDtypeStruct((16, OWN), f32), jax.ShapeDtypeStruct((16, 2 * FACE), f32)),
        in_specs=[vmem] * 6,
        out_specs=(vmem, vmem),
        scratch_shapes=[
            pltpu.VMEM((64, EXT), f32), pltpu.VMEM((2, 16, EXT), f32), pltpu.VMEM((16, EXT), f32),
            pltpu.VMEM((16, EXT), f32), pltpu.VMEM((16, 2 * FACE), f32), pltpu.VMEM((16, 2 * FACE), f32),
            dma((PARTS + 2, 2)), dma((PARTS + 2, 2)), dma((PARTS + 2,)), dma((PARTS + 2,)), dma((2,)), dma((2,)),
        ],
        compiler_params=pltpu.CompilerParams(collective_id=1, has_side_effects=True,
                                             vmem_limit_bytes=28 << 20),
    )(*accs)


def finish_kernel(faces_hbm, own_ref, ghost_ref, out_ref, ghost_t, full_t, faces_ref, idx_s):
    loads = [pltpu.make_async_copy(faces_hbm.at[f], faces_ref.at[pl.ds(f * FACE, FACE)], idx_s.at[f])
             for f in range(2)]
    for c in loads:
        c.start()

    @pl.loop(0, OWN // 128, unroll=8)
    def _(b):
        full_t[pl.ds(pl.multiple_of(b * 128, 128), 128), :] = jnp.zeros((128, 16), jnp.float32)

    @pl.loop(0, 2 * FACE // 128, unroll=8)
    def _(b):
        at = pl.ds(pl.multiple_of(b * 128, 128), 128)
        ghost_t[at, :] = ghost_ref[:, at].T

    for c in loads:
        c.wait()

    @pl.loop(0, 2 * FACE // 32)
    def _(b):
        rows = ghost_t.at[pl.ds(pl.multiple_of(b * 32, 32), 32), :]
        for g in range(4):
            near = faces_ref.at[pl.ds(pl.multiple_of(b * 32 + g * 8, 8), 8)]
            for k in range(8):
                full_t[pl.ds(near[k], 1), :] = rows[pl.ds(g * 8 + k, 1), :]

    @pl.loop(0, OWN // 128, unroll=8)
    def _(b):
        at = pl.ds(pl.multiple_of(b * 128, 128), 128)
        out_ref[:, at] = own_ref[:, at] + full_t[at, :].T


def finish(faces, own, ghost):
    vmem = pl.BlockSpec(memory_space=pltpu.VMEM)
    return pl.pallas_call(
        finish_kernel,
        name="finish",
        out_shape=jax.ShapeDtypeStruct((16, OWN), jnp.float32),
        in_specs=[pl.BlockSpec(memory_space=pl.ANY), vmem, vmem],
        out_specs=vmem,
        scratch_shapes=[pltpu.VMEM((2 * FACE, 16), jnp.float32), pltpu.VMEM((OWN, 16), jnp.float32),
                        pltpu.SMEM((2 * FACE,), jnp.int32), pltpu.SemaphoreType.DMA((2,))],
        compiler_params=pltpu.CompilerParams(vmem_limit_bytes=40 << 20),
    )(faces, own, ghost)


def per_device(field_in, faces, connectivity, curl_vectors, operating_point, material, bh_knots, curve_base,
               curve_slopes):
    point = jnp.transpose(operating_point, (1, 2, 3, 0))
    (field_in, point, material, curl_vectors, faces, connectivity, bh_knots, curve_base, curve_slopes) = [
        pltpu.with_memory_space_constraint(x, pltpu.HBM)
        for x in (field_in, point, material, curl_vectors, faces, connectivity, bh_knots, curve_base, curve_slopes)]
    contributions = forward(field_in, point, material, curl_vectors, faces, connectivity, bh_knots, curve_base,
                            curve_slopes)
    own, ghost = combine(scatter(connectivity, contributions))
    return finish(faces, own, ghost)


def solution(mesh):
    return jax.shard_map(
        per_device,
        mesh=mesh,
        in_specs=(P("harm", "mesh"), P(None, "mesh"), P(None, "mesh"), P(None, None, "mesh"),
                  P(None, None, None, ("mesh", "harm")), P(None, ("mesh", "harm")), P(), P(), P()),
        out_specs=P("harm", "mesh"),
        check_vma=False,
    )
```

```python
import functools

import numpy as np
import jax
import jax.numpy as jnp
from jax import lax
from jax.experimental import pallas as pl
from jax.experimental.pallas import tpu as pltpu
from jax.sharding import PartitionSpec as P

MESH = pl.DeviceIdType.MESH
N_MESH = 32
OWN = 5120
FACE = 1024
EXT = OWN + 2 * FACE
ROWS = 512
MSG = 56
PARTS = 4
CHUNK = OWN // PARTS
EDGE_ORDER = [(j + 3 * g, k) for g in range(2) for k in range(16) for j in range(3)]


def block_diag_tables():
    length = 64
    t = np.arange(length)
    c = np.arange(length)
    freq = np.where(c < 32, c, c - 31)
    freq[-1] = 32
    sine = (c >= 32) & (c < 63)
    angle = 2.0 * np.pi * ((freq[:, None] * t[None, :]) % length) / length
    basis = np.where(sine[:, None], np.sin(angle), np.cos(angle))
    weight = np.where((c == 0) | (c == 63), 1.0 / length, 2.0 / length)
    inverse = np.kron(np.eye(2), basis)
    forward = np.kron(np.eye(2), (basis * weight[:, None]).T)
    return split_table(inverse), split_table(forward)


def split_table(table):
    high = table.astype(jnp.bfloat16)
    rest = (table - high.astype(np.float64)).astype(jnp.bfloat16)
    return np.block([[high, rest], [high, np.zeros_like(rest)]])


def transform(parts, table_ref):
    x = jnp.concatenate(parts, axis=0)
    high = x.astype(jnp.bfloat16)
    rest = (x - high.astype(jnp.float32)).astype(jnp.bfloat16)
    y = jnp.dot(jnp.concatenate([high, rest], axis=1), table_ref[...], preferred_element_type=jnp.float32)
    y = y[:, 0:128] + y[:, 128:256]
    n = parts[0].shape[0]
    return [y[i * n:(i + 1) * n, :] for i in range(len(parts))]


def forward_kernel(field_ref, point_ref, mat_ref, curl_ref, faces_hbm, conn_hbm, knots_ref, base_ref, slopes_ref,
                   inv_hbm, fwd_hbm, out_ref,
                   field, point, curl, opsend, op_in, field_t, face_rows, face_cols, ext, ext2, curl_t, wide, got, flux, inv_ref, fwd_ref, faces_ref, conn_ref,
                   in_s, op_ss, op_rs, far_ss, far_rs, side_ss, side_rs, gh_ss, gh_rs, fw_ss, fw_rs, rel_ss, rel_rs, idx_s):
    m = lax.axis_index("mesh")
    h = lax.axis_index("harm")
    up, down = lax.rem(m + 1, N_MESH), lax.rem(m + N_MESH - 1, N_MESH)
    side = h + 1 - 2 * lax.rem(h, 2)
    far = lax.rem(h + 2, 4)
    half = m // 16

    def block_of(source, target):
        crossing = (source // 16 + target // 16) % 2
        return lax.rem(h + 2 * crossing * lax.rem(source, 2), 4)

    within = lax.rem(m, 16)
    barrier = pltpu.get_barrier_semaphore()
    crossing_h = [h, far]
    for peer in ((m, far), (m, side), (up, h), (down, h)):
        pl.semaphore_signal(barrier, inc=1, device_id=peer, device_id_type=MESH)

    @pl.loop(1, 16, unroll=3)
    def _(d):
        other = lax.rem(within + d, 16)
        pl.semaphore_signal(barrier, inc=1, device_id=(half * 16 + other, h), device_id_type=MESH)

    for odd in range(2):
        @pl.loop(0, 8, unroll=2)
        def _(d):
            pl.semaphore_signal(barrier, inc=1, device_id=((1 - half) * 16 + 2 * d + odd, crossing_h[odd]),
                                device_id_type=MESH)

    load_field = pltpu.make_async_copy(field_ref, field, in_s.at[0])
    load_point = pltpu.make_async_copy(point_ref, point, in_s.at[1])
    load_curl = pltpu.make_async_copy(curl_ref, curl, in_s.at[2])
    load_field.start()
    load_point.start()
    load_curl.start()
    load_faces = [pltpu.make_async_copy(faces_hbm.at[f], faces_ref.at[pl.ds(f * FACE, FACE)], idx_s.at[f])
                  for f in range(2)]
    load_conn = [pltpu.make_async_copy(conn_hbm.at[j], conn_ref.at[pl.ds(j * 4096, 4096)], idx_s.at[2 + j])
                 for j in range(6)]
    load_conn.append(pltpu.make_async_copy(inv_hbm, inv_ref, idx_s.at[8]))
    load_conn.append(pltpu.make_async_copy(fwd_hbm, fwd_ref, idx_s.at[9]))
    for c in (*load_faces, *load_conn):
        c.start()

    load_field.wait()

    pl.semaphore_wait(barrier, N_MESH - 1 + 4)

    def rows_of(who):
        return pl.ds(pl.multiple_of(16 * who, 16), 16)

    ghost_cols = pl.ds(OWN, 2 * FACE)

    def cols_of(c):
        return pl.ds(c * CHUNK, CHUNK)

    def own_copy(c, peer, ss, rs):
        return pltpu.make_async_remote_copy(
            src_ref=field.at[:, cols_of(c)], dst_ref=ext.at[rows_of(h), cols_of(c)],
            send_sem=ss.at[c], recv_sem=rs.at[c],
            device_id=(m, peer), device_id_type=MESH)

    to_far = [own_copy(c, far, far_ss, far_rs) for c in range(PARTS)]
    to_side = [own_copy(c, side, side_ss, side_rs) for c in range(PARTS)]
    for c in (*to_far, *to_side):
        c.start()
    keep = pltpu.make_async_copy(field, ext.at[rows_of(h), pl.ds(0, OWN)], in_s.at[3])
    keep.start()

    @pl.loop(0, OWN // 128, unroll=8)
    def _(b):
        at = pl.ds(pl.multiple_of(b * 128, 128), 128)
        field_t[at, :] = field[:, at].T

    for c in load_faces:
        c.wait()

    @pl.loop(0, 2 * FACE // 32)
    def _(b):
        near = faces_ref.at[pl.ds(pl.multiple_of(b * 32, 32), 32)]
        to = face_rows.at[pl.ds(pl.multiple_of(b * 32, 32), 32), :]
        for k in range(32):
            to[pl.ds(k, 1), :] = field_t[pl.ds(near[k], 1), :]

    @pl.loop(0, 2 * FACE // 128, unroll=8)
    def _(b):
        at = pl.ds(pl.multiple_of(b * 128, 128), 128)
        face_cols[:, at] = face_rows[at, :].T

    def ghost_copy(f, peer):
        return pltpu.make_async_remote_copy(
            src_ref=face_cols.at[:, pl.ds(f * FACE, FACE)],
            dst_ref=ext.at[rows_of(h), pl.ds(OWN + (1 - f) * FACE, FACE)],
            send_sem=gh_ss.at[f], recv_sem=gh_rs.at[f],
            device_id=(peer, h), device_id_type=MESH)

    ghosts = [ghost_copy(0, down), ghost_copy(1, up)]
    for c in ghosts:
        c.start()

    load_point.wait()

    @pl.loop(0, N_MESH)
    def _(p):
        for i in range(3):
            opsend[p, pl.ds(16 * i, 16), pl.ds(0, 64)] = point[i, p, pl.ds(0, 16), :]
            opsend[p, pl.ds(16 * i, 16), pl.ds(64, 64)] = point[i, p, pl.ds(16, 16), :]
        opsend[p, pl.ds(48, 8), :] = jnp.zeros((8, 128), jnp.float32)
        opsend[p, pl.ds(48, 1), pl.ds(0, 32)] = mat_ref[pl.ds(p, 1), :].astype(jnp.float32)

    def op_copy(slot):
        cross = slot // 16
        p = lax.rem(half + cross, 2) * 16 + lax.rem(within + slot, 16)
        target = lax.rem(h + 2 * cross * lax.rem(m, 2), 4)
        return pltpu.make_async_remote_copy(
            src_ref=opsend.at[p], dst_ref=op_in.at[m],
            send_sem=op_ss, recv_sem=op_rs,
            device_id=(p, target), device_id_type=MESH)

    @pl.loop(1, 16)
    def _(slot):
        op_copy(slot).start()
    op_keep = pltpu.make_async_copy(opsend.at[m], op_in.at[m], in_s.at[4])
    op_keep.start()

    for c in ghosts:
        c.wait_recv()

    def gfwd_copy(n, peer):
        return pltpu.make_async_remote_copy(
            src_ref=ext.at[rows_of(h), ghost_cols], dst_ref=ext.at[rows_of(h), ghost_cols],
            send_sem=fw_ss.at[n], recv_sem=fw_rs.at[n],
            device_id=(m, peer), device_id_type=MESH)

    gfar, gside = gfwd_copy(0, far), gfwd_copy(1, side)
    gfar.start()
    gside.start()

    def relay(c, cols):
        return pltpu.make_async_remote_copy(
            src_ref=ext.at[rows_of(far), cols], dst_ref=ext.at[rows_of(far), cols],
            send_sem=rel_ss.at[c], recv_sem=rel_rs.at[c],
            device_id=(m, side), device_id_type=MESH)

    relays = [relay(c, cols_of(c)) for c in range(PARTS)] + [relay(PARTS, ghost_cols)]

    low = lax.broadcasted_iota(jnp.int32, (16, 128), 1) < 64
    low1 = lax.broadcasted_iota(jnp.int32, (1, 128), 1) < 64

    load_curl.wait()

    @pl.loop(0, N_MESH, unroll=4)
    def _(s):
        at = pl.ds(pl.multiple_of(s * 128, 128), 128)
        pad = jnp.zeros((2, 128), jnp.float32)
        parts = []
        for i in range(3):
            parts += [curl[i, :, at], pad]
        curl_t[at, :] = jnp.concatenate(parts, axis=0).T

    for c in range(PARTS):
        @pl.loop(c * N_MESH // PARTS, (c + 1) * N_MESH // PARTS)
        def _(s):
            to = pl.ds(pl.multiple_of(s * 16, 16), 16)
            first = s * 128 + block_of(s, m) * 32
            c0 = curl_t[pl.ds(pl.multiple_of(first, 16), 16), :]
            c1 = curl_t[pl.ds(pl.multiple_of(first + 16, 16), 16), :]
            for i in range(3):
                for j in range(6):
                    col = i * 8 + j
                    wide[i * 6 + j, to, :] = jnp.where(low, jnp.broadcast_to(c0[:, col:col + 1], (16, 128)),
                                                       jnp.broadcast_to(c1[:, col:col + 1], (16, 128)))
        to_far[c].wait_recv()
        relays[c].start()
        if c == PARTS - 2:
            @pl.loop(16, N_MESH)
            def _(slot):
                op_copy(slot).start()
    gfar.wait_recv()
    relays[PARTS].start()

    for c in (*to_far, *to_side, *ghosts, gfar, gside):
        c.wait_send()


    for c in load_conn:
        c.wait()
    keep.wait()
    for c in range(PARTS + 1):
        if c < PARTS:
            to_side[c].wait_recv()
        else:
            gside.wait_recv()
        relays[c].wait_recv()
        blocks = CHUNK // 128 if c < PARTS else 2 * FACE // 128

        @pl.loop(0, blocks, unroll=2)
        def _(b):
            at = pl.ds(pl.multiple_of(c * CHUNK + b * 128, 128), 128)
            x = ext[:, at]
            ext2[at, :] = jnp.concatenate([x, x], axis=0).T

    @pl.loop(0, N_MESH // 2)
    def _(pair):
        for u in range(2):
            s = pair * 2 + u
            to = pl.ds(pl.multiple_of(s * 16, 16), 16)
            first = pl.multiple_of(s * 128 + block_of(s, m) * 32, 32)
            near = [conn_ref.at[pl.ds(first + j * 4096, 32)] for j in range(6)]
            for j, k in EDGE_ORDER:
                a = ext2[pl.ds(near[j][k], 1), :]
                b = ext2[pl.ds(near[j][16 + k], 1), :]
                got[u, pl.ds(j * 16 + k, 1), :] = jnp.where(low1, a, b)
            for i in range(3):
                s_i = wide[i * 6, to, :] * got[u, 0:16, :]
                for j in range(1, 6):
                    s_i = s_i + wide[i * 6 + j, to, :] * got[u, j * 16:(j + 1) * 16, :]
                flux[i, to, :] = s_i

    op_all = pltpu.make_async_remote_copy(
        src_ref=opsend.at[pl.ds(0, N_MESH - 1)], dst_ref=op_in.at[pl.ds(0, N_MESH - 1)],
        send_sem=op_ss, recv_sem=op_rs, device_id=(m, far), device_id_type=MESH)
    op_all.wait_recv()

    op_keep.wait()
    growth = [jnp.exp(jnp.float32(-0.5) * knots_ref[k].astype(jnp.float32)) for k in range(8)]

    @pl.loop(0, ROWS // 64)
    def _(r):
        to = pl.ds(pl.multiple_of(r * 64, 64), 64)
        f = transform([flux[i, to, :] for i in range(3)], inv_ref)
        b = [jnp.concatenate([op_in[r * 4 + s, 16 * i:16 * i + 16, :] for s in range(4)], axis=0)
             for i in range(3)]
        kinds = []
        for s in range(4):
            mt = jnp.broadcast_to(op_in[r * 4 + s, pl.ds(48, 1), :], (8, 128)).T
            kinds.append(jnp.where(low, jnp.broadcast_to(mt[0:16, 0:1], (16, 128)),
                                   jnp.broadcast_to(mt[16:32, 0:1], (16, 128))))
        mat = jnp.concatenate(kinds, axis=0)

        def pick(values):
            x = jnp.where(mat == 1.0, values[1], values[0])
            x = jnp.where(mat == 2.0, values[2], x)
            return jnp.where(mat == 3.0, values[3], x)

        q = b[0] * b[0] + b[1] * b[1] + b[2] * b[2]
        u = jnp.exp(2.0 * q)
        nu = pick([base_ref[a] for a in range(4)])
        dnu = jnp.zeros_like(q)
        for k in range(0, 8, 2):
            s0, s1 = [pick([slopes_ref[a, k + n] for a in range(4)]) for n in range(2)]
            e0, e1 = u * growth[k], u * growth[k + 1]
            w0, w1 = 1.0 + e0, 1.0 + e1
            nu = nu + s0 * jnp.log(w0) + s1 * jnp.log(w1)
            dnu = dnu + (s0 * e0 * w1 + s1 * e1 * w0) / (w0 * w1)
        proj = b[0] * f[0] + b[1] * f[1] + b[2] * f[2]
        scale = 4.0 * dnu * proj
        f = transform([nu * f[i] + scale * b[i] for i in range(3)], fwd_ref)
        for j in range(6):
            out_ref[r, j * 64:(j + 1) * 64, :] = (
                wide[j, to, :] * f[0] + wide[6 + j, to, :] * f[1] + wide[12 + j, to, :] * f[2])

    for c in relays:
        c.wait_send()

    op_all.wait_send()


def forward(field, point, material, curl, faces, conn, knots, base, slopes):
    inverse, forward_table = block_diag_tables()
    smem = pl.BlockSpec(memory_space=pltpu.SMEM)
    vmem = pl.BlockSpec(memory_space=pltpu.VMEM)
    hbm = pl.BlockSpec(memory_space=pltpu.HBM)
    f32 = jnp.float32
    dma = pltpu.SemaphoreType.DMA
    return pl.pallas_call(
        forward_kernel,
        name="forward",
        out_shape=jax.ShapeDtypeStruct((ROWS // 64, 384, 128), f32),
        in_specs=[hbm, hbm, vmem, hbm, hbm, hbm, smem, smem, smem, hbm, hbm],
        out_specs=vmem,
        scratch_shapes=[
            pltpu.VMEM((16, OWN), f32), pltpu.VMEM((3, 32, 32, 64), f32), pltpu.VMEM((3, 6, 4096), f32),
            pltpu.VMEM((N_MESH, MSG, 128), f32), pltpu.VMEM((N_MESH, MSG, 128), f32),
            pltpu.VMEM((OWN, 16), f32), pltpu.VMEM((2 * FACE, 16), f32), pltpu.VMEM((16, 2 * FACE), f32),
            pltpu.VMEM((64, EXT), f32), pltpu.VMEM((EXT, 128), f32), pltpu.VMEM((4096, 24), f32),
            pltpu.VMEM((18, ROWS, 128), f32), pltpu.VMEM((2, 96, 128), f32), pltpu.VMEM((3, ROWS, 128), f32),
            pltpu.VMEM((256, 256), jnp.bfloat16), pltpu.VMEM((256, 256), jnp.bfloat16),
            pltpu.SMEM((2 * FACE,), jnp.int32), pltpu.SMEM((6 * 4096,), jnp.int32),
            dma((5,)), dma, dma, dma((PARTS,)), dma((PARTS,)), dma((PARTS,)), dma((PARTS,)),
            dma((2,)), dma((2,)), dma((2,)), dma((2,)), dma((PARTS + 1,)), dma((PARTS + 1,)), dma((10,)),
        ],
        compiler_params=pltpu.CompilerParams(collective_id=0, has_side_effects=True,
                                             vmem_limit_bytes=34 << 20),
    )(field, point, material, curl, faces, conn, knots, base, slopes, pltpu.with_memory_space_constraint(jnp.asarray(inverse), pltpu.HBM),
      pltpu.with_memory_space_constraint(jnp.asarray(forward_table), pltpu.HBM))


def scatter_kernel(conn_hbm, con_ref, acc0, acc1, acc2, acc3, acc4, acc5, conn_ref, sem):
    m = lax.axis_index("mesh")
    h = lax.axis_index("harm")
    accs = (acc0, acc1, acc2, acc3, acc4, acc5)

    def block_of(source, target):
        crossing = (source // 16 + target // 16) % 2
        return lax.rem(h + 2 * crossing * lax.rem(source, 2), 4)

    loads = [pltpu.make_async_copy(conn_hbm.at[j], conn_ref.at[pl.ds(j * 4096, 4096)], sem.at[j]) for j in range(6)]
    for c in loads:
        c.start()

    @pl.loop(0, EXT // 64)
    def _(b):
        at = pl.ds(pl.multiple_of(b * 64, 64), 64)
        for a in accs:
            a[at, :] = jnp.zeros((64, 128), jnp.float32)

    for c in loads:
        c.wait()

    @pl.loop(0, N_MESH)
    def _(s):
        first = pl.multiple_of(s * 128 + block_of(s, m) * 32, 32)
        near = [conn_ref.at[pl.ds(first + j * 4096, 32)] for j in range(6)]
        rows = con_ref.at[s // 4, pl.ds(pl.multiple_of(lax.rem(s, 4) * 16, 16), 336), :]
        for j, k in EDGE_ORDER:
            row = rows[pl.ds(j * 64 + k, 1), :]
            n0 = near[j][k]
            n1 = near[j][16 + k]
            a0, a1 = accs[j % 3], accs[3 + j % 3]
            a0[pl.ds(n0, 1), :] = a0[pl.ds(n0, 1), :] + row
            a1[pl.ds(n1, 1), :] = a1[pl.ds(n1, 1), :] + row


def scatter(conn, con):
    vmem = pl.BlockSpec(memory_space=pltpu.VMEM)
    return pl.pallas_call(
        scatter_kernel,
        name="scatter",
        out_shape=(jax.ShapeDtypeStruct((EXT, 128), jnp.float32),) * 6,
        in_specs=[pl.BlockSpec(memory_space=pltpu.HBM), vmem],
        out_specs=(vmem,) * 6,
        scratch_shapes=[pltpu.SMEM((6 * 4096,), jnp.int32), pltpu.SemaphoreType.DMA((6,))],
        compiler_params=pltpu.CompilerParams(vmem_limit_bytes=28 << 20),
    )(conn, con)


def combine_kernel(acc0, acc1, acc2, acc3, acc4, acc5, faces_hbm, own_out, acc, pairs, summed, zin, ghost_sum,
                   ghost_in, faces_v, low_hot, stack, face_add, face_s,
                   p_ss, p_rs, z_ss, z_rs, g_ss, g_rs):
    m = lax.axis_index("mesh")
    h = lax.axis_index("harm")
    up, down = lax.rem(m + 1, N_MESH), lax.rem(m + N_MESH - 1, N_MESH)
    side = h + 1 - 2 * lax.rem(h, 2)
    far = lax.rem(h + 2, 4)
    cross = lax.rem(side + 2, 4)
    barrier = pltpu.get_barrier_semaphore()
    for peer in ((m, side), (m, far), (up, h), (down, h)):
        pl.semaphore_signal(barrier, inc=1, device_id=peer, device_id_type=MESH)

    load = pltpu.make_async_copy(faces_hbm, faces_v, face_s)
    load.start()

    bounds = [(OWN, FACE), (OWN + FACE, FACE)] + [(c * CHUNK, CHUNK) for c in range(PARTS)]
    chunks = [pl.ds(a, n) for a, n in bounds]

    def block(who):
        return pl.ds(pl.multiple_of(16 * who, 16), 16)

    low = lax.broadcasted_iota(jnp.int32, (128, 128), 1) < 64

    def turn(c):
        start, n = bounds[c]

        @pl.loop(0, n // 128, unroll=2)
        def _(b):
            at = pl.ds(pl.multiple_of(start + b * 128, 128), 128)
            x = jnp.where(low, acc0[at, :] + acc1[at, :] + acc2[at, :], acc3[at, :] + acc4[at, :] + acc5[at, :]).T
            acc[:, at] = x[0:64, :] + x[64:128, :]

    def pair_copy(c, n):
        return pltpu.make_async_remote_copy(
            src_ref=acc.at[block((side, cross)[n]), chunks[c]], dst_ref=pairs.at[n, :, chunks[c]],
            send_sem=p_ss.at[c, n], recv_sem=p_rs.at[c, n],
            device_id=(m, side), device_id_type=MESH)

    def z_copy(c):
        return pltpu.make_async_remote_copy(
            src_ref=summed.at[:, chunks[c]], dst_ref=zin.at[:, chunks[c]],
            send_sem=z_ss.at[c], recv_sem=z_rs.at[c],
            device_id=(m, far), device_id_type=MESH)

    def g_copy(f, peer):
        return pltpu.make_async_remote_copy(
            src_ref=ghost_sum.at[:, pl.ds(f * FACE, FACE)],
            dst_ref=ghost_in.at[:, pl.ds((1 - f) * FACE, FACE)],
            send_sem=g_ss.at[f], recv_sem=g_rs.at[f],
            device_id=(peer, h), device_id_type=MESH)

    count = PARTS + 2
    far_pairs = [pair_copy(c, 1) for c in range(count)]
    own_pairs = [pair_copy(c, 0) for c in range(count)]
    zs = [z_copy(c) for c in range(count)]
    gs = [g_copy(0, down), g_copy(1, up)]

    turn(0)
    pl.semaphore_wait(barrier, 4)
    far_pairs[0].start()
    own_pairs[0].start()
    for c in range(count):
        if c + 1 < count:
            turn(c + 1)
            far_pairs[c + 1].start()
            own_pairs[c + 1].start()
        far_pairs[c].wait_recv()
        summed[:, chunks[c]] = acc[block(far), chunks[c]] + pairs[1, :, chunks[c]]
        zs[c].start()

    load.wait()
    for f in range(2):
        @pl.loop(0, FACE // 128)
        def _(b):
            column = faces_v[pl.ds(f, 1), pl.ds(pl.multiple_of(b * 128, 128), 128)] & 127
            hot = jnp.where(lax.broadcasted_iota(jnp.int32, (128, 128), 0) == jnp.broadcast_to(column, (128, 128)),
                            1.0, 0.0)
            low_hot[pl.ds(pl.multiple_of(f * FACE + b * 128, 128), 128), :] = hot.T.astype(jnp.bfloat16)

    def total(c):
        own_pairs[c].wait_recv()
        zs[c].wait_recv()
        return acc[block(h), chunks[c]] + pairs[0, :, chunks[c]] + zin[:, chunks[c]]

    for f in range(2):
        ghost_sum[:, pl.ds(f * FACE, FACE)] = total(f)
        gs[f].start()
    for g in gs:
        g.wait_recv()

    @pl.loop(0, OWN // 1024)
    def _(g):
        for f in range(2):
            part = pl.ds(f * FACE, FACE)
            tile = jnp.broadcast_to(lax.shift_right_logical(faces_v[pl.ds(f, 1), :], 7), (16, FACE))
            x = ghost_in[:, part]
            high = x.astype(jnp.bfloat16).astype(jnp.float32)
            rest = x - high
            for u in range(8):
                here = tile == g * 8 + u
                stack[u * 32:u * 32 + 16, part] = jnp.where(here, high, 0.0).astype(jnp.bfloat16)
                stack[u * 32 + 16:u * 32 + 32, part] = jnp.where(here, rest, 0.0).astype(jnp.bfloat16)
        y = jnp.dot(stack[...], low_hot[...], preferred_element_type=jnp.float32)
        for u in range(8):
            face_add[:, pl.ds(pl.multiple_of((g * 8 + u) * 128, 128), 128)] = (
                y[u * 32:u * 32 + 16, :] + y[u * 32 + 16:u * 32 + 32, :])

    for c in range(2, count):
        own_out[:, chunks[c]] = total(c) + face_add[:, chunks[c]]
    for c in (*far_pairs, *own_pairs, *zs, *gs):
        c.wait_send()


def combine(accs, faces):
    vmem = pl.BlockSpec(memory_space=pltpu.VMEM)
    dma = pltpu.SemaphoreType.DMA
    f32 = jnp.float32
    return pl.pallas_call(
        combine_kernel,
        name="combine",
        out_shape=jax.ShapeDtypeStruct((16, OWN), f32),
        in_specs=[vmem] * 6 + [pl.BlockSpec(memory_space=pltpu.HBM)],
        out_specs=vmem,
        scratch_shapes=[
            pltpu.VMEM((64, EXT), f32), pltpu.VMEM((2, 16, EXT), f32), pltpu.VMEM((16, EXT), f32),
            pltpu.VMEM((16, EXT), f32), pltpu.VMEM((16, 2 * FACE), f32), pltpu.VMEM((16, 2 * FACE), f32),
            pltpu.VMEM((2, FACE), jnp.int32), pltpu.VMEM((2 * FACE, 128), jnp.bfloat16),
            pltpu.VMEM((256, 2 * FACE), jnp.bfloat16), pltpu.VMEM((16, OWN), f32), dma,
            dma((PARTS + 2, 2)), dma((PARTS + 2, 2)), dma((PARTS + 2,)), dma((PARTS + 2,)), dma((2,)), dma((2,)),
        ],
        compiler_params=pltpu.CompilerParams(collective_id=1, has_side_effects=True,
                                             vmem_limit_bytes=28 << 20),
    )(*accs, faces)


def per_device(field_in, faces, connectivity, curl_vectors, operating_point, material, bh_knots, curve_base,
               curve_slopes):
    point = jnp.transpose(operating_point, (1, 2, 3, 0))
    (field_in, point, material, curl_vectors, faces, connectivity, bh_knots, curve_base, curve_slopes) = [
        pltpu.with_memory_space_constraint(x, pltpu.HBM)
        for x in (field_in, point, material, curl_vectors, faces, connectivity, bh_knots, curve_base, curve_slopes)]
    contributions = forward(field_in, point, material, curl_vectors, faces, connectivity, bh_knots, curve_base,
                            curve_slopes)
    return combine(scatter(connectivity, contributions), faces)


def solution(mesh):
    return jax.shard_map(
        per_device,
        mesh=mesh,
        in_specs=(P("harm", "mesh"), P(None, "mesh"), P(None, "mesh"), P(None, None, "mesh"),
                  P(None, None, None, ("mesh", "harm")), P(None, ("mesh", "harm")), P(), P(), P()),
        out_specs=P("harm", "mesh"),
        check_vma=False,
    )
```

```python
import functools

import numpy as np
import jax
import jax.numpy as jnp
from jax import lax
from jax.experimental import pallas as pl
from jax.experimental.pallas import tpu as pltpu
from jax.sharding import PartitionSpec as P

MESH = pl.DeviceIdType.MESH
N_MESH = 32
OWN = 5120
FACE = 1024
EXT = OWN + 2 * FACE
ROWS = 512
MSG = 56
PARTS = 4
CHUNK = OWN // PARTS
EDGE_ORDER = [(j + 3 * g, k) for g in range(2) for k in range(16) for j in range(3)]


def block_diag_tables():
    length = 64
    t = np.arange(length)
    c = np.arange(length)
    freq = np.where(c < 32, c, c - 31)
    freq[-1] = 32
    sine = (c >= 32) & (c < 63)
    angle = 2.0 * np.pi * ((freq[:, None] * t[None, :]) % length) / length
    basis = np.where(sine[:, None], np.sin(angle), np.cos(angle))
    weight = np.where((c == 0) | (c == 63), 1.0 / length, 2.0 / length)
    inverse = np.kron(np.eye(2), basis)
    forward = np.kron(np.eye(2), (basis * weight[:, None]).T)
    return split_table(inverse), split_table(forward)


def split_table(table):
    high = table.astype(jnp.bfloat16)
    rest = (table - high.astype(np.float64)).astype(jnp.bfloat16)
    return np.block([[high, rest], [high, np.zeros_like(rest)]])


def transform(parts, table_ref):
    x = jnp.concatenate(parts, axis=0)
    high = x.astype(jnp.bfloat16)
    rest = (x - high.astype(jnp.float32)).astype(jnp.bfloat16)
    y = jnp.dot(jnp.concatenate([high, rest], axis=1), table_ref[...], preferred_element_type=jnp.float32)
    y = y[:, 0:128] + y[:, 128:256]
    n = parts[0].shape[0]
    return [y[i * n:(i + 1) * n, :] for i in range(len(parts))]


def forward_kernel(field_ref, point_ref, mat_ref, curl_ref, faces_hbm, conn_hbm, knots_ref, base_ref, slopes_ref,
                   inv_hbm, fwd_hbm, out_ref,
                   field, point, curl, opsend, op_in, field_t, face_rows, face_cols, ext, ext2, curl_t, wide, got, flux, inv_ref, fwd_ref, faces_ref, conn_ref,
                   in_s, op_ss, op_rs, far_ss, far_rs, side_ss, side_rs, gh_ss, gh_rs, fw_ss, fw_rs, rel_ss, rel_rs, idx_s,
                   go_near, go_all):
    m = lax.axis_index("mesh")
    h = lax.axis_index("harm")
    up, down = lax.rem(m + 1, N_MESH), lax.rem(m + N_MESH - 1, N_MESH)
    side = h + 1 - 2 * lax.rem(h, 2)
    far = lax.rem(h + 2, 4)
    half = m // 16

    def block_of(source, target):
        crossing = (source // 16 + target // 16) % 2
        return lax.rem(h + 2 * crossing * lax.rem(source, 2), 4)

    within = lax.rem(m, 16)
    barrier = pltpu.get_barrier_semaphore()
    core = lax.rem(h, 2)
    leader, desk = h - core, h - core + 1
    far_leader, far_desk = lax.rem(leader + 2, 4), lax.rem(desk + 2, 4)
    pl.semaphore_signal(barrier, inc=1, device_id=(m, far_leader), device_id_type=MESH)

    @pl.when(core == 1)
    def _():
        pl.semaphore_signal(barrier, inc=1, device_id=(m, leader), device_id_type=MESH)

    for peer in (up, down):
        pl.semaphore_signal(barrier, inc=1, device_id=(peer, desk), device_id_type=MESH)

    @pl.loop(1, 16, unroll=3)
    def _(d):
        other = lax.rem(within + d, 16)
        pl.semaphore_signal(barrier, inc=1, device_id=(half * 16 + other, desk), device_id_type=MESH)

    for odd in range(2):
        @pl.loop(0, 8, unroll=2)
        def _(d):
            pl.semaphore_signal(barrier, inc=1, device_id=((1 - half) * 16 + 2 * d + odd, (desk, far_desk)[odd]),
                                device_id_type=MESH)

    load_field = pltpu.make_async_copy(field_ref, field, in_s.at[0])
    load_point = pltpu.make_async_copy(point_ref, point, in_s.at[1])
    load_curl = pltpu.make_async_copy(curl_ref, curl, in_s.at[2])
    load_field.start()
    load_point.start()
    load_curl.start()
    load_faces = [pltpu.make_async_copy(faces_hbm.at[f], faces_ref.at[pl.ds(f * FACE, FACE)], idx_s.at[f])
                  for f in range(2)]
    load_conn = [pltpu.make_async_copy(conn_hbm.at[j], conn_ref.at[pl.ds(j * 4096, 4096)], idx_s.at[2 + j])
                 for j in range(6)]
    load_conn.append(pltpu.make_async_copy(inv_hbm, inv_ref, idx_s.at[8]))
    load_conn.append(pltpu.make_async_copy(fwd_hbm, fwd_ref, idx_s.at[9]))
    for c in (*load_faces, *load_conn):
        c.start()

    load_field.wait()

    @pl.when(core == 0)
    def _():
        pl.semaphore_wait(barrier, 3)
        pl.semaphore_signal(go_near, inc=1, device_id=(m, side), device_id_type=MESH)

    @pl.when(core == 1)
    def _():
        pl.semaphore_wait(go_near, 1)

    def rows_of(who):
        return pl.ds(pl.multiple_of(16 * who, 16), 16)

    ghost_cols = pl.ds(OWN, 2 * FACE)

    def cols_of(c):
        return pl.ds(c * CHUNK, CHUNK)

    def own_copy(c, peer, ss, rs):
        return pltpu.make_async_remote_copy(
            src_ref=field.at[:, cols_of(c)], dst_ref=ext.at[rows_of(h), cols_of(c)],
            send_sem=ss.at[c], recv_sem=rs.at[c],
            device_id=(m, peer), device_id_type=MESH)

    to_far = [own_copy(c, far, far_ss, far_rs) for c in range(PARTS)]
    to_side = [own_copy(c, side, side_ss, side_rs) for c in range(PARTS)]
    for c in (*to_far, *to_side):
        c.start()
    keep = pltpu.make_async_copy(field, ext.at[rows_of(h), pl.ds(0, OWN)], in_s.at[3])
    keep.start()

    @pl.loop(0, OWN // 128, unroll=8)
    def _(b):
        at = pl.ds(pl.multiple_of(b * 128, 128), 128)
        field_t[at, :] = field[:, at].T

    for c in load_faces:
        c.wait()

    @pl.loop(0, 2 * FACE // 32)
    def _(b):
        near = faces_ref.at[pl.ds(pl.multiple_of(b * 32, 32), 32)]
        to = face_rows.at[pl.ds(pl.multiple_of(b * 32, 32), 32), :]
        for k in range(32):
            to[pl.ds(k, 1), :] = field_t[pl.ds(near[k], 1), :]

    @pl.loop(0, 2 * FACE // 128, unroll=8)
    def _(b):
        at = pl.ds(pl.multiple_of(b * 128, 128), 128)
        face_cols[:, at] = face_rows[at, :].T

    def ghost_copy(f, peer):
        return pltpu.make_async_remote_copy(
            src_ref=face_cols.at[:, pl.ds(f * FACE, FACE)],
            dst_ref=ext.at[rows_of(h), pl.ds(OWN + (1 - f) * FACE, FACE)],
            send_sem=gh_ss.at[f], recv_sem=gh_rs.at[f],
            device_id=(peer, h), device_id_type=MESH)

    @pl.when(core == 1)
    def _():
        pl.semaphore_wait(barrier, 2 * (N_MESH - 1 + 2))
        pl.semaphore_signal(go_all, inc=1, device_id=(m, side), device_id_type=MESH)

    @pl.when(core == 0)
    def _():
        pl.semaphore_wait(go_all, 1)

    ghosts = [ghost_copy(0, down), ghost_copy(1, up)]
    for c in ghosts:
        c.start()

    load_point.wait()

    @pl.loop(0, N_MESH)
    def _(p):
        for i in range(3):
            opsend[p, pl.ds(16 * i, 16), pl.ds(0, 64)] = point[i, p, pl.ds(0, 16), :]
            opsend[p, pl.ds(16 * i, 16), pl.ds(64, 64)] = point[i, p, pl.ds(16, 16), :]
        opsend[p, pl.ds(48, 8), :] = jnp.zeros((8, 128), jnp.float32)
        opsend[p, pl.ds(48, 1), pl.ds(0, 32)] = mat_ref[pl.ds(p, 1), :].astype(jnp.float32)

    def op_copy(slot):
        cross = slot // 16
        p = lax.rem(half + cross, 2) * 16 + lax.rem(within + slot, 16)
        target = lax.rem(h + 2 * cross * lax.rem(m, 2), 4)
        return pltpu.make_async_remote_copy(
            src_ref=opsend.at[p], dst_ref=op_in.at[m],
            send_sem=op_ss, recv_sem=op_rs,
            device_id=(p, target), device_id_type=MESH)

    @pl.loop(1, 16)
    def _(slot):
        op_copy(slot).start()
    op_keep = pltpu.make_async_copy(opsend.at[m], op_in.at[m], in_s.at[4])
    op_keep.start()

    for c in ghosts:
        c.wait_recv()

    def gfwd_copy(n, peer):
        return pltpu.make_async_remote_copy(
            src_ref=ext.at[rows_of(h), ghost_cols], dst_ref=ext.at[rows_of(h), ghost_cols],
            send_sem=fw_ss.at[n], recv_sem=fw_rs.at[n],
            device_id=(m, peer), device_id_type=MESH)

    gfar, gside = gfwd_copy(0, far), gfwd_copy(1, side)
    gfar.start()
    gside.start()

    def relay(c, cols):
        return pltpu.make_async_remote_copy(
            src_ref=ext.at[rows_of(far), cols], dst_ref=ext.at[rows_of(far), cols],
            send_sem=rel_ss.at[c], recv_sem=rel_rs.at[c],
            device_id=(m, side), device_id_type=MESH)

    relays = [relay(c, cols_of(c)) for c in range(PARTS)] + [relay(PARTS, ghost_cols)]

    low = lax.broadcasted_iota(jnp.int32, (16, 128), 1) < 64
    low1 = lax.broadcasted_iota(jnp.int32, (1, 128), 1) < 64

    load_curl.wait()

    @pl.loop(0, N_MESH, unroll=4)
    def _(s):
        at = pl.ds(pl.multiple_of(s * 128, 128), 128)
        pad = jnp.zeros((2, 128), jnp.float32)
        parts = []
        for i in range(3):
            parts += [curl[i, :, at], pad]
        curl_t[at, :] = jnp.concatenate(parts, axis=0).T

    for c in range(PARTS):
        @pl.loop(c * N_MESH // PARTS, (c + 1) * N_MESH // PARTS)
        def _(s):
            to = pl.ds(pl.multiple_of(s * 16, 16), 16)
            first = s * 128 + block_of(s, m) * 32
            c0 = curl_t[pl.ds(pl.multiple_of(first, 16), 16), :]
            c1 = curl_t[pl.ds(pl.multiple_of(first + 16, 16), 16), :]
            for i in range(3):
                for j in range(6):
                    col = i * 8 + j
                    wide[i * 6 + j, to, :] = jnp.where(low, jnp.broadcast_to(c0[:, col:col + 1], (16, 128)),
                                                       jnp.broadcast_to(c1[:, col:col + 1], (16, 128)))
        to_far[c].wait_recv()
        relays[c].start()
        if c == PARTS - 2:
            @pl.loop(16, N_MESH)
            def _(slot):
                op_copy(slot).start()
    gfar.wait_recv()
    relays[PARTS].start()

    for c in (*to_far, *to_side, *ghosts, gfar, gside):
        c.wait_send()


    for c in load_conn:
        c.wait()
    keep.wait()
    for c in range(PARTS + 1):
        if c < PARTS:
            to_side[c].wait_recv()
        else:
            gside.wait_recv()
        relays[c].wait_recv()
        blocks = CHUNK // 128 if c < PARTS else 2 * FACE // 128

        @pl.loop(0, blocks, unroll=2)
        def _(b):
            at = pl.ds(pl.multiple_of(c * CHUNK + b * 128, 128), 128)
            x = ext[:, at]
            ext2[at, :] = jnp.concatenate([x, x], axis=0).T

    @pl.loop(0, N_MESH // 2)
    def _(pair):
        for u in range(2):
            s = pair * 2 + u
            to = pl.ds(pl.multiple_of(s * 16, 16), 16)
            first = pl.multiple_of(s * 128 + block_of(s, m) * 32, 32)
            near = [conn_ref.at[pl.ds(first + j * 4096, 32)] for j in range(6)]
            for j, k in EDGE_ORDER:
                a = ext2[pl.ds(near[j][k], 1), :]
                b = ext2[pl.ds(near[j][16 + k], 1), :]
                got[u, pl.ds(j * 16 + k, 1), :] = jnp.where(low1, a, b)
            for i in range(3):
                s_i = wide[i * 6, to, :] * got[u, 0:16, :]
                for j in range(1, 6):
                    s_i = s_i + wide[i * 6 + j, to, :] * got[u, j * 16:(j + 1) * 16, :]
                flux[i, to, :] = s_i

    op_all = pltpu.make_async_remote_copy(
        src_ref=opsend.at[pl.ds(0, N_MESH - 1)], dst_ref=op_in.at[pl.ds(0, N_MESH - 1)],
        send_sem=op_ss, recv_sem=op_rs, device_id=(m, far), device_id_type=MESH)
    op_all.wait_recv()

    op_keep.wait()
    growth = [jnp.exp(jnp.float32(-0.5) * knots_ref[k].astype(jnp.float32)) for k in range(8)]

    @pl.loop(0, ROWS // 64)
    def _(r):
        to = pl.ds(pl.multiple_of(r * 64, 64), 64)
        f = transform([flux[i, to, :] for i in range(3)], inv_ref)
        b = [jnp.concatenate([op_in[r * 4 + s, 16 * i:16 * i + 16, :] for s in range(4)], axis=0)
             for i in range(3)]
        kinds = []
        for s in range(4):
            mt = jnp.broadcast_to(op_in[r * 4 + s, pl.ds(48, 1), :], (8, 128)).T
            kinds.append(jnp.where(low, jnp.broadcast_to(mt[0:16, 0:1], (16, 128)),
                                   jnp.broadcast_to(mt[16:32, 0:1], (16, 128))))
        mat = jnp.concatenate(kinds, axis=0)

        def pick(values):
            x = jnp.where(mat == 1.0, values[1], values[0])
            x = jnp.where(mat == 2.0, values[2], x)
            return jnp.where(mat == 3.0, values[3], x)

        q = b[0] * b[0] + b[1] * b[1] + b[2] * b[2]
        u = jnp.exp(2.0 * q)
        nu = pick([base_ref[a] for a in range(4)])
        dnu = jnp.zeros_like(q)
        for k in range(0, 8, 2):
            s0, s1 = [pick([slopes_ref[a, k + n] for a in range(4)]) for n in range(2)]
            e0, e1 = u * growth[k], u * growth[k + 1]
            w0, w1 = 1.0 + e0, 1.0 + e1
            nu = nu + s0 * jnp.log(w0) + s1 * jnp.log(w1)
            dnu = dnu + (s0 * e0 * w1 + s1 * e1 * w0) / (w0 * w1)
        proj = b[0] * f[0] + b[1] * f[1] + b[2] * f[2]
        scale = 4.0 * dnu * proj
        f = transform([nu * f[i] + scale * b[i] for i in range(3)], fwd_ref)
        for j in range(6):
            out_ref[r, j * 64:(j + 1) * 64, :] = (
                wide[j, to, :] * f[0] + wide[6 + j, to, :] * f[1] + wide[12 + j, to, :] * f[2])

    for c in relays:
        c.wait_send()

    op_all.wait_send()


def forward(field, point, material, curl, faces, conn, knots, base, slopes):
    inverse, forward_table = block_diag_tables()
    smem = pl.BlockSpec(memory_space=pltpu.SMEM)
    vmem = pl.BlockSpec(memory_space=pltpu.VMEM)
    hbm = pl.BlockSpec(memory_space=pltpu.HBM)
    f32 = jnp.float32
    dma = pltpu.SemaphoreType.DMA
    return pl.pallas_call(
        forward_kernel,
        name="forward",
        out_shape=jax.ShapeDtypeStruct((ROWS // 64, 384, 128), f32),
        in_specs=[hbm, hbm, vmem, hbm, hbm, hbm, smem, smem, smem, hbm, hbm],
        out_specs=vmem,
        scratch_shapes=[
            pltpu.VMEM((16, OWN), f32), pltpu.VMEM((3, 32, 32, 64), f32), pltpu.VMEM((3, 6, 4096), f32),
            pltpu.VMEM((N_MESH, MSG, 128), f32), pltpu.VMEM((N_MESH, MSG, 128), f32),
            pltpu.VMEM((OWN, 16), f32), pltpu.VMEM((2 * FACE, 16), f32), pltpu.VMEM((16, 2 * FACE), f32),
            pltpu.VMEM((64, EXT), f32), pltpu.VMEM((EXT, 128), f32), pltpu.VMEM((4096, 24), f32),
            pltpu.VMEM((18, ROWS, 128), f32), pltpu.VMEM((2, 96, 128), f32), pltpu.VMEM((3, ROWS, 128), f32),
            pltpu.VMEM((256, 256), jnp.bfloat16), pltpu.VMEM((256, 256), jnp.bfloat16),
            pltpu.SMEM((2 * FACE,), jnp.int32), pltpu.SMEM((6 * 4096,), jnp.int32),
            dma((5,)), dma, dma, dma((PARTS,)), dma((PARTS,)), dma((PARTS,)), dma((PARTS,)),
            dma((2,)), dma((2,)), dma((2,)), dma((2,)), dma((PARTS + 1,)), dma((PARTS + 1,)), dma((10,)),
            pltpu.SemaphoreType.REGULAR, pltpu.SemaphoreType.REGULAR,
        ],
        compiler_params=pltpu.CompilerParams(collective_id=0, has_side_effects=True,
                                             vmem_limit_bytes=34 << 20),
    )(field, point, material, curl, faces, conn, knots, base, slopes, pltpu.with_memory_space_constraint(jnp.asarray(inverse), pltpu.HBM),
      pltpu.with_memory_space_constraint(jnp.asarray(forward_table), pltpu.HBM))


def scatter_kernel(conn_hbm, con_ref, acc0, acc1, acc2, acc3, acc4, acc5, conn_ref, sem):
    m = lax.axis_index("mesh")
    h = lax.axis_index("harm")
    accs = (acc0, acc1, acc2, acc3, acc4, acc5)

    def block_of(source, target):
        crossing = (source // 16 + target // 16) % 2
        return lax.rem(h + 2 * crossing * lax.rem(source, 2), 4)

    loads = [pltpu.make_async_copy(conn_hbm.at[j], conn_ref.at[pl.ds(j * 4096, 4096)], sem.at[j]) for j in range(6)]
    for c in loads:
        c.start()

    @pl.loop(0, EXT // 64)
    def _(b):
        at = pl.ds(pl.multiple_of(b * 64, 64), 64)
        for a in accs:
            a[at, :] = jnp.zeros((64, 128), jnp.float32)

    for c in loads:
        c.wait()

    @pl.loop(0, N_MESH)
    def _(s):
        first = pl.multiple_of(s * 128 + block_of(s, m) * 32, 32)
        near = [conn_ref.at[pl.ds(first + j * 4096, 32)] for j in range(6)]
        rows = con_ref.at[s // 4, pl.ds(pl.multiple_of(lax.rem(s, 4) * 16, 16), 336), :]
        for j, k in EDGE_ORDER:
            row = rows[pl.ds(j * 64 + k, 1), :]
            n0 = near[j][k]
            n1 = near[j][16 + k]
            a0, a1 = accs[j % 3], accs[3 + j % 3]
            a0[pl.ds(n0, 1), :] = a0[pl.ds(n0, 1), :] + row
            a1[pl.ds(n1, 1), :] = a1[pl.ds(n1, 1), :] + row


def scatter(conn, con):
    vmem = pl.BlockSpec(memory_space=pltpu.VMEM)
    return pl.pallas_call(
        scatter_kernel,
        name="scatter",
        out_shape=(jax.ShapeDtypeStruct((EXT, 128), jnp.float32),) * 6,
        in_specs=[pl.BlockSpec(memory_space=pltpu.HBM), vmem],
        out_specs=(vmem,) * 6,
        scratch_shapes=[pltpu.SMEM((6 * 4096,), jnp.int32), pltpu.SemaphoreType.DMA((6,))],
        compiler_params=pltpu.CompilerParams(vmem_limit_bytes=28 << 20),
    )(conn, con)


def combine_kernel(acc0, acc1, acc2, acc3, acc4, acc5, faces_hbm, own_out, acc, pairs, summed, zin, ghost_sum,
                   ghost_in, faces_v, low_hot, stack, face_add, face_s,
                   p_ss, p_rs, z_ss, z_rs, g_ss, g_rs):
    m = lax.axis_index("mesh")
    h = lax.axis_index("harm")
    up, down = lax.rem(m + 1, N_MESH), lax.rem(m + N_MESH - 1, N_MESH)
    side = h + 1 - 2 * lax.rem(h, 2)
    far = lax.rem(h + 2, 4)
    cross = lax.rem(side + 2, 4)
    barrier = pltpu.get_barrier_semaphore()
    for peer in ((m, side), (m, far), (up, h), (down, h)):
        pl.semaphore_signal(barrier, inc=1, device_id=peer, device_id_type=MESH)

    load = pltpu.make_async_copy(faces_hbm, faces_v, face_s)
    load.start()

    bounds = [(OWN, FACE), (OWN + FACE, FACE)] + [(c * CHUNK, CHUNK) for c in range(PARTS)]
    chunks = [pl.ds(a, n) for a, n in bounds]

    def block(who):
        return pl.ds(pl.multiple_of(16 * who, 16), 16)

    low = lax.broadcasted_iota(jnp.int32, (128, 128), 1) < 64

    def turn(c):
        start, n = bounds[c]

        @pl.loop(0, n // 128, unroll=2)
        def _(b):
            at = pl.ds(pl.multiple_of(start + b * 128, 128), 128)
            x = jnp.where(low, acc0[at, :] + acc1[at, :] + acc2[at, :], acc3[at, :] + acc4[at, :] + acc5[at, :]).T
            acc[:, at] = x[0:64, :] + x[64:128, :]

    def pair_copy(c, n):
        return pltpu.make_async_remote_copy(
            src_ref=acc.at[block((side, cross)[n]), chunks[c]], dst_ref=pairs.at[n, :, chunks[c]],
            send_sem=p_ss.at[c, n], recv_sem=p_rs.at[c, n],
            device_id=(m, side), device_id_type=MESH)

    def z_copy(c):
        return pltpu.make_async_remote_copy(
            src_ref=summed.at[:, chunks[c]], dst_ref=zin.at[:, chunks[c]],
            send_sem=z_ss.at[c], recv_sem=z_rs.at[c],
            device_id=(m, far), device_id_type=MESH)

    def g_copy(f, peer):
        return pltpu.make_async_remote_copy(
            src_ref=ghost_sum.at[:, pl.ds(f * FACE, FACE)],
            dst_ref=ghost_in.at[:, pl.ds((1 - f) * FACE, FACE)],
            send_sem=g_ss.at[f], recv_sem=g_rs.at[f],
            device_id=(peer, h), device_id_type=MESH)

    count = PARTS + 2
    far_pairs = [pair_copy(c, 1) for c in range(count)]
    own_pairs = [pair_copy(c, 0) for c in range(count)]
    zs = [z_copy(c) for c in range(count)]
    gs = [g_copy(0, down), g_copy(1, up)]

    turn(0)
    pl.semaphore_wait(barrier, 4)
    far_pairs[0].start()
    own_pairs[0].start()
    for c in range(count):
        if c + 1 < count:
            turn(c + 1)
            far_pairs[c + 1].start()
            own_pairs[c + 1].start()
        far_pairs[c].wait_recv()
        summed[:, chunks[c]] = acc[block(far), chunks[c]] + pairs[1, :, chunks[c]]
        zs[c].start()

    load.wait()
    for f in range(2):
        @pl.loop(0, FACE // 128)
        def _(b):
            column = faces_v[pl.ds(f, 1), pl.ds(pl.multiple_of(b * 128, 128), 128)] & 127
            hot = jnp.where(lax.broadcasted_iota(jnp.int32, (128, 128), 0) == jnp.broadcast_to(column, (128, 128)),
                            1.0, 0.0)
            low_hot[pl.ds(pl.multiple_of(f * FACE + b * 128, 128), 128), :] = hot.T.astype(jnp.bfloat16)

    def total(c):
        own_pairs[c].wait_recv()
        zs[c].wait_recv()
        return acc[block(h), chunks[c]] + pairs[0, :, chunks[c]] + zin[:, chunks[c]]

    for f in range(2):
        ghost_sum[:, pl.ds(f * FACE, FACE)] = total(f)
        gs[f].start()
    for g in gs:
        g.wait_recv()

    @pl.loop(0, OWN // 1024)
    def _(g):
        for f in range(2):
            part = pl.ds(f * FACE, FACE)
            tile = jnp.broadcast_to(lax.shift_right_logical(faces_v[pl.ds(f, 1), :], 7), (16, FACE))
            x = ghost_in[:, part]
            high = x.astype(jnp.bfloat16).astype(jnp.float32)
            rest = x - high
            for u in range(8):
                here = tile == g * 8 + u
                stack[u * 32:u * 32 + 16, part] = jnp.where(here, high, 0.0).astype(jnp.bfloat16)
                stack[u * 32 + 16:u * 32 + 32, part] = jnp.where(here, rest, 0.0).astype(jnp.bfloat16)
        y = jnp.dot(stack[...], low_hot[...], preferred_element_type=jnp.float32)
        for u in range(8):
            face_add[:, pl.ds(pl.multiple_of((g * 8 + u) * 128, 128), 128)] = (
                y[u * 32:u * 32 + 16, :] + y[u * 32 + 16:u * 32 + 32, :])

    for c in range(2, count):
        own_out[:, chunks[c]] = total(c) + face_add[:, chunks[c]]
    for c in (*far_pairs, *own_pairs, *zs, *gs):
        c.wait_send()


def combine(accs, faces):
    vmem = pl.BlockSpec(memory_space=pltpu.VMEM)
    dma = pltpu.SemaphoreType.DMA
    f32 = jnp.float32
    return pl.pallas_call(
        combine_kernel,
        name="combine",
        out_shape=jax.ShapeDtypeStruct((16, OWN), f32),
        in_specs=[vmem] * 6 + [pl.BlockSpec(memory_space=pltpu.HBM)],
        out_specs=vmem,
        scratch_shapes=[
            pltpu.VMEM((64, EXT), f32), pltpu.VMEM((2, 16, EXT), f32), pltpu.VMEM((16, EXT), f32),
            pltpu.VMEM((16, EXT), f32), pltpu.VMEM((16, 2 * FACE), f32), pltpu.VMEM((16, 2 * FACE), f32),
            pltpu.VMEM((2, FACE), jnp.int32), pltpu.VMEM((2 * FACE, 128), jnp.bfloat16),
            pltpu.VMEM((256, 2 * FACE), jnp.bfloat16), pltpu.VMEM((16, OWN), f32), dma,
            dma((PARTS + 2, 2)), dma((PARTS + 2, 2)), dma((PARTS + 2,)), dma((PARTS + 2,)), dma((2,)), dma((2,)),
        ],
        compiler_params=pltpu.CompilerParams(collective_id=1, has_side_effects=True,
                                             vmem_limit_bytes=28 << 20),
    )(*accs, faces)


def per_device(field_in, faces, connectivity, curl_vectors, operating_point, material, bh_knots, curve_base,
               curve_slopes):
    point = jnp.transpose(operating_point, (1, 2, 3, 0))
    (field_in, point, material, curl_vectors, faces, connectivity, bh_knots, curve_base, curve_slopes) = [
        pltpu.with_memory_space_constraint(x, pltpu.HBM)
        for x in (field_in, point, material, curl_vectors, faces, connectivity, bh_knots, curve_base, curve_slopes)]
    contributions = forward(field_in, point, material, curl_vectors, faces, connectivity, bh_knots, curve_base,
                            curve_slopes)
    return combine(scatter(connectivity, contributions), faces)


def solution(mesh):
    return jax.shard_map(
        per_device,
        mesh=mesh,
        in_specs=(P("harm", "mesh"), P(None, "mesh"), P(None, "mesh"), P(None, None, "mesh"),
                  P(None, None, None, ("mesh", "harm")), P(None, ("mesh", "harm")), P(), P(), P()),
        out_specs=P("harm", "mesh"),
        check_vma=False,
    )
```

```python
import functools

import numpy as np
import jax
import jax.numpy as jnp
from jax import lax
from jax.experimental import pallas as pl
from jax.experimental.pallas import tpu as pltpu
from jax.sharding import PartitionSpec as P

MESH = pl.DeviceIdType.MESH
N_MESH = 32
OWN = 5120
FACE = 1024
EXT = OWN + 2 * FACE
ROWS = 512
MSG = 56
PARTS = 4
CHUNK = OWN // PARTS
EDGE_ORDER = [(j + 3 * g, k) for g in range(2) for k in range(16) for j in range(3)]


def block_diag_tables():
    length = 64
    t = np.arange(length)
    c = np.arange(length)
    freq = np.where(c < 32, c, c - 31)
    freq[-1] = 32
    sine = (c >= 32) & (c < 63)
    angle = 2.0 * np.pi * ((freq[:, None] * t[None, :]) % length) / length
    basis = np.where(sine[:, None], np.sin(angle), np.cos(angle))
    weight = np.where((c == 0) | (c == 63), 1.0 / length, 2.0 / length)
    inverse = np.kron(np.eye(2), basis)
    forward = np.kron(np.eye(2), (basis * weight[:, None]).T)
    return split_table(inverse), split_table(forward)


def split_table(table):
    high = table.astype(jnp.bfloat16)
    rest = (table - high.astype(np.float64)).astype(jnp.bfloat16)
    return np.block([[high, rest], [high, np.zeros_like(rest)]])


def transform(parts, table_ref):
    x = jnp.concatenate(parts, axis=0)
    high = x.astype(jnp.bfloat16)
    rest = (x - high.astype(jnp.float32)).astype(jnp.bfloat16)
    y = jnp.dot(jnp.concatenate([high, rest], axis=1), table_ref[...], preferred_element_type=jnp.float32)
    y = y[:, 0:128] + y[:, 128:256]
    n = parts[0].shape[0]
    return [y[i * n:(i + 1) * n, :] for i in range(len(parts))]


def forward_kernel(field_ref, point_ref, mat_ref, curl_ref, faces_hbm, conn_hbm, knots_ref, base_ref, slopes_ref,
                   inv_hbm, fwd_hbm, out_ref,
                   field, point, curl, opsend, op_in, field_t, face_rows, face_cols, ext, ext2, curl_t, wide, got, flux, inv_ref, fwd_ref, faces_ref, conn_ref,
                   in_s, op_ss, op_rs, far_ss, far_rs, side_ss, side_rs, gh_ss, gh_rs, fw_ss, fw_rs, rel_ss, rel_rs, idx_s,
                   go_near, go_all):
    m = lax.axis_index("mesh")
    h = lax.axis_index("harm")
    up, down = lax.rem(m + 1, N_MESH), lax.rem(m + N_MESH - 1, N_MESH)
    side = h + 1 - 2 * lax.rem(h, 2)
    far = lax.rem(h + 2, 4)
    half = m // 16

    def block_of(source, target):
        crossing = (source // 16 + target // 16) % 2
        return lax.rem(h + 2 * crossing * lax.rem(source, 2), 4)

    within = lax.rem(m, 16)
    barrier = pltpu.get_barrier_semaphore()
    core = lax.rem(h, 2)
    leader, desk = h - core, h - core + 1
    far_leader, far_desk = lax.rem(leader + 2, 4), lax.rem(desk + 2, 4)
    pl.semaphore_signal(barrier, inc=1, device_id=(m, far_leader), device_id_type=MESH)

    @pl.when(core == 1)
    def _():
        pl.semaphore_signal(barrier, inc=1, device_id=(m, leader), device_id_type=MESH)

    for peer in (up, down):
        pl.semaphore_signal(barrier, inc=1, device_id=(peer, desk), device_id_type=MESH)

    @pl.loop(1, 16, unroll=3)
    def _(d):
        other = lax.rem(within + d, 16)
        pl.semaphore_signal(barrier, inc=1, device_id=(half * 16 + other, desk), device_id_type=MESH)

    for odd in range(2):
        @pl.loop(0, 8, unroll=2)
        def _(d):
            pl.semaphore_signal(barrier, inc=1, device_id=((1 - half) * 16 + 2 * d + odd, (desk, far_desk)[odd]),
                                device_id_type=MESH)

    load_field = pltpu.make_async_copy(field_ref, field, in_s.at[0])
    load_point = pltpu.make_async_copy(point_ref, point, in_s.at[1])
    load_curl = pltpu.make_async_copy(curl_ref, curl, in_s.at[2])
    load_field.start()
    load_point.start()
    load_curl.start()
    load_faces = [pltpu.make_async_copy(faces_hbm.at[f], faces_ref.at[pl.ds(f * FACE, FACE)], idx_s.at[f])
                  for f in range(2)]
    load_conn = [pltpu.make_async_copy(conn_hbm.at[j], conn_ref.at[pl.ds(j * 4096, 4096)], idx_s.at[2 + j])
                 for j in range(6)]
    load_conn.append(pltpu.make_async_copy(inv_hbm, inv_ref, idx_s.at[8]))
    load_conn.append(pltpu.make_async_copy(fwd_hbm, fwd_ref, idx_s.at[9]))
    for c in (*load_faces, *load_conn):
        c.start()

    load_field.wait()

    @pl.when(core == 0)
    def _():
        pl.semaphore_wait(barrier, 3)
        pl.semaphore_signal(go_near, inc=1, device_id=(m, side), device_id_type=MESH)

    @pl.when(core == 1)
    def _():
        pl.semaphore_wait(go_near, 1)

    def rows_of(who):
        return pl.ds(pl.multiple_of(16 * who, 16), 16)

    ghost_cols = pl.ds(OWN, 2 * FACE)

    def cols_of(c):
        return pl.ds(c * CHUNK, CHUNK)

    def own_copy(c, peer, ss, rs):
        return pltpu.make_async_remote_copy(
            src_ref=field.at[:, cols_of(c)], dst_ref=ext.at[rows_of(h), cols_of(c)],
            send_sem=ss.at[c], recv_sem=rs.at[c],
            device_id=(m, peer), device_id_type=MESH)

    to_far = [own_copy(c, far, far_ss, far_rs) for c in range(PARTS)]
    to_side = [own_copy(c, side, side_ss, side_rs) for c in range(PARTS)]
    for c in (*to_far, *to_side):
        c.start()
    keep = pltpu.make_async_copy(field, ext.at[rows_of(h), pl.ds(0, OWN)], in_s.at[3])
    keep.start()

    @pl.loop(0, OWN // 128, unroll=8)
    def _(b):
        at = pl.ds(pl.multiple_of(b * 128, 128), 128)
        field_t[at, :] = field[:, at].T

    for c in load_faces:
        c.wait()

    @pl.loop(0, 2 * FACE // 32)
    def _(b):
        near = faces_ref.at[pl.ds(pl.multiple_of(b * 32, 32), 32)]
        to = face_rows.at[pl.ds(pl.multiple_of(b * 32, 32), 32), :]
        for k in range(32):
            to[pl.ds(k, 1), :] = field_t[pl.ds(near[k], 1), :]

    @pl.loop(0, 2 * FACE // 128, unroll=8)
    def _(b):
        at = pl.ds(pl.multiple_of(b * 128, 128), 128)
        face_cols[:, at] = face_rows[at, :].T

    def ghost_copy(f, peer):
        return pltpu.make_async_remote_copy(
            src_ref=face_cols.at[:, pl.ds(f * FACE, FACE)],
            dst_ref=ext.at[rows_of(h), pl.ds(OWN + (1 - f) * FACE, FACE)],
            send_sem=gh_ss.at[f], recv_sem=gh_rs.at[f],
            device_id=(peer, h), device_id_type=MESH)

    @pl.when(core == 1)
    def _():
        pl.semaphore_wait(barrier, 2 * (N_MESH - 1 + 2))
        pl.semaphore_signal(go_all, inc=1, device_id=(m, side), device_id_type=MESH)

    @pl.when(core == 0)
    def _():
        pl.semaphore_wait(go_all, 1)

    ghosts = [ghost_copy(0, down), ghost_copy(1, up)]
    for c in ghosts:
        c.start()

    load_point.wait()

    @pl.loop(0, N_MESH)
    def _(p):
        for i in range(3):
            opsend[p, pl.ds(16 * i, 16), pl.ds(0, 64)] = point[i, p, pl.ds(0, 16), :]
            opsend[p, pl.ds(16 * i, 16), pl.ds(64, 64)] = point[i, p, pl.ds(16, 16), :]
        opsend[p, pl.ds(48, 8), :] = jnp.zeros((8, 128), jnp.float32)
        opsend[p, pl.ds(48, 1), pl.ds(0, 32)] = mat_ref[pl.ds(p, 1), :].astype(jnp.float32)

    def op_copy(slot):
        cross = slot // 16
        p = lax.rem(half + cross, 2) * 16 + lax.rem(within + slot, 16)
        target = lax.rem(h + 2 * cross * lax.rem(m, 2), 4)
        return pltpu.make_async_remote_copy(
            src_ref=opsend.at[p], dst_ref=op_in.at[m],
            send_sem=op_ss, recv_sem=op_rs,
            device_id=(p, target), device_id_type=MESH)

    op_keep = pltpu.make_async_copy(opsend.at[m], op_in.at[m], in_s.at[4])
    op_keep.start()

    for c in ghosts:
        c.wait_recv()

    def gfwd_copy(n, peer):
        return pltpu.make_async_remote_copy(
            src_ref=ext.at[rows_of(h), ghost_cols], dst_ref=ext.at[rows_of(h), ghost_cols],
            send_sem=fw_ss.at[n], recv_sem=fw_rs.at[n],
            device_id=(m, peer), device_id_type=MESH)

    gfar, gside = gfwd_copy(0, far), gfwd_copy(1, side)
    gfar.start()
    gside.start()

    @pl.loop(1, 16)
    def _(slot):
        op_copy(slot).start()


    def relay(c, cols):
        return pltpu.make_async_remote_copy(
            src_ref=ext.at[rows_of(far), cols], dst_ref=ext.at[rows_of(far), cols],
            send_sem=rel_ss.at[c], recv_sem=rel_rs.at[c],
            device_id=(m, side), device_id_type=MESH)

    relays = [relay(c, cols_of(c)) for c in range(PARTS)] + [relay(PARTS, ghost_cols)]

    low = lax.broadcasted_iota(jnp.int32, (16, 128), 1) < 64
    low1 = lax.broadcasted_iota(jnp.int32, (1, 128), 1) < 64

    load_curl.wait()

    @pl.loop(0, N_MESH, unroll=4)
    def _(s):
        at = pl.ds(pl.multiple_of(s * 128, 128), 128)
        pad = jnp.zeros((2, 128), jnp.float32)
        parts = []
        for i in range(3):
            parts += [curl[i, :, at], pad]
        curl_t[at, :] = jnp.concatenate(parts, axis=0).T

    for c in range(PARTS):
        @pl.loop(c * N_MESH // PARTS, (c + 1) * N_MESH // PARTS)
        def _(s):
            to = pl.ds(pl.multiple_of(s * 16, 16), 16)
            first = s * 128 + block_of(s, m) * 32
            c0 = curl_t[pl.ds(pl.multiple_of(first, 16), 16), :]
            c1 = curl_t[pl.ds(pl.multiple_of(first + 16, 16), 16), :]
            for i in range(3):
                for j in range(6):
                    col = i * 8 + j
                    wide[i * 6 + j, to, :] = jnp.where(low, jnp.broadcast_to(c0[:, col:col + 1], (16, 128)),
                                                       jnp.broadcast_to(c1[:, col:col + 1], (16, 128)))
        to_far[c].wait_recv()
        relays[c].start()
        if c == PARTS - 2:
            @pl.loop(16, N_MESH)
            def _(slot):
                op_copy(slot).start()
    gfar.wait_recv()
    relays[PARTS].start()

    for c in (*to_far, *to_side, *ghosts, gfar, gside):
        c.wait_send()


    for c in load_conn:
        c.wait()
    keep.wait()
    for c in range(PARTS + 1):
        if c < PARTS:
            to_side[c].wait_recv()
        else:
            gside.wait_recv()
        relays[c].wait_recv()
        blocks = CHUNK // 128 if c < PARTS else 2 * FACE // 128

        @pl.loop(0, blocks, unroll=2)
        def _(b):
            at = pl.ds(pl.multiple_of(c * CHUNK + b * 128, 128), 128)
            x = ext[:, at]
            ext2[at, :] = jnp.concatenate([x, x], axis=0).T

    @pl.loop(0, N_MESH // 2)
    def _(pair):
        for u in range(2):
            s = pair * 2 + u
            to = pl.ds(pl.multiple_of(s * 16, 16), 16)
            first = pl.multiple_of(s * 128 + block_of(s, m) * 32, 32)
            near = [conn_ref.at[pl.ds(first + j * 4096, 32)] for j in range(6)]
            for j, k in EDGE_ORDER:
                a = ext2[pl.ds(near[j][k], 1), :]
                b = ext2[pl.ds(near[j][16 + k], 1), :]
                got[u, pl.ds(j * 16 + k, 1), :] = jnp.where(low1, a, b)
            for i in range(3):
                s_i = wide[i * 6, to, :] * got[u, 0:16, :]
                for j in range(1, 6):
                    s_i = s_i + wide[i * 6 + j, to, :] * got[u, j * 16:(j + 1) * 16, :]
                flux[i, to, :] = s_i

    op_all = pltpu.make_async_remote_copy(
        src_ref=opsend.at[pl.ds(0, N_MESH - 1)], dst_ref=op_in.at[pl.ds(0, N_MESH - 1)],
        send_sem=op_ss, recv_sem=op_rs, device_id=(m, far), device_id_type=MESH)
    op_all.wait_recv()

    op_keep.wait()
    growth = [jnp.exp(jnp.float32(-0.5) * knots_ref[k].astype(jnp.float32)) for k in range(8)]

    @pl.loop(0, ROWS // 64)
    def _(r):
        to = pl.ds(pl.multiple_of(r * 64, 64), 64)
        f = transform([flux[i, to, :] for i in range(3)], inv_ref)
        b = [jnp.concatenate([op_in[r * 4 + s, 16 * i:16 * i + 16, :] for s in range(4)], axis=0)
             for i in range(3)]
        kinds = []
        for s in range(4):
            mt = jnp.broadcast_to(op_in[r * 4 + s, pl.ds(48, 1), :], (8, 128)).T
            kinds.append(jnp.where(low, jnp.broadcast_to(mt[0:16, 0:1], (16, 128)),
                                   jnp.broadcast_to(mt[16:32, 0:1], (16, 128))))
        mat = jnp.concatenate(kinds, axis=0)

        def pick(values):
            x = jnp.where(mat == 1.0, values[1], values[0])
            x = jnp.where(mat == 2.0, values[2], x)
            return jnp.where(mat == 3.0, values[3], x)

        q = b[0] * b[0] + b[1] * b[1] + b[2] * b[2]
        u = jnp.exp(2.0 * q)
        nu = pick([base_ref[a] for a in range(4)])
        dnu = jnp.zeros_like(q)
        for k in range(0, 8, 2):
            s0, s1 = [pick([slopes_ref[a, k + n] for a in range(4)]) for n in range(2)]
            e0, e1 = u * growth[k], u * growth[k + 1]
            w0, w1 = 1.0 + e0, 1.0 + e1
            nu = nu + s0 * jnp.log(w0) + s1 * jnp.log(w1)
            dnu = dnu + (s0 * e0 * w1 + s1 * e1 * w0) / (w0 * w1)
        proj = b[0] * f[0] + b[1] * f[1] + b[2] * f[2]
        scale = 4.0 * dnu * proj
        f = transform([nu * f[i] + scale * b[i] for i in range(3)], fwd_ref)
        for j in range(6):
            out_ref[r, j * 64:(j + 1) * 64, :] = (
                wide[j, to, :] * f[0] + wide[6 + j, to, :] * f[1] + wide[12 + j, to, :] * f[2])

    for c in relays:
        c.wait_send()

    op_all.wait_send()


def forward(field, point, material, curl, faces, conn, knots, base, slopes):
    inverse, forward_table = block_diag_tables()
    smem = pl.BlockSpec(memory_space=pltpu.SMEM)
    vmem = pl.BlockSpec(memory_space=pltpu.VMEM)
    hbm = pl.BlockSpec(memory_space=pltpu.HBM)
    f32 = jnp.float32
    dma = pltpu.SemaphoreType.DMA
    return pl.pallas_call(
        forward_kernel,
        name="forward",
        out_shape=jax.ShapeDtypeStruct((ROWS // 64, 384, 128), f32),
        in_specs=[hbm, hbm, vmem, hbm, hbm, hbm, smem, smem, smem, hbm, hbm],
        out_specs=vmem,
        scratch_shapes=[
            pltpu.VMEM((16, OWN), f32), pltpu.VMEM((3, 32, 32, 64), f32), pltpu.VMEM((3, 6, 4096), f32),
            pltpu.VMEM((N_MESH, MSG, 128), f32), pltpu.VMEM((N_MESH, MSG, 128), f32),
            pltpu.VMEM((OWN, 16), f32), pltpu.VMEM((2 * FACE, 16), f32), pltpu.VMEM((16, 2 * FACE), f32),
            pltpu.VMEM((64, EXT), f32), pltpu.VMEM((EXT, 128), f32), pltpu.VMEM((4096, 24), f32),
            pltpu.VMEM((18, ROWS, 128), f32), pltpu.VMEM((2, 96, 128), f32), pltpu.VMEM((3, ROWS, 128), f32),
            pltpu.VMEM((256, 256), jnp.bfloat16), pltpu.VMEM((256, 256), jnp.bfloat16),
            pltpu.SMEM((2 * FACE,), jnp.int32), pltpu.SMEM((6 * 4096,), jnp.int32),
            dma((5,)), dma, dma, dma((PARTS,)), dma((PARTS,)), dma((PARTS,)), dma((PARTS,)),
            dma((2,)), dma((2,)), dma((2,)), dma((2,)), dma((PARTS + 1,)), dma((PARTS + 1,)), dma((10,)),
            pltpu.SemaphoreType.REGULAR, pltpu.SemaphoreType.REGULAR,
        ],
        compiler_params=pltpu.CompilerParams(collective_id=0, has_side_effects=True,
                                             vmem_limit_bytes=34 << 20),
    )(field, point, material, curl, faces, conn, knots, base, slopes, pltpu.with_memory_space_constraint(jnp.asarray(inverse), pltpu.HBM),
      pltpu.with_memory_space_constraint(jnp.asarray(forward_table), pltpu.HBM))


def scatter_kernel(conn_hbm, con_ref, acc0, acc1, acc2, acc3, acc4, acc5, conn_ref, sem):
    m = lax.axis_index("mesh")
    h = lax.axis_index("harm")
    accs = (acc0, acc1, acc2, acc3, acc4, acc5)

    def block_of(source, target):
        crossing = (source // 16 + target // 16) % 2
        return lax.rem(h + 2 * crossing * lax.rem(source, 2), 4)

    loads = [pltpu.make_async_copy(conn_hbm.at[j], conn_ref.at[pl.ds(j * 4096, 4096)], sem.at[j]) for j in range(6)]
    for c in loads:
        c.start()

    @pl.loop(0, EXT // 64)
    def _(b):
        at = pl.ds(pl.multiple_of(b * 64, 64), 64)
        for a in accs:
            a[at, :] = jnp.zeros((64, 128), jnp.float32)

    for c in loads:
        c.wait()

    @pl.loop(0, N_MESH)
    def _(s):
        first = pl.multiple_of(s * 128 + block_of(s, m) * 32, 32)
        near = [conn_ref.at[pl.ds(first + j * 4096, 32)] for j in range(6)]
        rows = con_ref.at[s // 4, pl.ds(pl.multiple_of(lax.rem(s, 4) * 16, 16), 336), :]
        for j, k in EDGE_ORDER:
            row = rows[pl.ds(j * 64 + k, 1), :]
            n0 = near[j][k]
            n1 = near[j][16 + k]
            a0, a1 = accs[j % 3], accs[3 + j % 3]
            a0[pl.ds(n0, 1), :] = a0[pl.ds(n0, 1), :] + row
            a1[pl.ds(n1, 1), :] = a1[pl.ds(n1, 1), :] + row


def scatter(conn, con):
    vmem = pl.BlockSpec(memory_space=pltpu.VMEM)
    return pl.pallas_call(
        scatter_kernel,
        name="scatter",
        out_shape=(jax.ShapeDtypeStruct((EXT, 128), jnp.float32),) * 6,
        in_specs=[pl.BlockSpec(memory_space=pltpu.HBM), vmem],
        out_specs=(vmem,) * 6,
        scratch_shapes=[pltpu.SMEM((6 * 4096,), jnp.int32), pltpu.SemaphoreType.DMA((6,))],
        compiler_params=pltpu.CompilerParams(vmem_limit_bytes=28 << 20),
    )(conn, con)


def combine_kernel(acc0, acc1, acc2, acc3, acc4, acc5, faces_hbm, own_out, acc, pairs, summed, zin, ghost_sum,
                   ghost_in, faces_v, low_hot, stack, face_add, face_s,
                   p_ss, p_rs, z_ss, z_rs, g_ss, g_rs):
    m = lax.axis_index("mesh")
    h = lax.axis_index("harm")
    up, down = lax.rem(m + 1, N_MESH), lax.rem(m + N_MESH - 1, N_MESH)
    side = h + 1 - 2 * lax.rem(h, 2)
    far = lax.rem(h + 2, 4)
    cross = lax.rem(side + 2, 4)
    barrier = pltpu.get_barrier_semaphore()
    for peer in ((m, side), (m, far), (up, h), (down, h)):
        pl.semaphore_signal(barrier, inc=1, device_id=peer, device_id_type=MESH)

    load = pltpu.make_async_copy(faces_hbm, faces_v, face_s)
    load.start()

    bounds = [(OWN, FACE), (OWN + FACE, FACE)] + [(c * CHUNK, CHUNK) for c in range(PARTS)]
    chunks = [pl.ds(a, n) for a, n in bounds]

    def block(who):
        return pl.ds(pl.multiple_of(16 * who, 16), 16)

    low = lax.broadcasted_iota(jnp.int32, (128, 128), 1) < 64

    def turn(c):
        start, n = bounds[c]

        @pl.loop(0, n // 128, unroll=2)
        def _(b):
            at = pl.ds(pl.multiple_of(start + b * 128, 128), 128)
            x = jnp.where(low, acc0[at, :] + acc1[at, :] + acc2[at, :], acc3[at, :] + acc4[at, :] + acc5[at, :]).T
            acc[:, at] = x[0:64, :] + x[64:128, :]

    def pair_copy(c, n):
        return pltpu.make_async_remote_copy(
            src_ref=acc.at[block((side, cross)[n]), chunks[c]], dst_ref=pairs.at[n, :, chunks[c]],
            send_sem=p_ss.at[c, n], recv_sem=p_rs.at[c, n],
            device_id=(m, side), device_id_type=MESH)

    def z_copy(c):
        return pltpu.make_async_remote_copy(
            src_ref=summed.at[:, chunks[c]], dst_ref=zin.at[:, chunks[c]],
            send_sem=z_ss.at[c], recv_sem=z_rs.at[c],
            device_id=(m, far), device_id_type=MESH)

    def g_copy(f, peer):
        return pltpu.make_async_remote_copy(
            src_ref=ghost_sum.at[:, pl.ds(f * FACE, FACE)],
            dst_ref=ghost_in.at[:, pl.ds((1 - f) * FACE, FACE)],
            send_sem=g_ss.at[f], recv_sem=g_rs.at[f],
            device_id=(peer, h), device_id_type=MESH)

    count = PARTS + 2
    far_pairs = [pair_copy(c, 1) for c in range(count)]
    own_pairs = [pair_copy(c, 0) for c in range(count)]
    zs = [z_copy(c) for c in range(count)]
    gs = [g_copy(0, down), g_copy(1, up)]

    turn(0)
    pl.semaphore_wait(barrier, 4)
    far_pairs[0].start()
    own_pairs[0].start()
    for c in range(count):
        if c + 1 < count:
            turn(c + 1)
            far_pairs[c + 1].start()
            own_pairs[c + 1].start()
        far_pairs[c].wait_recv()
        summed[:, chunks[c]] = acc[block(far), chunks[c]] + pairs[1, :, chunks[c]]
        zs[c].start()

    load.wait()
    for f in range(2):
        @pl.loop(0, FACE // 128)
        def _(b):
            column = faces_v[pl.ds(f, 1), pl.ds(pl.multiple_of(b * 128, 128), 128)] & 127
            hot = jnp.where(lax.broadcasted_iota(jnp.int32, (128, 128), 0) == jnp.broadcast_to(column, (128, 128)),
                            1.0, 0.0)
            low_hot[pl.ds(pl.multiple_of(f * FACE + b * 128, 128), 128), :] = hot.T.astype(jnp.bfloat16)

    def total(c):
        own_pairs[c].wait_recv()
        zs[c].wait_recv()
        return acc[block(h), chunks[c]] + pairs[0, :, chunks[c]] + zin[:, chunks[c]]

    for f in range(2):
        ghost_sum[:, pl.ds(f * FACE, FACE)] = total(f)
        gs[f].start()
    for g in gs:
        g.wait_recv()

    @pl.loop(0, OWN // 1024)
    def _(g):
        for f in range(2):
            part = pl.ds(f * FACE, FACE)
            tile = jnp.broadcast_to(lax.shift_right_logical(faces_v[pl.ds(f, 1), :], 7), (16, FACE))
            x = ghost_in[:, part]
            high = x.astype(jnp.bfloat16).astype(jnp.float32)
            rest = x - high
            for u in range(8):
                here = tile == g * 8 + u
                stack[u * 32:u * 32 + 16, part] = jnp.where(here, high, 0.0).astype(jnp.bfloat16)
                stack[u * 32 + 16:u * 32 + 32, part] = jnp.where(here, rest, 0.0).astype(jnp.bfloat16)
        y = jnp.dot(stack[...], low_hot[...], preferred_element_type=jnp.float32)
        for u in range(8):
            face_add[:, pl.ds(pl.multiple_of((g * 8 + u) * 128, 128), 128)] = (
                y[u * 32:u * 32 + 16, :] + y[u * 32 + 16:u * 32 + 32, :])

    for c in range(2, count):
        own_out[:, chunks[c]] = total(c) + face_add[:, chunks[c]]
    for c in (*far_pairs, *own_pairs, *zs, *gs):
        c.wait_send()


def combine(accs, faces):
    vmem = pl.BlockSpec(memory_space=pltpu.VMEM)
    dma = pltpu.SemaphoreType.DMA
    f32 = jnp.float32
    return pl.pallas_call(
        combine_kernel,
        name="combine",
        out_shape=jax.ShapeDtypeStruct((16, OWN), f32),
        in_specs=[vmem] * 6 + [pl.BlockSpec(memory_space=pltpu.HBM)],
        out_specs=vmem,
        scratch_shapes=[
            pltpu.VMEM((64, EXT), f32), pltpu.VMEM((2, 16, EXT), f32), pltpu.VMEM((16, EXT), f32),
            pltpu.VMEM((16, EXT), f32), pltpu.VMEM((16, 2 * FACE), f32), pltpu.VMEM((16, 2 * FACE), f32),
            pltpu.VMEM((2, FACE), jnp.int32), pltpu.VMEM((2 * FACE, 128), jnp.bfloat16),
            pltpu.VMEM((256, 2 * FACE), jnp.bfloat16), pltpu.VMEM((16, OWN), f32), dma,
            dma((PARTS + 2, 2)), dma((PARTS + 2, 2)), dma((PARTS + 2,)), dma((PARTS + 2,)), dma((2,)), dma((2,)),
        ],
        compiler_params=pltpu.CompilerParams(collective_id=1, has_side_effects=True,
                                             vmem_limit_bytes=28 << 20),
    )(*accs, faces)


def per_device(field_in, faces, connectivity, curl_vectors, operating_point, material, bh_knots, curve_base,
               curve_slopes):
    point = jnp.transpose(operating_point, (1, 2, 3, 0))
    (field_in, point, material, curl_vectors, faces, connectivity, bh_knots, curve_base, curve_slopes) = [
        pltpu.with_memory_space_constraint(x, pltpu.HBM)
        for x in (field_in, point, material, curl_vectors, faces, connectivity, bh_knots, curve_base, curve_slopes)]
    contributions = forward(field_in, point, material, curl_vectors, faces, connectivity, bh_knots, curve_base,
                            curve_slopes)
    return combine(scatter(connectivity, contributions), faces)


def solution(mesh):
    return jax.shard_map(
        per_device,
        mesh=mesh,
        in_specs=(P("harm", "mesh"), P(None, "mesh"), P(None, "mesh"), P(None, None, "mesh"),
                  P(None, None, None, ("mesh", "harm")), P(None, ("mesh", "harm")), P(), P(), P()),
        out_specs=P("harm", "mesh"),
        check_vma=False,
    )
```

```python
import functools

import numpy as np
import jax
import jax.numpy as jnp
from jax import lax
from jax.experimental import pallas as pl
from jax.experimental.pallas import tpu as pltpu
from jax.sharding import PartitionSpec as P

MESH = pl.DeviceIdType.MESH
N_MESH = 32
OWN = 5120
FACE = 1024
EXT = OWN + 2 * FACE
ROWS = 512
MSG = 56
PARTS = 4
CHUNK = OWN // PARTS
EDGE_ORDER = [(j + 3 * g, k) for g in range(2) for k in range(16) for j in range(3)]


def block_diag_tables():
    length = 64
    t = np.arange(length)
    c = np.arange(length)
    freq = np.where(c < 32, c, c - 31)
    freq[-1] = 32
    sine = (c >= 32) & (c < 63)
    angle = 2.0 * np.pi * ((freq[:, None] * t[None, :]) % length) / length
    basis = np.where(sine[:, None], np.sin(angle), np.cos(angle))
    weight = np.where((c == 0) | (c == 63), 1.0 / length, 2.0 / length)
    inverse = np.kron(np.eye(2), basis)
    forward = np.kron(np.eye(2), (basis * weight[:, None]).T)
    return split_table(inverse), split_table(forward)


def split_table(table):
    high = table.astype(jnp.bfloat16)
    rest = (table - high.astype(np.float64)).astype(jnp.bfloat16)
    return np.block([[high, rest], [high, np.zeros_like(rest)]])


def transform(parts, table_ref):
    x = jnp.concatenate(parts, axis=0)
    high = x.astype(jnp.bfloat16)
    rest = (x - high.astype(jnp.float32)).astype(jnp.bfloat16)
    y = jnp.dot(jnp.concatenate([high, rest], axis=1), table_ref[...], preferred_element_type=jnp.float32)
    y = y[:, 0:128] + y[:, 128:256]
    n = parts[0].shape[0]
    return [y[i * n:(i + 1) * n, :] for i in range(len(parts))]


def forward_kernel(field_ref, point_ref, mat_ref, curl_ref, faces_hbm, conn_hbm, knots_ref, base_ref, slopes_ref,
                   inv_hbm, fwd_hbm, out_ref,
                   field, point, curl, opsend, op_in, field_t, face_rows, face_cols, ext, ext2, curl_t, wide, got, flux, inv_ref, fwd_ref, faces_ref, conn_ref,
                   in_s, op_ss, op_rs, far_ss, far_rs, side_ss, side_rs, gh_ss, gh_rs, fw_ss, fw_rs, rel_ss, rel_rs, idx_s,
                   go_near, go_all):
    m = lax.axis_index("mesh")
    h = lax.axis_index("harm")
    up, down = lax.rem(m + 1, N_MESH), lax.rem(m + N_MESH - 1, N_MESH)
    side = h + 1 - 2 * lax.rem(h, 2)
    far = lax.rem(h + 2, 4)
    half = m // 16

    def block_of(source, target):
        crossing = (source // 16 + target // 16) % 2
        return lax.rem(h + 2 * crossing * lax.rem(source, 2), 4)

    within = lax.rem(m, 16)
    barrier = pltpu.get_barrier_semaphore()
    core = lax.rem(h, 2)
    leader, desk = h - core, h - core + 1
    far_leader, far_desk = lax.rem(leader + 2, 4), lax.rem(desk + 2, 4)
    pl.semaphore_signal(barrier, inc=1, device_id=(m, far_leader), device_id_type=MESH)

    @pl.when(core == 1)
    def _():
        pl.semaphore_signal(barrier, inc=1, device_id=(m, leader), device_id_type=MESH)

    for peer in (up, down):
        pl.semaphore_signal(barrier, inc=1, device_id=(peer, desk), device_id_type=MESH)

    @pl.loop(1, 16, unroll=3)
    def _(d):
        other = lax.rem(within + d, 16)
        pl.semaphore_signal(barrier, inc=1, device_id=(half * 16 + other, desk), device_id_type=MESH)

    for odd in range(2):
        @pl.loop(0, 8, unroll=2)
        def _(d):
            pl.semaphore_signal(barrier, inc=1, device_id=((1 - half) * 16 + 2 * d + odd, (desk, far_desk)[odd]),
                                device_id_type=MESH)

    load_field = pltpu.make_async_copy(field_ref, field, in_s.at[0])
    load_point = pltpu.make_async_copy(point_ref, point, in_s.at[1])
    load_curl = pltpu.make_async_copy(curl_ref, curl, in_s.at[2])
    load_field.start()
    load_point.start()
    load_curl.start()
    load_faces = [pltpu.make_async_copy(faces_hbm.at[f], faces_ref.at[pl.ds(f * FACE, FACE)], idx_s.at[f])
                  for f in range(2)]
    load_conn = [pltpu.make_async_copy(conn_hbm.at[j], conn_ref.at[pl.ds(j * 4096, 4096)], idx_s.at[2 + j])
                 for j in range(6)]
    load_conn.append(pltpu.make_async_copy(inv_hbm, inv_ref, idx_s.at[8]))
    load_conn.append(pltpu.make_async_copy(fwd_hbm, fwd_ref, idx_s.at[9]))
    for c in (*load_faces, *load_conn):
        c.start()

    load_field.wait()

    @pl.when(core == 0)
    def _():
        pl.semaphore_wait(barrier, 3)
        pl.semaphore_signal(go_near, inc=1, device_id=(m, side), device_id_type=MESH)

    @pl.when(core == 1)
    def _():
        pl.semaphore_wait(go_near, 1)

    def rows_of(who):
        return pl.ds(pl.multiple_of(16 * who, 16), 16)

    ghost_cols = pl.ds(OWN, 2 * FACE)

    def cols_of(c):
        return pl.ds(c * CHUNK, CHUNK)

    def own_copy(c, peer, ss, rs):
        return pltpu.make_async_remote_copy(
            src_ref=field.at[:, cols_of(c)], dst_ref=ext.at[rows_of(h), cols_of(c)],
            send_sem=ss.at[c], recv_sem=rs.at[c],
            device_id=(m, peer), device_id_type=MESH)

    to_far = [own_copy(c, far, far_ss, far_rs) for c in range(PARTS)]
    to_side = [own_copy(c, side, side_ss, side_rs) for c in range(PARTS)]
    for c in (*to_far, *to_side):
        c.start()
    keep = pltpu.make_async_copy(field, ext.at[rows_of(h), pl.ds(0, OWN)], in_s.at[3])
    keep.start()

    @pl.loop(0, OWN // 128, unroll=8)
    def _(b):
        at = pl.ds(pl.multiple_of(b * 128, 128), 128)
        field_t[at, :] = field[:, at].T

    for c in load_faces:
        c.wait()

    @pl.loop(0, 2 * FACE // 32)
    def _(b):
        near = faces_ref.at[pl.ds(pl.multiple_of(b * 32, 32), 32)]
        to = face_rows.at[pl.ds(pl.multiple_of(b * 32, 32), 32), :]
        for k in range(32):
            to[pl.ds(k, 1), :] = field_t[pl.ds(near[k], 1), :]

    @pl.loop(0, 2 * FACE // 128, unroll=8)
    def _(b):
        at = pl.ds(pl.multiple_of(b * 128, 128), 128)
        face_cols[:, at] = face_rows[at, :].T

    def ghost_copy(f, peer):
        return pltpu.make_async_remote_copy(
            src_ref=face_cols.at[:, pl.ds(f * FACE, FACE)],
            dst_ref=ext.at[rows_of(h), pl.ds(OWN + (1 - f) * FACE, FACE)],
            send_sem=gh_ss.at[f], recv_sem=gh_rs.at[f],
            device_id=(peer, h), device_id_type=MESH)

    @pl.when(core == 1)
    def _():
        pl.semaphore_wait(barrier, 2 * (N_MESH - 1 + 2))
        pl.semaphore_signal(go_all, inc=1, device_id=(m, side), device_id_type=MESH)

    @pl.when(core == 0)
    def _():
        pl.semaphore_wait(go_all, 1)

    ghosts = [ghost_copy(0, down), ghost_copy(1, up)]
    for c in ghosts:
        c.start()

    load_point.wait()

    @pl.loop(0, N_MESH)
    def _(p):
        for i in range(3):
            opsend[p, pl.ds(16 * i, 16), pl.ds(0, 64)] = point[i, p, pl.ds(0, 16), :]
            opsend[p, pl.ds(16 * i, 16), pl.ds(64, 64)] = point[i, p, pl.ds(16, 16), :]
        opsend[p, pl.ds(48, 8), :] = jnp.zeros((8, 128), jnp.float32)
        opsend[p, pl.ds(48, 1), pl.ds(0, 32)] = mat_ref[pl.ds(p, 1), :].astype(jnp.float32)

    def op_copy(slot):
        cross = slot // 16
        p = lax.rem(half + cross, 2) * 16 + lax.rem(within + slot, 16)
        target = lax.rem(h + 2 * cross * lax.rem(m, 2), 4)
        return pltpu.make_async_remote_copy(
            src_ref=opsend.at[p], dst_ref=op_in.at[m],
            send_sem=op_ss, recv_sem=op_rs,
            device_id=(p, target), device_id_type=MESH)

    op_keep = pltpu.make_async_copy(opsend.at[m], op_in.at[m], in_s.at[4])
    op_keep.start()

    for c in ghosts:
        c.wait_recv()

    def gfwd_copy(n, peer):
        return pltpu.make_async_remote_copy(
            src_ref=ext.at[rows_of(h), ghost_cols], dst_ref=ext.at[rows_of(h), ghost_cols],
            send_sem=fw_ss.at[n], recv_sem=fw_rs.at[n],
            device_id=(m, peer), device_id_type=MESH)

    gfar, gside = gfwd_copy(0, far), gfwd_copy(1, side)
    gfar.start()
    gside.start()

    @pl.loop(1, 16)
    def _(slot):
        op_copy(slot).start()


    def relay(c, cols):
        return pltpu.make_async_remote_copy(
            src_ref=ext.at[rows_of(far), cols], dst_ref=ext.at[rows_of(far), cols],
            send_sem=rel_ss.at[c], recv_sem=rel_rs.at[c],
            device_id=(m, side), device_id_type=MESH)

    relays = [relay(c, cols_of(c)) for c in range(PARTS)] + [relay(PARTS, ghost_cols)]

    low = lax.broadcasted_iota(jnp.int32, (16, 128), 1) < 64
    low1 = lax.broadcasted_iota(jnp.int32, (1, 128), 1) < 64

    load_curl.wait()

    @pl.loop(0, N_MESH, unroll=4)
    def _(s):
        at = pl.ds(pl.multiple_of(s * 128, 128), 128)
        pad = jnp.zeros((2, 128), jnp.float32)
        parts = []
        for i in range(3):
            parts += [curl[i, :, at], pad]
        curl_t[at, :] = jnp.concatenate(parts, axis=0).T

    for c in range(PARTS):
        @pl.loop(c * N_MESH // PARTS, (c + 1) * N_MESH // PARTS)
        def _(s):
            to = pl.ds(pl.multiple_of(s * 16, 16), 16)
            first = s * 128 + block_of(s, m) * 32
            c0 = curl_t[pl.ds(pl.multiple_of(first, 16), 16), :]
            c1 = curl_t[pl.ds(pl.multiple_of(first + 16, 16), 16), :]
            for i in range(3):
                for j in range(6):
                    col = i * 8 + j
                    wide[i * 6 + j, to, :] = jnp.where(low, jnp.broadcast_to(c0[:, col:col + 1], (16, 128)),
                                                       jnp.broadcast_to(c1[:, col:col + 1], (16, 128)))
        to_far[c].wait_recv()
        relays[c].start()
        if c == PARTS - 2:
            @pl.loop(16, N_MESH)
            def _(slot):
                op_copy(slot).start()
    gfar.wait_recv()
    relays[PARTS].start()

    for c in (*to_far, *to_side, *ghosts, gfar, gside):
        c.wait_send()


    for c in load_conn:
        c.wait()
    keep.wait()
    for c in range(PARTS + 1):
        if c < PARTS:
            to_side[c].wait_recv()
        else:
            gside.wait_recv()
        relays[c].wait_recv()
        blocks = CHUNK // 128 if c < PARTS else 2 * FACE // 128

        @pl.loop(0, blocks, unroll=2)
        def _(b):
            at = pl.ds(pl.multiple_of(c * CHUNK + b * 128, 128), 128)
            x = ext[:, at]
            ext2[at, :] = jnp.concatenate([x, x], axis=0).T

    @pl.loop(0, N_MESH // 2)
    def _(pair):
        for u in range(2):
            s = pair * 2 + u
            to = pl.ds(pl.multiple_of(s * 16, 16), 16)
            first = pl.multiple_of(s * 128 + block_of(s, m) * 32, 32)
            near = [conn_ref.at[pl.ds(first + j * 4096, 32)] for j in range(6)]
            for j, k in EDGE_ORDER:
                a = ext2[pl.ds(near[j][k], 1), :]
                b = ext2[pl.ds(near[j][16 + k], 1), :]
                got[u, pl.ds(j * 16 + k, 1), :] = jnp.where(low1, a, b)
            for i in range(3):
                s_i = wide[i * 6, to, :] * got[u, 0:16, :]
                for j in range(1, 6):
                    s_i = s_i + wide[i * 6 + j, to, :] * got[u, j * 16:(j + 1) * 16, :]
                flux[i, to, :] = s_i

    op_all = pltpu.make_async_remote_copy(
        src_ref=opsend.at[pl.ds(0, N_MESH - 1)], dst_ref=op_in.at[pl.ds(0, N_MESH - 1)],
        send_sem=op_ss, recv_sem=op_rs, device_id=(m, far), device_id_type=MESH)
    op_all.wait_recv()

    op_keep.wait()
    growth = [jnp.exp(jnp.float32(-0.5) * knots_ref[k].astype(jnp.float32)) for k in range(8)]

    @pl.loop(0, ROWS // 64)
    def _(r):
        to = pl.ds(pl.multiple_of(r * 64, 64), 64)
        f = transform([flux[i, to, :] for i in range(3)], inv_ref)
        b = [jnp.concatenate([op_in[r * 4 + s, 16 * i:16 * i + 16, :] for s in range(4)], axis=0)
             for i in range(3)]
        kinds = []
        for s in range(4):
            mt = jnp.broadcast_to(op_in[r * 4 + s, pl.ds(48, 1), :], (8, 128)).T
            kinds.append(jnp.where(low, jnp.broadcast_to(mt[0:16, 0:1], (16, 128)),
                                   jnp.broadcast_to(mt[16:32, 0:1], (16, 128))))
        mat = jnp.concatenate(kinds, axis=0)

        def pick(values):
            x = jnp.where(mat == 1.0, values[1], values[0])
            x = jnp.where(mat == 2.0, values[2], x)
            return jnp.where(mat == 3.0, values[3], x)

        q = b[0] * b[0] + b[1] * b[1] + b[2] * b[2]
        u = jnp.exp(2.0 * q)
        nu = pick([base_ref[a] for a in range(4)])
        dnu = jnp.zeros_like(q)
        for k in range(0, 8, 2):
            s0, s1 = [pick([slopes_ref[a, k + n] for a in range(4)]) for n in range(2)]
            e0, e1 = u * growth[k], u * growth[k + 1]
            w0, w1 = 1.0 + e0, 1.0 + e1
            nu = nu + s0 * jnp.log(w0) + s1 * jnp.log(w1)
            dnu = dnu + (s0 * e0 * w1 + s1 * e1 * w0) / (w0 * w1)
        proj = b[0] * f[0] + b[1] * f[1] + b[2] * f[2]
        scale = 4.0 * dnu * proj
        f = transform([nu * f[i] + scale * b[i] for i in range(3)], fwd_ref)
        for j in range(6):
            out_ref[r, j * 64:(j + 1) * 64, :] = (
                wide[j, to, :] * f[0] + wide[6 + j, to, :] * f[1] + wide[12 + j, to, :] * f[2])

    for c in relays:
        c.wait_send()

    op_all.wait_send()


def forward(field, point, material, curl, faces, conn, knots, base, slopes):
    inverse, forward_table = block_diag_tables()
    smem = pl.BlockSpec(memory_space=pltpu.SMEM)
    vmem = pl.BlockSpec(memory_space=pltpu.VMEM)
    hbm = pl.BlockSpec(memory_space=pltpu.HBM)
    f32 = jnp.float32
    dma = pltpu.SemaphoreType.DMA
    return pl.pallas_call(
        forward_kernel,
        name="forward",
        out_shape=jax.ShapeDtypeStruct((ROWS // 64, 384, 128), f32),
        in_specs=[hbm, hbm, vmem, hbm, hbm, hbm, smem, smem, smem, hbm, hbm],
        out_specs=vmem,
        scratch_shapes=[
            pltpu.VMEM((16, OWN), f32), pltpu.VMEM((3, 32, 32, 64), f32), pltpu.VMEM((3, 6, 4096), f32),
            pltpu.VMEM((N_MESH, MSG, 128), f32), pltpu.VMEM((N_MESH, MSG, 128), f32),
            pltpu.VMEM((OWN, 16), f32), pltpu.VMEM((2 * FACE, 16), f32), pltpu.VMEM((16, 2 * FACE), f32),
            pltpu.VMEM((64, EXT), f32), pltpu.VMEM((EXT, 128), f32), pltpu.VMEM((4096, 24), f32),
            pltpu.VMEM((18, ROWS, 128), f32), pltpu.VMEM((2, 96, 128), f32), pltpu.VMEM((3, ROWS, 128), f32),
            pltpu.VMEM((256, 256), jnp.bfloat16), pltpu.VMEM((256, 256), jnp.bfloat16),
            pltpu.SMEM((2 * FACE,), jnp.int32), pltpu.SMEM((6 * 4096,), jnp.int32),
            dma((5,)), dma, dma, dma((PARTS,)), dma((PARTS,)), dma((PARTS,)), dma((PARTS,)),
            dma((2,)), dma((2,)), dma((2,)), dma((2,)), dma((PARTS + 1,)), dma((PARTS + 1,)), dma((10,)),
            pltpu.SemaphoreType.REGULAR, pltpu.SemaphoreType.REGULAR,
        ],
        compiler_params=pltpu.CompilerParams(collective_id=0, has_side_effects=True,
                                             vmem_limit_bytes=34 << 20),
    )(field, point, material, curl, faces, conn, knots, base, slopes, pltpu.with_memory_space_constraint(jnp.asarray(inverse), pltpu.HBM),
      pltpu.with_memory_space_constraint(jnp.asarray(forward_table), pltpu.HBM))


def scatter_kernel(conn_hbm, con_ref, acc0, acc1, acc2, acc3, acc4, acc5, conn_ref, sem):
    m = lax.axis_index("mesh")
    h = lax.axis_index("harm")
    accs = (acc0, acc1, acc2, acc3, acc4, acc5)

    def block_of(source, target):
        crossing = (source // 16 + target // 16) % 2
        return lax.rem(h + 2 * crossing * lax.rem(source, 2), 4)

    loads = [pltpu.make_async_copy(conn_hbm.at[j], conn_ref.at[pl.ds(j * 4096, 4096)], sem.at[j]) for j in range(6)]
    for c in loads:
        c.start()

    @pl.loop(0, EXT // 256)
    def _(b):
        at = pl.ds(pl.multiple_of(b * 256, 256), 256)
        for a in accs:
            a[at, :] = jnp.zeros((256, 128), jnp.float32)

    for c in loads:
        c.wait()

    @pl.loop(0, N_MESH)
    def _(s):
        first = pl.multiple_of(s * 128 + block_of(s, m) * 32, 32)
        near = [conn_ref.at[pl.ds(first + j * 4096, 32)] for j in range(6)]
        rows = con_ref.at[s // 4, pl.ds(pl.multiple_of(lax.rem(s, 4) * 16, 16), 336), :]
        for j, k in EDGE_ORDER:
            row = rows[pl.ds(j * 64 + k, 1), :]
            n0 = near[j][k]
            n1 = near[j][16 + k]
            a0, a1 = accs[j % 3], accs[3 + j % 3]
            a0[pl.ds(n0, 1), :] = a0[pl.ds(n0, 1), :] + row
            a1[pl.ds(n1, 1), :] = a1[pl.ds(n1, 1), :] + row


def scatter(conn, con):
    vmem = pl.BlockSpec(memory_space=pltpu.VMEM)
    return pl.pallas_call(
        scatter_kernel,
        name="scatter",
        out_shape=(jax.ShapeDtypeStruct((EXT, 128), jnp.float32),) * 6,
        in_specs=[pl.BlockSpec(memory_space=pltpu.HBM), vmem],
        out_specs=(vmem,) * 6,
        scratch_shapes=[pltpu.SMEM((6 * 4096,), jnp.int32), pltpu.SemaphoreType.DMA((6,))],
        compiler_params=pltpu.CompilerParams(vmem_limit_bytes=28 << 20),
    )(conn, con)


def combine_kernel(acc0, acc1, acc2, acc3, acc4, acc5, faces_hbm, own_out, acc, pairs, summed, zin, ghost_sum,
                   ghost_in, faces_v, low_hot, stack, face_add, face_s,
                   p_ss, p_rs, z_ss, z_rs, g_ss, g_rs):
    m = lax.axis_index("mesh")
    h = lax.axis_index("harm")
    up, down = lax.rem(m + 1, N_MESH), lax.rem(m + N_MESH - 1, N_MESH)
    side = h + 1 - 2 * lax.rem(h, 2)
    far = lax.rem(h + 2, 4)
    cross = lax.rem(side + 2, 4)
    barrier = pltpu.get_barrier_semaphore()
    for peer in ((m, side), (m, far), (up, h), (down, h)):
        pl.semaphore_signal(barrier, inc=1, device_id=peer, device_id_type=MESH)

    load = pltpu.make_async_copy(faces_hbm, faces_v, face_s)
    load.start()

    bounds = [(OWN, FACE), (OWN + FACE, FACE)] + [(c * CHUNK, CHUNK) for c in range(PARTS)]
    chunks = [pl.ds(a, n) for a, n in bounds]

    def block(who):
        return pl.ds(pl.multiple_of(16 * who, 16), 16)

    low = lax.broadcasted_iota(jnp.int32, (128, 128), 1) < 64

    def turn(c):
        start, n = bounds[c]

        @pl.loop(0, n // 128, unroll=2)
        def _(b):
            at = pl.ds(pl.multiple_of(start + b * 128, 128), 128)
            x = jnp.where(low, acc0[at, :] + acc1[at, :] + acc2[at, :], acc3[at, :] + acc4[at, :] + acc5[at, :]).T
            acc[:, at] = x[0:64, :] + x[64:128, :]

    def pair_copy(c, n):
        return pltpu.make_async_remote_copy(
            src_ref=acc.at[block((side, cross)[n]), chunks[c]], dst_ref=pairs.at[n, :, chunks[c]],
            send_sem=p_ss.at[c, n], recv_sem=p_rs.at[c, n],
            device_id=(m, side), device_id_type=MESH)

    def z_copy(c):
        return pltpu.make_async_remote_copy(
            src_ref=summed.at[:, chunks[c]], dst_ref=zin.at[:, chunks[c]],
            send_sem=z_ss.at[c], recv_sem=z_rs.at[c],
            device_id=(m, far), device_id_type=MESH)

    def g_copy(f, peer):
        return pltpu.make_async_remote_copy(
            src_ref=ghost_sum.at[:, pl.ds(f * FACE, FACE)],
            dst_ref=ghost_in.at[:, pl.ds((1 - f) * FACE, FACE)],
            send_sem=g_ss.at[f], recv_sem=g_rs.at[f],
            device_id=(peer, h), device_id_type=MESH)

    count = PARTS + 2
    far_pairs = [pair_copy(c, 1) for c in range(count)]
    own_pairs = [pair_copy(c, 0) for c in range(count)]
    zs = [z_copy(c) for c in range(count)]
    gs = [g_copy(0, down), g_copy(1, up)]

    turn(0)
    pl.semaphore_wait(barrier, 4)
    far_pairs[0].start()
    own_pairs[0].start()
    for c in range(count):
        if c + 1 < count:
            turn(c + 1)
            far_pairs[c + 1].start()
            own_pairs[c + 1].start()
        far_pairs[c].wait_recv()
        summed[:, chunks[c]] = acc[block(far), chunks[c]] + pairs[1, :, chunks[c]]
        zs[c].start()

    load.wait()
    for f in range(2):
        @pl.loop(0, FACE // 128)
        def _(b):
            column = faces_v[pl.ds(f, 1), pl.ds(pl.multiple_of(b * 128, 128), 128)] & 127
            hot = jnp.where(lax.broadcasted_iota(jnp.int32, (128, 128), 0) == jnp.broadcast_to(column, (128, 128)),
                            1.0, 0.0)
            low_hot[pl.ds(pl.multiple_of(f * FACE + b * 128, 128), 128), :] = hot.T.astype(jnp.bfloat16)

    def total(c):
        own_pairs[c].wait_recv()
        zs[c].wait_recv()
        return acc[block(h), chunks[c]] + pairs[0, :, chunks[c]] + zin[:, chunks[c]]

    for f in range(2):
        ghost_sum[:, pl.ds(f * FACE, FACE)] = total(f)
        gs[f].start()
    for g in gs:
        g.wait_recv()

    @pl.loop(0, OWN // 1024)
    def _(g):
        for f in range(2):
            part = pl.ds(f * FACE, FACE)
            tile = jnp.broadcast_to(lax.shift_right_logical(faces_v[pl.ds(f, 1), :], 7), (16, FACE))
            x = ghost_in[:, part]
            high = x.astype(jnp.bfloat16).astype(jnp.float32)
            rest = x - high
            for u in range(8):
                here = tile == g * 8 + u
                stack[u * 32:u * 32 + 16, part] = jnp.where(here, high, 0.0).astype(jnp.bfloat16)
                stack[u * 32 + 16:u * 32 + 32, part] = jnp.where(here, rest, 0.0).astype(jnp.bfloat16)
        y = jnp.dot(stack[...], low_hot[...], preferred_element_type=jnp.float32)
        for u in range(8):
            face_add[:, pl.ds(pl.multiple_of((g * 8 + u) * 128, 128), 128)] = (
                y[u * 32:u * 32 + 16, :] + y[u * 32 + 16:u * 32 + 32, :])

    for c in range(2, count):
        own_out[:, chunks[c]] = total(c) + face_add[:, chunks[c]]
    for c in (*far_pairs, *own_pairs, *zs, *gs):
        c.wait_send()


def combine(accs, faces):
    vmem = pl.BlockSpec(memory_space=pltpu.VMEM)
    dma = pltpu.SemaphoreType.DMA
    f32 = jnp.float32
    return pl.pallas_call(
        combine_kernel,
        name="combine",
        out_shape=jax.ShapeDtypeStruct((16, OWN), f32),
        in_specs=[vmem] * 6 + [pl.BlockSpec(memory_space=pltpu.HBM)],
        out_specs=vmem,
        scratch_shapes=[
            pltpu.VMEM((64, EXT), f32), pltpu.VMEM((2, 16, EXT), f32), pltpu.VMEM((16, EXT), f32),
            pltpu.VMEM((16, EXT), f32), pltpu.VMEM((16, 2 * FACE), f32), pltpu.VMEM((16, 2 * FACE), f32),
            pltpu.VMEM((2, FACE), jnp.int32), pltpu.VMEM((2 * FACE, 128), jnp.bfloat16),
            pltpu.VMEM((256, 2 * FACE), jnp.bfloat16), pltpu.VMEM((16, OWN), f32), dma,
            dma((PARTS + 2, 2)), dma((PARTS + 2, 2)), dma((PARTS + 2,)), dma((PARTS + 2,)), dma((2,)), dma((2,)),
        ],
        compiler_params=pltpu.CompilerParams(collective_id=1, has_side_effects=True,
                                             vmem_limit_bytes=28 << 20),
    )(*accs, faces)


def per_device(field_in, faces, connectivity, curl_vectors, operating_point, material, bh_knots, curve_base,
               curve_slopes):
    point = jnp.transpose(operating_point, (1, 2, 3, 0))
    (field_in, point, material, curl_vectors, faces, connectivity, bh_knots, curve_base, curve_slopes) = [
        pltpu.with_memory_space_constraint(x, pltpu.HBM)
        for x in (field_in, point, material, curl_vectors, faces, connectivity, bh_knots, curve_base, curve_slopes)]
    contributions = forward(field_in, point, material, curl_vectors, faces, connectivity, bh_knots, curve_base,
                            curve_slopes)
    return combine(scatter(connectivity, contributions), faces)


def solution(mesh):
    return jax.shard_map(
        per_device,
        mesh=mesh,
        in_specs=(P("harm", "mesh"), P(None, "mesh"), P(None, "mesh"), P(None, None, "mesh"),
                  P(None, None, None, ("mesh", "harm")), P(None, ("mesh", "harm")), P(), P(), P()),
        out_specs=P("harm", "mesh"),
        check_vma=False,
    )
```
